256 devices in a mesh: visit: 32 (over x, y, core), ccd: 8 (over z).
Axes of the slice: x: 4, y: 4, z: 8, core: 2. Of those that a mesh axis runs over, the one named last changes fastest.
Arguments:
- raw_rows: bfloat16 [128, 8192, 128], P('visit', 'ccd')
- resample: bfloat16 [128, 128, 128], P('visit')
- slot_row: int32 [32, 8, 32, 128], P('visit', 'ccd'), may hold values from 0 to 4092, as said below
- tap_weight: float32 [4, 32, 8, 32, 128], P(None, 'visit', 'ccd'), may hold values from 0 to 1
- patch_id: int32 [32, 8, 32, 128], P('visit', 'ccd'), may hold values from 0 to 15
- live_mask: int32 [32, 8, 32, 128], P('visit', 'ccd'), may hold values 0 or 1
Outputs:
- offsets: float32 [128, 64], P('visit')
- background: float32 [4096, 128], P(('visit', 'ccd'))
The draws below stay inside these ranges and needn't reach their ends.
Inputs may be any that keep to these rules, and one draw needn't show every extreme that they name: `slot_row`: each value is v * 1024 + b with v below 4 and b at most 1020.
All inputs are finite; a program needn't handle non-finite values. No bound on the sum of `live_mask` on one device may be relied on, other than what follows from the above.
Results may differ from the reference program's by a relative error of at most 0.0041.
Values may be sent and summed in bfloat16 or wider, within the bound.
No kernel may reach another device: no remote copies, remote signals or barrier semaphores. Data moves between devices by JAX's collectives and lax.ppermute only.
A program may use at most 64 MiB of HBM per device.

```python
import math
import jax
import jax.numpy as jnp
import numpy as np
from jax import lax

PIX = 128
ORDER = 8
TAPS = 4
ITERS = 2
VIS_DEV = 4
R_DEV = 1024
SLOT = 128
P_DEV = 16
NTERM = 64
VISITS = 128
ROWS_VIS = 8192
PATCHES = 4096
N_VISIT = 32
N_CCD = 8


def draw_raw_rows(key, part):
    noise_key, level_key = jax.random.split(key)
    levels = jax.random.normal(level_key, (VISITS, 4), jnp.float32)
    coord_y = (2 * jnp.arange(ROWS_VIS) + 1).astype(jnp.float32) / ROWS_VIS - 1.0
    coord_x = (2 * jnp.arange(PIX) + 1).astype(jnp.float32) / PIX - 1.0
    smooth = levels[:, 0, None, None] + levels[:, 1, None, None] * coord_y[None, :, None]
    smooth = smooth + levels[:, 2, None, None] * coord_x[None, None, :]
    smooth = smooth + levels[:, 3, None, None] * coord_y[None, :, None] * coord_x[None, None, :]
    noise = 0.3 * jax.random.normal(noise_key, (VISITS, ROWS_VIS, PIX), jnp.float32)
    return (smooth + noise).astype(jnp.bfloat16)


def draw_resample(key, part):
    pixels = jnp.arange(PIX)
    identity = (pixels[:, None] == pixels[None, :]).astype(jnp.float32)
    noise = jax.random.normal(key, (VISITS, PIX, PIX), jnp.float32)
    return (identity[None] + 0.35 * noise / PIX ** 0.5).astype(jnp.bfloat16)


def draw_slot_row(key, part):
    visit_key, base_key = jax.random.split(jax.random.fold_in(key, 7))
    shape = (N_VISIT, N_CCD, N_VISIT, SLOT)
    local_visit = jax.random.randint(visit_key, shape, 0, VIS_DEV)
    base_row = jax.random.randint(base_key, shape, 0, R_DEV - TAPS + 1)
    values = (local_visit * R_DEV + base_row).astype(jnp.int32).reshape(-1)
    values = values.at[0].set(VIS_DEV * R_DEV - TAPS)
    values = values.at[values.shape[0] - 1].set(0)
    return values.reshape(shape).astype(jnp.int32)


def set_ends(entries, stream_key, low, high):
    extent = entries.shape
    index_at = [jax.random.randint(jax.random.fold_in(stream_key, axis), (), 0, extent[axis]) for axis in range(len(extent))]
    entries = entries.at[tuple(index_at)].set(low)
    longest = extent.index(max(extent))
    index_at[longest] = (index_at[longest] + 1) % extent[longest]
    return entries.at[tuple(index_at)].set(high)


def level_of(key, dims, shards, low, largest):
    gain, own = 1.0, jax.random.fold_in(key, 6)
    for axis_at, blocks in shards:
        steps = jnp.exp(jax.random.uniform(jax.random.fold_in(own, axis_at), (blocks,), jnp.float32, low / len(shards), largest / len(shards)))
        gain = gain * jnp.repeat(steps, dims[axis_at] // blocks).reshape([-1 if axis == axis_at else 1 for axis in range(len(dims))])
    return gain


def cumulative_ranks(count, slope):
    portions = [(1 << 20) // math.isqrt(grade ** slope) + 1 for grade in range(1, count + 1)]
    deviation = 1 + sum(portions) // (1 << 30)
    return np.cumsum(np.array([max(1, weight // deviation) for weight in portions]))


def ranked(rng, extent, count, skew):
    grid = cumulative_ranks(count, skew)
    ticket = jax.random.randint(jax.random.fold_in(rng, 1), extent, 0, int(grid[count - 1]))
    grade = jnp.searchsorted(jnp.asarray(grid, jnp.int32), ticket, side="right")
    return jax.random.permutation(jax.random.fold_in(rng, 2), count)[grade].astype(jnp.int32)


def setup_inputs(seed: int = 0) -> dict:
    arg_keys = jax.random.split(jax.random.key(seed), 7)
    raw_rows = draw_raw_rows(jax.random.fold_in(arg_keys[6], 71), 0)
    resample = draw_resample(jax.random.fold_in(arg_keys[6], 71), 0)
    slot_row = draw_slot_row(jax.random.fold_in(arg_keys[6], 71), 0)
    tap_weight = jnp.clip(1.0 * jax.random.uniform(arg_keys[3], (TAPS, N_VISIT, N_CCD, N_VISIT, SLOT), jnp.float32) ** level_of(arg_keys[3], (TAPS, N_VISIT, N_CCD, N_VISIT, SLOT), ((1, 32), (2, 8)), -0.2, 0.2), 0.0, 1.0)
    patch_id = set_ends(ranked(arg_keys[4], (N_VISIT, N_CCD, N_VISIT, SLOT), P_DEV, 2), jax.random.fold_in(arg_keys[4], 3), 0, P_DEV - 1).astype(jnp.int32)
    live_mask = set_ends((jax.random.randint(arg_keys[5], (N_VISIT, N_CCD, N_VISIT, SLOT), 0, 5) < 3).astype(jnp.int32), jax.random.fold_in(arg_keys[5], 1), 0, 1)
    return dict(raw_rows=raw_rows, resample=resample, slot_row=slot_row, tap_weight=tap_weight, patch_id=patch_id, live_mask=live_mask)


ridge_weight = 1.0

def chebyshev(coords):
    series = [jnp.ones_like(coords), coords]
    for degree in range(2, ORDER):
        series.append(2.0 * coords * series[-1] - series[-2])
    return jnp.stack(series[:ORDER])

def model_of(coef_rows, cheb_rows, cheb_x):
    shaped = coef_rows.reshape(coef_rows.shape[:-1] + (ORDER, ORDER))
    reduced = jnp.sum(shaped * cheb_rows[..., None, :], axis=-1)
    return jnp.einsum('...i,ip->...p', reduced, cheb_x, precision=lax.Precision.HIGHEST)

def reference(raw_rows, resample, slot_row, tap_weight, patch_id, live_mask):
    f32 = jnp.float32
    visit_devs = N_VISIT
    ccd_devs = N_CCD
    raw_split = raw_rows.reshape(visit_devs, VIS_DEV, ccd_devs, R_DEV, PIX).transpose(0, 2, 1, 3, 4)
    res_split = resample.reshape(visit_devs, VIS_DEV, PIX, PIX)
    weight_split = tap_weight.transpose(1, 2, 0, 3, 4)

    def warp_block(inputs):
        raw_part, res_part, start_part, weight_part = inputs

        def per_ccd(raw_ccd, start_ccd, weight_ccd):
            resampled = jnp.einsum('vrp,vpq->vrq', raw_ccd.astype(f32), res_part.astype(f32)).reshape(-1, PIX)
            blended = jnp.zeros(start_ccd.shape + (PIX,), f32)
            for tap_index in range(TAPS):
                blended = blended + weight_ccd[tap_index][..., None] * resampled[start_ccd + tap_index]
            return blended.astype(jnp.bfloat16)
        return jax.vmap(per_ccd)(raw_part, start_part, weight_part)
    warped = lax.map(warp_block, (raw_split, res_split, slot_row, weight_split))
    local_visit = slot_row // R_DEV
    ccd_pos = jnp.arange(ccd_devs, dtype=jnp.int32)[None, :, None, None]
    src_pos = jnp.arange(visit_devs, dtype=jnp.int32)[:, None, None, None]
    row_pos = ccd_pos * R_DEV + slot_row % R_DEV
    global_visit = src_pos * VIS_DEV + local_visit
    coord_y = (2 * row_pos + TAPS).astype(f32) / (R_DEV * ccd_devs) - 1.0
    cheb_y = jnp.moveaxis(chebyshev(coord_y), 0, -1)
    cheb_x = chebyshev((2 * jnp.arange(PIX) + 1).astype(f32) / PIX - 1.0)
    gram_x = jnp.dot(cheb_x, cheb_x.T, precision=lax.Precision.HIGHEST)
    live_float = live_mask.astype(f32)
    codes = patch_id + P_DEV * (1 - live_mask)
    visit_hot = (local_visit[..., None] == jnp.arange(VIS_DEV, dtype=jnp.int32)).astype(f32)

    def design_block(inputs):
        hot_part, cheb_part, live_part = inputs
        outer = cheb_part[..., :, None] * cheb_part[..., None, :] * live_part[..., None, None]
        outer = outer.reshape(outer.shape[:-2] + (ORDER * ORDER,))
        return jnp.einsum('cnsv,cnsm->vm', hot_part, outer, precision=lax.Precision.HIGHEST)
    design = lax.map(design_block, (visit_hot, cheb_y, live_float)).reshape(VISITS, ORDER, ORDER)
    gram = jnp.einsum('ac,vbd->vabcd', gram_x, design).reshape(VISITS, NTERM, NTERM)
    gram = gram + ridge_weight * jnp.eye(NTERM, dtype=f32)
    factor = jnp.linalg.cholesky(gram)
    offsets = jnp.zeros((VISITS, NTERM), f32)
    codes_owner = codes.transpose(2, 1, 0, 3)
    background = None
    for sweep in range(ITERS):

        def correct_block(inputs):
            warped_part, visit_part, cheb_part = inputs
            model = model_of(offsets[visit_part], cheb_part, cheb_x)
            return (warped_part.astype(f32) - model).astype(jnp.bfloat16)
        corrected = lax.map(correct_block, (warped, global_visit, cheb_y))
        corrected_owner = corrected.transpose(2, 1, 0, 3, 4)

        def consensus_block(inputs):
            rows_part, code_part = inputs

            def per_ccd(rows_ccd, code_ccd):
                patch_hot = (code_ccd[..., None] == jnp.arange(P_DEV, dtype=jnp.int32)).astype(f32)
                sums = jnp.einsum('nsk,nsq->kq', patch_hot, rows_ccd.astype(f32))
                counts = jnp.sum(patch_hot, axis=(0, 1))
                patch_bg = sums / (counts + 1.0)[:, None]
                shared = patch_bg.astype(jnp.bfloat16).astype(f32)
                returned = jnp.einsum('nsk,kq->nsq', patch_hot, shared).astype(jnp.bfloat16)
                return (patch_bg, returned)
            return jax.vmap(per_ccd)(rows_part, code_part)
        patch_bgs, returned = lax.map(consensus_block, (corrected_owner, codes_owner))
        background = patch_bgs.reshape(PATCHES, PIX)
        matched = returned.transpose(2, 1, 0, 3, 4)

        def moment_block(inputs):
            warped_part, matched_part, live_part, cheb_part, hot_part = inputs
            resid = (warped_part.astype(f32) - matched_part.astype(f32)) * live_part[..., None]
            projected = jnp.einsum('...p,ip->...i', resid, cheb_x, precision=lax.Precision.HIGHEST)
            outer = projected[..., :, None] * cheb_part[..., None, :]
            outer = outer.reshape(outer.shape[:-2] + (ORDER * ORDER,))
            return jnp.einsum('cnsv,cnsm->vm', hot_part, outer, precision=lax.Precision.HIGHEST)
        moments = lax.map(moment_block, (warped, matched, live_float, cheb_y, visit_hot)).reshape(VISITS, NTERM)
        offsets = jax.scipy.linalg.cho_solve((factor, True), moments[..., None])[..., 0]
    return (offsets, background)
```

```python
import functools

import jax
import jax.numpy as jnp
import numpy as np
from jax import lax
from jax.experimental import pallas as pl
from jax.experimental.pallas import tpu as pltpu
from jax.sharding import PartitionSpec as P

ORDER = 8
TAPS = 4
P_DEV = 16
RIDGE = 1.0
HI = lax.Precision.HIGHEST
F32 = jnp.float32
BF16 = jnp.bfloat16
VMEM = pl.BlockSpec(memory_space=pltpu.VMEM)
SMEM = pl.BlockSpec(memory_space=pltpu.SMEM)


def constants(pixels):
    x = (2 * np.arange(pixels) + 1) / pixels - 1.0
    cx = [np.ones_like(x), x]
    for _ in range(2, ORDER):
        cx.append(2 * x * cx[-1] - cx[-2])
    cx = np.stack(cx)
    lam, rot = np.linalg.eigh(cx @ cx.T)
    return lam, rot, rot.T @ cx


def dot(a, b, precision=None):
    return lax.dot_general(
        a, b, (((1,), (0,)), ((), ())), precision=precision, preferred_element_type=F32
    )


def dot_t(a, b, precision=None):
    return lax.dot_general(
        a, b, (((1,), (1,)), ((), ())), precision=precision, preferred_element_type=F32
    )


def iota(shape, dim):
    return lax.broadcasted_iota(jnp.int32, shape, dim)


def cheb_rows(y, count):
    sub = iota(y.shape, 0)
    prev, cur = jnp.ones_like(y), y
    out = jnp.where(sub == 0, prev, cur)
    for k in range(2, count):
        prev, cur = cur, 2.0 * y * cur - prev
        out = jnp.where(sub == k, cur, out)
    return out


def coord(b_pos, ccd, rows_local, ccd_devs):
    base = (ccd * rows_local).astype(F32)
    return (2.0 * (base + b_pos) + float(TAPS)) / float(rows_local * ccd_devs) - 1.0


def gather_kernel(
    ccd_devs, rows_smem, raw_ref, res_ref, srow_ref, w_ref, pid_ref, live_ref, cxt_ref,
    pay_ref, t_ref, q_ref, res_sc, row_sc, code_sc, wi_sc, h_sc,
):
    vis, rows, pix = raw_ref.shape
    owners, slots = srow_ref.shape
    wide = slots * TAPS
    ccd = lax.axis_index("ccd")
    for v in range(vis):
        res_sc[pl.ds(8 + v * rows, rows), :] = dot(raw_ref[v], res_ref[v])
    off = iota((slots, wide), 1) - TAPS * iota((slots, wide), 0)
    rep = jnp.where((off >= 0) & (off < TAPS), 1.0, 0.0).astype(BF16)
    srow = srow_ref[...]
    code = pid_ref[...] + P_DEV * (1 - live_ref[...])
    high, low = srow >> 8, srow & 255
    row_sc[...] = 256.0 * dot(high.astype(F32).astype(BF16), rep) + dot(
        low.astype(F32).astype(BF16), rep
    )
    code_sc[...] = dot(code.astype(F32).astype(BF16), rep)
    wi = None
    for t in range(TAPS):
        pick = jnp.where(off == t, 1.0, 0.0).astype(BF16)
        part = dot(w_ref[t].astype(BF16), pick)
        wi = part if wi is None else wi + part
    wi_sc[...] = wi
    q_ref[...] = jnp.zeros_like(q_ref)
    half = iota((8, pix), 0) < TAPS
    kid = iota((P_DEV, wide), 0).astype(F32)
    kid_s = iota((P_DEV, slots), 0)

    def body(j, carry):
        pieces = []
        for g in range(slots // 4):
            pair = []
            for h in range(2):
                s = 4 * g + 2 * h
                first = res_sc[pl.ds(rows_smem[j, s] + 8, 8), :]
                second = res_sc[pl.ds(rows_smem[j, s + 1] + 4, 8), :]
                pair.append(jnp.where(half, first, second))
            pieces.append(jnp.concatenate(pair, axis=0).astype(BF16))
        taps = jnp.concatenate(pieces, axis=0)
        row = row_sc[pl.ds(j, 1), :]
        cod = code_sc[pl.ds(j, 1), :]
        wgt = wi_sc[pl.ds(j, 1), :]
        visit = jnp.floor(row * (1.0 / rows))
        y = coord(row - visit * rows, ccd, rows, ccd_devs)
        ty = cheb_rows(jnp.broadcast_to(y, (ORDER, wide)), ORDER)
        ty = ty * jnp.where(cod < float(P_DEV), wgt, 0.0)
        lhs = [jnp.where(cod == kid, wgt, 0.0)]
        for v in range(vis):
            lhs.append(jnp.where(visit == float(v), ty, 0.0))
        lhs = jnp.concatenate(lhs, axis=0).astype(BF16)
        sums = dot(lhs, taps)
        t_ref[pl.ds(pl.multiple_of(j * P_DEV, P_DEV), P_DEV), :] = sums[:P_DEV]
        q_ref[...] += sums[P_DEV:]
        live = live_ref[pl.ds(j, 1), :]
        member = jnp.where((pid_ref[pl.ds(j, 1), :] == kid_s) & (live > 0), 1.0, 0.0)
        h_sc[pl.ds(pl.multiple_of(j * P_DEV, P_DEV), P_DEV), :] = member
        return carry

    lax.fori_loop(0, owners, body, 0)
    proj = dot_t(cxt_ref[...], t_ref[...], HI)
    counts = dot_t(jnp.ones((8, slots), BF16), h_sc[...].astype(BF16))
    blocks = owners * P_DEV // 128
    sub = iota((16, 128), 0)
    rows_out = [proj[:, 128 * q : 128 * (q + 1)] for q in range(blocks)]
    tail = jnp.zeros((16, 128), F32)
    for q in range(blocks):
        tail = jnp.where(sub == q, counts[0:1, 128 * q : 128 * (q + 1)], tail)
    block = jnp.concatenate(rows_out + [tail], axis=0).astype(BF16)
    for i in range(owners):
        pay_ref[i] = block


def design_kernel(
    ccd_devs, rows, srow_ref, pid_ref, live_ref, q_ref, cxt_ref, mt_ref, qb_ref, sy_ref, m_sc
):
    owners, slots = srow_ref.shape
    vis = q_ref.shape[0] // ORDER
    ccd = lax.axis_index("ccd")
    kid = iota((P_DEV, slots), 0)
    m_sc[...] = jnp.zeros_like(m_sc)

    def body(j, acc):
        srow = srow_ref[pl.ds(j, 1), :]
        live = live_ref[pl.ds(j, 1), :]
        pid = pid_ref[pl.ds(j, 1), :]
        visit = srow // rows
        y = coord((srow - visit * rows).astype(F32), ccd, rows, ccd_devs)
        ty = cheb_rows(jnp.broadcast_to(y, (ORDER, slots)), ORDER)
        member = jnp.where((pid == kid) & (live > 0), 1.0, 0.0)
        vt = jnp.concatenate(
            [jnp.where((visit == v) & (live > 0), ty, 0.0) for v in range(vis)], axis=0
        )
        both = dot_t(jnp.concatenate([member, ty], axis=0), vt, HI)
        m_sc[pl.ds(pl.multiple_of(j * P_DEV, P_DEV), P_DEV), 0 : vis * ORDER] = both[:P_DEV]
        return acc + both[P_DEV:]

    sy = lax.fori_loop(0, owners, body, jnp.zeros((ORDER, vis * ORDER), F32))
    sy_ref[...] = jnp.concatenate([sy, jnp.zeros((ORDER, 128 - vis * ORDER), F32)], axis=1)
    mt_ref[...] = m_sc[...].T[: vis * ORDER]
    qb_ref[...] = blocks_of(dot_t(q_ref[...], tile_rows(cxt_ref[...], 128 // ORDER), HI), vis)


def tile_rows(x, times):
    return jnp.concatenate([x] * times, axis=0)


def blocks_of(full, vis):
    lane = iota((ORDER, full.shape[1]), 1) // ORDER
    out = jnp.zeros((ORDER, full.shape[1]), F32)
    for v in range(vis):
        out = out + jnp.where(lane == v, full[v * ORDER : (v + 1) * ORDER], 0.0)
    return out


def moments_block(mt, back, q, vis):
    full = None
    for i, piece in enumerate(back):
        part = dot_t(mt[:, 128 * i : 128 * (i + 1)], tile_rows(piece, 128 // ORDER), HI)
        full = part if full is None else full + part
    return q - blocks_of(full, vis)


def senders_sum(ref, lo, hi):
    total = ref[0, lo:hi].astype(F32)
    for i in range(1, ref.shape[0]):
        total = total + ref[i, lo:hi].astype(F32)
    return total


def first_kernel(arr_ref, mt_ref, qb_ref, sy_ref, b_ref, den_ref, pay_ref):
    blocks = b_ref.shape[1] // 128
    vis = mt_ref.shape[0] // ORDER
    total = senders_sum(arr_ref, 0, arr_ref.shape[1])
    back = []
    for q in range(blocks):
        den = total[ORDER * blocks + q : ORDER * blocks + q + 1] + 1.0
        den = jnp.broadcast_to(den, (ORDER, 128))
        piece = total[ORDER * q : ORDER * (q + 1)] / den
        den_ref[:, 128 * q : 128 * (q + 1)] = den
        b_ref[:, 128 * q : 128 * (q + 1)] = piece
        back.append(piece)
    mom = moments_block(mt_ref[...], back, qb_ref[...], vis)
    block = jnp.concatenate([mom, sy_ref[...]], axis=0)
    for i in range(pay_ref.shape[0]):
        pay_ref[i] = block


def solve(mom, sy, lam, vis):
    n = vis * ORDER
    rows, lanes = iota((n, ORDER * 128), 0), iota((n, ORDER * 128), 1)
    pos = lanes % 128
    pick = (rows // ORDER == pos // ORDER) & (rows % ORDER == lanes // 128)
    spread = dot(sy[:, :n], jnp.where(pick, 1.0, 0.0), HI)
    sub = iota((ORDER, 128), 0)
    mat = [
        spread[:, 128 * b : 128 * (b + 1)] * lam + jnp.where(sub == b, RIDGE, 0.0)
        for b in range(ORDER)
    ]
    rhs = [mom[b : b + 1] for b in range(ORDER)]
    for p in range(ORDER):
        inv = 1.0 / mat[p][p : p + 1]
        mat[p] = mat[p] * inv
        rhs[p] = rhs[p] * inv
        for b in range(ORDER):
            if b != p:
                factor = mat[b][p : p + 1]
                mat[b] = mat[b] - factor * mat[p]
                rhs[b] = rhs[b] - factor * rhs[p]
    out = jnp.zeros((ORDER, 128), F32)
    for b in range(ORDER):
        out = jnp.where(sub == b, rhs[b], out)
    return jnp.where(iota((ORDER, 128), 1) < n, out, 0.0)


def block_diag_t(z, vis):
    n = vis * ORDER
    tiled = tile_rows(z, vis)
    keep = iota((n, 128), 0) // ORDER == iota((n, 128), 1) // ORDER
    return jnp.where(keep, tiled, 0.0).T[:n]


def model_kernel(arr_ref, lam_ref, mt_ref, m_ref, t_ref, cxt_ref, sy_ref, pay_ref):
    vis = mt_ref.shape[0] // ORDER
    total = arr_ref[0]
    for i in range(1, arr_ref.shape[0]):
        total = total + arr_ref[i]
    sy_ref[...] = total[ORDER:]
    z = solve(total[:ORDER], total[ORDER:], lam_ref[0:1], vis)
    diag = block_diag_t(z, vis)
    weights = diag[:ORDER]
    for v in range(1, vis):
        weights = weights + diag[v * ORDER : (v + 1) * ORDER]
    model = dot(weights, mt_ref[...], HI)
    surface = lax.dot_general(
        weights, cxt_ref[...], (((0,), (0,)), ((), ())), precision=HI, preferred_element_type=F32
    )
    surface = jnp.concatenate([surface, jnp.zeros((128 - vis * ORDER, 128), F32)], axis=0)
    corrected = t_ref[...] - dot(m_ref[...], surface, HI)
    blocks = model.shape[1] // 128
    block = jnp.concatenate(
        [model[:, 128 * q : 128 * (q + 1)] for q in range(blocks)], axis=0
    ).astype(BF16)
    rows = ORDER * blocks
    for i in range(pay_ref.shape[0]):
        pay_ref[i, 0:rows] = block
        pay_ref[i, rows : rows + P_DEV] = corrected[P_DEV * i : P_DEV * (i + 1)].astype(BF16)


def second_kernel(arr_ref, b_ref, den_ref, mt_ref, qb_ref, lam_ref, pay_ref):
    blocks = b_ref.shape[1] // 128
    vis = mt_ref.shape[0] // ORDER
    total = senders_sum(arr_ref, 0, ORDER * blocks)
    lam = lam_ref[:, 0:1]
    back = []
    for q in range(blocks):
        cols = slice(128 * q, 128 * (q + 1))
        model = total[ORDER * q : ORDER * (q + 1)]
        back.append(b_ref[:, cols] - lam * model / den_ref[:, cols])
    mom = moments_block(mt_ref[...], back, qb_ref[...], vis)
    for i in range(pay_ref.shape[0]):
        pay_ref[i] = mom


def background_kernel(arr_ref, den_ref, out_ref):
    rows = arr_ref.shape[1] - P_DEV
    sums = senders_sum(arr_ref, rows, rows + P_DEV)
    own = lax.axis_index("visit") * P_DEV
    width = den_ref.shape[1]
    pick = iota((P_DEV, width), 1) == iota((P_DEV, width), 0) + own
    den = dot_t(jnp.where(pick, 1.0, 0.0), den_ref[...], HI)
    out_ref[...] = sums / den[:, 0:1]


def final_kernel(arr_ref, sy_ref, lam_ref, rot_ref, out_ref):
    vis = out_ref.shape[0]
    n = vis * ORDER
    total = arr_ref[0]
    for i in range(1, arr_ref.shape[0]):
        total = total + arr_ref[i]
    z = solve(total, sy_ref[...], lam_ref[0:1], vis)
    zt = z.T[:n]
    coef = jnp.concatenate(
        [dot(rot_ref[...], zt[v * ORDER : (v + 1) * ORDER], HI) for v in range(vis)], axis=0
    )
    wide = ORDER * ORDER
    spread = jnp.where(iota((ORDER, wide), 1) % ORDER == iota((ORDER, wide), 0), 1.0, 0.0)
    flat = dot(coef, spread, HI)
    keep = iota((n, wide), 1) // ORDER == iota((n, wide), 0) % ORDER
    flat = jnp.where(keep, flat, 0.0)
    for v in range(vis):
        out_ref[v : v + 1] = jnp.sum(flat[v * ORDER : (v + 1) * ORDER], axis=0, keepdims=True)


def call(kernel, out_shape, scratch=(), n_in=1, smem=()):
    return pl.pallas_call(
        kernel,
        out_shape=out_shape,
        in_specs=[SMEM if i in smem else VMEM for i in range(n_in)],
        out_specs=jax.tree.map(lambda _: VMEM, out_shape),
        scratch_shapes=list(scratch),
    )


def shape(dims, dtype=F32):
    return jax.ShapeDtypeStruct(dims, dtype)


def exchange(x, axis):
    return lax.all_to_all(x, axis, split_axis=0, concat_axis=0, tiled=True)


def per_device(raw_rows, resample, slot_row, tap_weight, patch_id, live_mask):
    owners = lax.axis_size("visit")
    ccd_devs = lax.axis_size("ccd")
    vis, rows, pix = raw_rows.shape
    slots = slot_row.shape[3]
    patches = owners * P_DEV
    blocks = patches // 128
    nvb = vis * ORDER
    lam, rot, cxt = constants(pix)
    lam_lane = np.zeros((8, 128))
    lam_lane[0, :nvb] = np.tile(lam, vis)
    lam_sub = np.broadcast_to(lam[:, None], (8, 128))
    lam_lane, lam_sub = jnp.asarray(lam_lane, F32), jnp.asarray(lam_sub, F32)
    cxt, rot = jnp.asarray(cxt, F32), jnp.asarray(rot, F32)
    srow, pid, live = slot_row[0, 0], patch_id[0, 0], live_mask[0, 0]
    weights = tap_weight[:, 0, 0]
    pay_rows = ORDER * blocks + P_DEV

    pay1, tsum, qsum = call(
        functools.partial(gather_kernel, ccd_devs),
        (
            shape((owners, pay_rows, 128), BF16),
            shape((patches, pix)),
            shape((nvb, pix)),
        ),
        scratch=(
            pltpu.VMEM((vis * rows + 16, pix), F32),
            pltpu.VMEM((owners, slots * TAPS), F32),
            pltpu.VMEM((owners, slots * TAPS), F32),
            pltpu.VMEM((owners, slots * TAPS), F32),
            pltpu.VMEM((patches, slots), F32),
        ),
        n_in=8,
        smem=(0,),
    )(srow, raw_rows, resample, srow, weights, pid, live, cxt)
    arr1 = exchange(pay1, "visit")
    mt, qb, sy, m = call(
        functools.partial(design_kernel, ccd_devs, rows),
        (
            shape((nvb, patches)),
            shape((ORDER, 128)),
            shape((ORDER, 128)),
            shape((patches, 128)),
        ),
        n_in=5,
    )(srow, pid, live, qsum, cxt)
    back, den, pay2 = call(
        first_kernel,
        (
            shape((ORDER, patches)),
            shape((ORDER, patches)),
            shape((ccd_devs, 2 * ORDER, 128)),
        ),
        n_in=4,
    )(arr1, mt, qb, sy)
    arr2 = exchange(pay2, "ccd")
    sy_all, pay3 = call(
        model_kernel,
        (shape((ORDER, 128)), shape((owners, pay_rows, 128), BF16)),
        n_in=6,
    )(arr2, lam_lane, mt, m, tsum, cxt)
    arr3 = exchange(pay3, "visit")
    pay4 = call(
        second_kernel,
        shape((ccd_devs, ORDER, 128)),
        n_in=6,
    )(arr3, back, den, mt, qb, lam_sub)
    arr4 = exchange(pay4, "ccd")
    background = call(background_kernel, shape((P_DEV, pix)), n_in=2)(arr3, den)
    offsets = call(final_kernel, shape((vis, ORDER * ORDER)), n_in=4)(
        arr4, sy_all, lam_lane, rot
    )
    return offsets, background


def solution(mesh):
    in_specs = (
        P("visit", "ccd", None),
        P("visit", None, None),
        P("visit", "ccd", None, None),
        P(None, "visit", "ccd", None, None),
        P("visit", "ccd", None, None),
        P("visit", "ccd", None, None),
    )
    out_specs = (P("visit", None), P(("visit", "ccd"), None))
    return jax.shard_map(
        per_device, mesh=mesh, in_specs=in_specs, out_specs=out_specs, check_vma=False
    )
```

```python
import functools

import jax
import jax.numpy as jnp
import numpy as np
from jax import lax
from jax.experimental import pallas as pl
from jax.experimental.pallas import tpu as pltpu
from jax.sharding import PartitionSpec as P

ORDER = 8
TAPS = 4
P_DEV = 16
RIDGE = 1.0
HI = lax.Precision.HIGHEST
F32 = jnp.float32
BF16 = jnp.bfloat16
VMEM = pl.BlockSpec(memory_space=pltpu.VMEM)
SMEM = pl.BlockSpec(memory_space=pltpu.SMEM)


def constants(pixels):
    x = (2 * np.arange(pixels) + 1) / pixels - 1.0
    cx = [np.ones_like(x), x]
    for _ in range(2, ORDER):
        cx.append(2 * x * cx[-1] - cx[-2])
    cx = np.stack(cx)
    lam, rot = np.linalg.eigh(cx @ cx.T)
    return lam, rot, rot.T @ cx


def dot(a, b, precision=None):
    return lax.dot_general(
        a, b, (((1,), (0,)), ((), ())), precision=precision, preferred_element_type=F32
    )


def dot_t(a, b, precision=None):
    return lax.dot_general(
        a, b, (((1,), (1,)), ((), ())), precision=precision, preferred_element_type=F32
    )


def iota(shape, dim):
    return lax.broadcasted_iota(jnp.int32, shape, dim)


def cheb_rows(y, count):
    sub = iota(y.shape, 0)
    prev, cur = jnp.ones_like(y), y
    out = jnp.where(sub == 0, prev, cur)
    for k in range(2, count):
        prev, cur = cur, 2.0 * y * cur - prev
        out = jnp.where(sub == k, cur, out)
    return out


def coord(b_pos, ccd, rows_local, ccd_devs):
    base = (ccd * rows_local).astype(F32)
    return (2.0 * (base + b_pos) + float(TAPS)) / float(rows_local * ccd_devs) - 1.0


def gather_kernel(
    ccd_devs, rows_smem, raw_ref, res_ref, srow_ref, w_ref, pid_ref, live_ref, cxt_ref,
    pay_ref, t_ref, q_ref, res_sc, row_sc, code_sc, wi_sc, h_sc,
):
    vis, rows, pix = raw_ref.shape
    owners, slots = srow_ref.shape
    wide = slots * TAPS
    ccd = lax.axis_index("ccd")
    for v in range(vis):
        res_sc[pl.ds(8 + v * rows, rows), :] = dot(raw_ref[v], res_ref[v])
    off = iota((slots, wide), 1) - TAPS * iota((slots, wide), 0)
    rep = jnp.where((off >= 0) & (off < TAPS), 1.0, 0.0).astype(BF16)
    srow = srow_ref[...]
    code = pid_ref[...] + P_DEV * (1 - live_ref[...])
    high, low = srow >> 8, srow & 255
    row_sc[...] = 256.0 * dot(high.astype(F32).astype(BF16), rep) + dot(
        low.astype(F32).astype(BF16), rep
    )
    code_sc[...] = dot(code.astype(F32).astype(BF16), rep)
    wi = None
    for t in range(TAPS):
        pick = jnp.where(off == t, 1.0, 0.0).astype(BF16)
        part = dot(w_ref[t].astype(BF16), pick)
        wi = part if wi is None else wi + part
    wi_sc[...] = wi
    q_ref[...] = jnp.zeros_like(q_ref)
    half = iota((8, pix), 0) < TAPS
    kid = iota((P_DEV, wide), 0).astype(F32)
    kid_s = iota((P_DEV, slots), 0)

    def body(j, carry):
        start = pl.multiple_of(j * slots, slots)
        row_at = [
            rows_smem.at[pl.ds(i, (owners - 1) * slots + 1)][start] for i in range(slots)
        ]
        pieces = []
        for g in range(slots // 4):
            pair = []
            for h in range(2):
                s = 4 * g + 2 * h
                first = res_sc[pl.ds(row_at[s] + 8, 8), :]
                second = res_sc[pl.ds(row_at[s + 1] + 4, 8), :]
                pair.append(jnp.where(half, first, second))
            pieces.append(jnp.concatenate(pair, axis=0).astype(BF16))
        taps = jnp.concatenate(pieces, axis=0)
        row = row_sc[pl.ds(j, 1), :]
        cod = code_sc[pl.ds(j, 1), :]
        wgt = wi_sc[pl.ds(j, 1), :]
        visit = jnp.floor(row * (1.0 / rows))
        y = coord(row - visit * rows, ccd, rows, ccd_devs)
        ty = cheb_rows(jnp.broadcast_to(y, (ORDER, wide)), ORDER)
        ty = ty * jnp.where(cod < float(P_DEV), wgt, 0.0)
        lhs = [jnp.where(cod == kid, wgt, 0.0)]
        for v in range(vis):
            lhs.append(jnp.where(visit == float(v), ty, 0.0))
        lhs = jnp.concatenate(lhs, axis=0).astype(BF16)
        sums = dot(lhs, taps)
        t_ref[pl.ds(pl.multiple_of(j * P_DEV, P_DEV), P_DEV), :] = sums[:P_DEV]
        q_ref[...] += sums[P_DEV:]
        live = live_ref[pl.ds(j, 1), :]
        member = jnp.where((pid_ref[pl.ds(j, 1), :] == kid_s) & (live > 0), 1.0, 0.0)
        h_sc[pl.ds(pl.multiple_of(j * P_DEV, P_DEV), P_DEV), :] = member
        return carry

    lax.fori_loop(0, owners, body, 0, unroll=4)
    proj = dot_t(cxt_ref[...], t_ref[...], HI)
    counts = dot_t(jnp.ones((8, slots), BF16), h_sc[...].astype(BF16))
    blocks = owners * P_DEV // 128
    sub = iota((16, 128), 0)
    rows_out = [proj[:, 128 * q : 128 * (q + 1)] for q in range(blocks)]
    tail = jnp.zeros((16, 128), F32)
    for q in range(blocks):
        tail = jnp.where(sub == q, counts[0:1, 128 * q : 128 * (q + 1)], tail)
    block = jnp.concatenate(rows_out + [tail], axis=0).astype(BF16)
    for i in range(owners):
        pay_ref[i] = block


def design_kernel(
    ccd_devs, rows, srow_ref, pid_ref, live_ref, q_ref, cxt_ref, mt_ref, qb_ref, sy_ref, m_sc
):
    owners, slots = srow_ref.shape
    vis = q_ref.shape[0] // ORDER
    ccd = lax.axis_index("ccd")
    kid = iota((P_DEV, slots), 0)
    m_sc[...] = jnp.zeros_like(m_sc)

    def body(j, acc):
        srow = srow_ref[pl.ds(j, 1), :]
        live = live_ref[pl.ds(j, 1), :]
        pid = pid_ref[pl.ds(j, 1), :]
        visit = srow // rows
        y = coord((srow - visit * rows).astype(F32), ccd, rows, ccd_devs)
        ty = cheb_rows(jnp.broadcast_to(y, (ORDER, slots)), ORDER)
        member = jnp.where((pid == kid) & (live > 0), 1.0, 0.0)
        vt = jnp.concatenate(
            [jnp.where((visit == v) & (live > 0), ty, 0.0) for v in range(vis)], axis=0
        )
        both = dot_t(jnp.concatenate([member, ty], axis=0), vt, HI)
        m_sc[pl.ds(pl.multiple_of(j * P_DEV, P_DEV), P_DEV), 0 : vis * ORDER] = both[:P_DEV]
        return acc + both[P_DEV:]

    sy = lax.fori_loop(0, owners, body, jnp.zeros((ORDER, vis * ORDER), F32))
    sy_ref[...] = jnp.concatenate([sy, jnp.zeros((ORDER, 128 - vis * ORDER), F32)], axis=1)
    mt_ref[...] = m_sc[...].T[: vis * ORDER]
    qb_ref[...] = blocks_of(dot_t(q_ref[...], tile_rows(cxt_ref[...], 128 // ORDER), HI), vis)


def tile_rows(x, times):
    return jnp.concatenate([x] * times, axis=0)


def blocks_of(full, vis):
    lane = iota((ORDER, full.shape[1]), 1) // ORDER
    out = jnp.zeros((ORDER, full.shape[1]), F32)
    for v in range(vis):
        out = out + jnp.where(lane == v, full[v * ORDER : (v + 1) * ORDER], 0.0)
    return out


def moments_block(mt, back, q, vis):
    full = None
    for i, piece in enumerate(back):
        part = dot_t(mt[:, 128 * i : 128 * (i + 1)], tile_rows(piece, 128 // ORDER), HI)
        full = part if full is None else full + part
    return q - blocks_of(full, vis)


def senders_sum(ref, lo, hi):
    total = ref[0, lo:hi].astype(F32)
    for i in range(1, ref.shape[0]):
        total = total + ref[i, lo:hi].astype(F32)
    return total


def first_kernel(arr_ref, mt_ref, qb_ref, sy_ref, b_ref, den_ref, pay_ref):
    blocks = b_ref.shape[1] // 128
    vis = mt_ref.shape[0] // ORDER
    total = senders_sum(arr_ref, 0, arr_ref.shape[1])
    back = []
    for q in range(blocks):
        den = total[ORDER * blocks + q : ORDER * blocks + q + 1] + 1.0
        den = jnp.broadcast_to(den, (ORDER, 128))
        piece = total[ORDER * q : ORDER * (q + 1)] / den
        den_ref[:, 128 * q : 128 * (q + 1)] = den
        b_ref[:, 128 * q : 128 * (q + 1)] = piece
        back.append(piece)
    mom = moments_block(mt_ref[...], back, qb_ref[...], vis)
    block = jnp.concatenate([mom, sy_ref[...]], axis=0)
    for i in range(pay_ref.shape[0]):
        pay_ref[i] = block


def solve(mom, sy, lam, vis):
    n = vis * ORDER
    rows, lanes = iota((n, ORDER * 128), 0), iota((n, ORDER * 128), 1)
    pos = lanes % 128
    pick = (rows // ORDER == pos // ORDER) & (rows % ORDER == lanes // 128)
    spread = dot(sy[:, :n], jnp.where(pick, 1.0, 0.0), HI)
    sub = iota((ORDER, 128), 0)
    mat = [
        spread[:, 128 * b : 128 * (b + 1)] * lam + jnp.where(sub == b, RIDGE, 0.0)
        for b in range(ORDER)
    ]
    rhs = [mom[b : b + 1] for b in range(ORDER)]
    for p in range(ORDER):
        inv = 1.0 / mat[p][p : p + 1]
        mat[p] = mat[p] * inv
        rhs[p] = rhs[p] * inv
        for b in range(ORDER):
            if b != p:
                factor = mat[b][p : p + 1]
                mat[b] = mat[b] - factor * mat[p]
                rhs[b] = rhs[b] - factor * rhs[p]
    out = jnp.zeros((ORDER, 128), F32)
    for b in range(ORDER):
        out = jnp.where(sub == b, rhs[b], out)
    return jnp.where(iota((ORDER, 128), 1) < n, out, 0.0)


def block_diag_t(z, vis):
    n = vis * ORDER
    tiled = tile_rows(z, vis)
    keep = iota((n, 128), 0) // ORDER == iota((n, 128), 1) // ORDER
    return jnp.where(keep, tiled, 0.0).T[:n]


def model_kernel(arr_ref, lam_ref, mt_ref, m_ref, t_ref, cxt_ref, sy_ref, pay_ref):
    vis = mt_ref.shape[0] // ORDER
    total = arr_ref[0]
    for i in range(1, arr_ref.shape[0]):
        total = total + arr_ref[i]
    sy_ref[...] = total[ORDER:]
    z = solve(total[:ORDER], total[ORDER:], lam_ref[0:1], vis)
    diag = block_diag_t(z, vis)
    weights = diag[:ORDER]
    for v in range(1, vis):
        weights = weights + diag[v * ORDER : (v + 1) * ORDER]
    model = dot(weights, mt_ref[...], HI)
    surface = lax.dot_general(
        weights, cxt_ref[...], (((0,), (0,)), ((), ())), precision=HI, preferred_element_type=F32
    )
    surface = jnp.concatenate([surface, jnp.zeros((128 - vis * ORDER, 128), F32)], axis=0)
    corrected = t_ref[...] - dot(m_ref[...], surface, HI)
    blocks = model.shape[1] // 128
    block = jnp.concatenate(
        [model[:, 128 * q : 128 * (q + 1)] for q in range(blocks)], axis=0
    ).astype(BF16)
    rows = ORDER * blocks
    for i in range(pay_ref.shape[0]):
        pay_ref[i, 0:rows] = block
        pay_ref[i, rows : rows + P_DEV] = corrected[P_DEV * i : P_DEV * (i + 1)].astype(BF16)


def second_kernel(arr_ref, b_ref, den_ref, mt_ref, qb_ref, lam_ref, pay_ref):
    blocks = b_ref.shape[1] // 128
    vis = mt_ref.shape[0] // ORDER
    total = senders_sum(arr_ref, 0, ORDER * blocks)
    lam = lam_ref[:, 0:1]
    back = []
    for q in range(blocks):
        cols = slice(128 * q, 128 * (q + 1))
        model = total[ORDER * q : ORDER * (q + 1)]
        back.append(b_ref[:, cols] - lam * model / den_ref[:, cols])
    mom = moments_block(mt_ref[...], back, qb_ref[...], vis)
    for i in range(pay_ref.shape[0]):
        pay_ref[i] = mom


def background_kernel(arr_ref, den_ref, out_ref):
    rows = arr_ref.shape[1] - P_DEV
    sums = senders_sum(arr_ref, rows, rows + P_DEV)
    own = lax.axis_index("visit") * P_DEV
    width = den_ref.shape[1]
    pick = iota((P_DEV, width), 1) == iota((P_DEV, width), 0) + own
    den = dot_t(jnp.where(pick, 1.0, 0.0), den_ref[...], HI)
    out_ref[...] = sums / den[:, 0:1]


def final_kernel(arr_ref, sy_ref, lam_ref, rot_ref, out_ref):
    vis = out_ref.shape[0]
    n = vis * ORDER
    total = arr_ref[0]
    for i in range(1, arr_ref.shape[0]):
        total = total + arr_ref[i]
    z = solve(total, sy_ref[...], lam_ref[0:1], vis)
    zt = z.T[:n]
    coef = jnp.concatenate(
        [dot(rot_ref[...], zt[v * ORDER : (v + 1) * ORDER], HI) for v in range(vis)], axis=0
    )
    wide = ORDER * ORDER
    spread = jnp.where(iota((ORDER, wide), 1) % ORDER == iota((ORDER, wide), 0), 1.0, 0.0)
    flat = dot(coef, spread, HI)
    keep = iota((n, wide), 1) // ORDER == iota((n, wide), 0) % ORDER
    flat = jnp.where(keep, flat, 0.0)
    for v in range(vis):
        out_ref[v : v + 1] = jnp.sum(flat[v * ORDER : (v + 1) * ORDER], axis=0, keepdims=True)


def call(kernel, out_shape, scratch=(), n_in=1, smem=(), plain=()):
    fn = pl.pallas_call(
        kernel,
        out_shape=out_shape,
        in_specs=[SMEM if i in smem else VMEM for i in range(n_in)],
        out_specs=jax.tree.map(lambda _: VMEM, out_shape),
        scratch_shapes=list(scratch),
    )

    def run(*args):
        return fn(
            *(
                x if i in plain or i in smem else pltpu.with_memory_space_constraint(x, pltpu.VMEM)
                for i, x in enumerate(args)
            )
        )

    return run


def shape(dims, dtype=F32):
    return pltpu.VMEM(dims, dtype)


def result(dims, dtype=F32):
    return jax.ShapeDtypeStruct(dims, dtype)


def exchange(x, axis):
    return lax.all_to_all(x, axis, split_axis=0, concat_axis=0, tiled=True)


def per_device(raw_rows, resample, slot_row, tap_weight, patch_id, live_mask):
    owners = lax.axis_size("visit")
    ccd_devs = lax.axis_size("ccd")
    vis, rows, pix = raw_rows.shape
    slots = slot_row.shape[3]
    patches = owners * P_DEV
    blocks = patches // 128
    nvb = vis * ORDER
    lam, rot, cxt = constants(pix)
    lam_lane = np.zeros((8, 128))
    lam_lane[0, :nvb] = np.tile(lam, vis)
    lam_sub = np.broadcast_to(lam[:, None], (8, 128))
    lam_lane, lam_sub = jnp.asarray(lam_lane, F32), jnp.asarray(lam_sub, F32)
    cxt, rot = jnp.asarray(cxt, F32), jnp.asarray(rot, F32)
    srow, pid, live = slot_row[0, 0], patch_id[0, 0], live_mask[0, 0]
    weights = tap_weight[:, 0, 0]
    pay_rows = ORDER * blocks + P_DEV

    pay1, tsum, qsum = call(
        functools.partial(gather_kernel, ccd_devs),
        (
            shape((owners, pay_rows, 128), BF16),
            shape((patches, pix)),
            shape((nvb, pix)),
        ),
        scratch=(
            pltpu.VMEM((vis * rows + 16, pix), F32),
            pltpu.VMEM((owners, slots * TAPS), F32),
            pltpu.VMEM((owners, slots * TAPS), F32),
            pltpu.VMEM((owners, slots * TAPS), F32),
            pltpu.VMEM((patches, slots), F32),
        ),
        n_in=8,
        smem=(0,),
        plain=range(8),
    )(srow.reshape(-1), raw_rows, resample, srow, weights, pid, live, cxt)
    arr1 = exchange(pay1, "visit")
    mt, qb, sy, m = call(
        functools.partial(design_kernel, ccd_devs, rows),
        (
            shape((nvb, patches)),
            shape((ORDER, 128)),
            shape((ORDER, 128)),
            shape((patches, 128)),
        ),
        n_in=5,
        plain=(0, 1, 2, 4),
    )(srow, pid, live, qsum, cxt)
    back, den, pay2 = call(
        first_kernel,
        (
            shape((ORDER, patches)),
            shape((ORDER, patches)),
            shape((ccd_devs, 2 * ORDER, 128)),
        ),
        n_in=4,
    )(arr1, mt, qb, sy)
    arr2 = exchange(pay2, "ccd")
    sy_all, pay3 = call(
        model_kernel,
        (shape((ORDER, 128)), shape((owners, pay_rows, 128), BF16)),
        n_in=6,
    )(arr2, lam_lane, mt, m, tsum, cxt)
    arr3 = exchange(pay3, "visit")
    pay4 = call(
        second_kernel,
        shape((ccd_devs, ORDER, 128)),
        n_in=6,
    )(arr3, back, den, mt, qb, lam_sub)
    arr4 = exchange(pay4, "ccd")
    background = call(background_kernel, result((P_DEV, pix)), n_in=2)(arr3, den)
    offsets = call(final_kernel, result((vis, ORDER * ORDER)), n_in=4)(
        arr4, sy_all, lam_lane, rot
    )
    return offsets, background


def solution(mesh):
    in_specs = (
        P("visit", "ccd", None),
        P("visit", None, None),
        P("visit", "ccd", None, None),
        P(None, "visit", "ccd", None, None),
        P("visit", "ccd", None, None),
        P("visit", "ccd", None, None),
    )
    out_specs = (P("visit", None), P(("visit", "ccd"), None))
    return jax.shard_map(
        per_device, mesh=mesh, in_specs=in_specs, out_specs=out_specs, check_vma=False
    )
```

```python
import functools

import jax
import jax.numpy as jnp
import numpy as np
from jax import lax
from jax.experimental import pallas as pl
from jax.experimental.pallas import tpu as pltpu
from jax.sharding import PartitionSpec as P

ORDER = 8
TAPS = 4
P_DEV = 16
RIDGE = 1.0
UNROLL = 8
HI = lax.Precision.HIGHEST
F32 = jnp.float32
BF16 = jnp.bfloat16
VMEM = pl.BlockSpec(memory_space=pltpu.VMEM)
HBM = pl.BlockSpec(memory_space=pl.ANY)


def constants(pixels):
    x = (2 * np.arange(pixels) + 1) / pixels - 1.0
    cx = [np.ones_like(x), x]
    for _ in range(2, ORDER):
        cx.append(2 * x * cx[-1] - cx[-2])
    cx = np.stack(cx)
    lam, rot = np.linalg.eigh(cx @ cx.T)
    return lam, rot, rot.T @ cx


def dot(a, b, precision=None):
    return lax.dot_general(
        a, b, (((1,), (0,)), ((), ())), precision=precision, preferred_element_type=F32
    )


def dot_t(a, b, precision=None):
    return lax.dot_general(
        a, b, (((1,), (1,)), ((), ())), precision=precision, preferred_element_type=F32
    )


def split(x, parts):
    out = []
    for _ in range(parts):
        out.append(x.astype(BF16))
        x = x - out[-1].astype(F32)
    return out


def iota(shape, dim):
    return lax.broadcasted_iota(jnp.int32, shape, dim)


def cheb_rows(y, count):
    sub = iota(y.shape, 0)
    prev, cur = jnp.ones_like(y), y
    out = jnp.where(sub == 0, prev, cur)
    for k in range(2, count):
        prev, cur = cur, 2.0 * y * cur - prev
        out = jnp.where(sub == k, cur, out)
    return out


def coord(b_pos, ccd, rows_local, ccd_devs):
    base = (ccd * rows_local).astype(F32)
    return (2.0 * (base + b_pos) + float(TAPS)) / float(rows_local * ccd_devs) - 1.0


def gather_kernel(
    ccd_devs, rows_hbm, raw_hbm, res_hbm, srow_hbm, w_hbm, pid_hbm, live_hbm, cxt_hbm,
    pay_ref, t_ref, q_ref, res_sc, row_sc, code_sc, wi_sc, h_sc,
    rows_smem, raw_ref, res_ref, srow_ref, w_ref, pid_ref, live_ref, cxt_ref, sems,
):
    vis, rows, pix = raw_ref.shape
    owners, slots = srow_ref.shape
    wide = slots * TAPS
    ccd = lax.axis_index("ccd")
    small = [
        pltpu.make_async_copy(src, dst, sems.at[n])
        for n, (src, dst) in enumerate(
            ((srow_hbm, srow_ref), (pid_hbm, pid_ref), (live_hbm, live_ref), (w_hbm, w_ref))
        )
    ]
    index = pltpu.make_async_copy(rows_hbm, rows_smem, sems.at[4])
    warp = pltpu.make_async_copy(res_hbm, res_ref, sems.at[5])
    proj_copy = pltpu.make_async_copy(cxt_hbm, cxt_ref, sems.at[6 + vis])
    raw = [
        pltpu.make_async_copy(raw_hbm.at[v], raw_ref.at[v], sems.at[6 + v]) for v in range(vis)
    ]
    for copy in small + [warp] + raw + [index, proj_copy]:
        copy.start()
    for copy in small:
        copy.wait()
    off = iota((slots, wide), 1) - TAPS * iota((slots, wide), 0)
    rep = jnp.where((off >= 0) & (off < TAPS), 1.0, 0.0).astype(BF16)
    srow = srow_ref[...]
    code = pid_ref[...] + P_DEV * (1 - live_ref[...])
    high, low = srow >> 8, srow & 255
    whole = jnp.concatenate([high, low, code], axis=0).astype(F32).astype(BF16)
    whole = dot(whole, rep)
    row_sc[...] = 256.0 * whole[:owners] + whole[owners : 2 * owners]
    code_sc[...] = whole[2 * owners :]
    wi = None
    for t in range(TAPS):
        pick = jnp.where(off == t, 1.0, 0.0).astype(BF16)
        part = dot(w_ref[t].astype(BF16), pick)
        wi = part if wi is None else wi + part
    wi_sc[...] = wi
    q_ref[...] = jnp.zeros_like(q_ref)
    half = iota((8, pix), 0) < TAPS
    kid = iota((P_DEV, wide), 0).astype(F32)
    kid_s = iota((P_DEV, slots), 0)
    for copy in [warp] + raw + [index, proj_copy]:
        copy.wait()
    zero = jnp.zeros((pix, pix), BF16)
    for v in range(0, vis, 2):
        pair = jnp.concatenate([raw_ref[v], raw_ref[v + 1]], axis=1)
        diag = jnp.concatenate(
            [
                jnp.concatenate([res_ref[v], zero], axis=1),
                jnp.concatenate([zero, res_ref[v + 1]], axis=1),
            ],
            axis=0,
        )
        both = dot(pair, diag)
        res_sc[pl.ds(8 + v * rows, rows), :] = both[:, :pix]
        res_sc[pl.ds(8 + (v + 1) * rows, rows), :] = both[:, pix:]

    def body(j, carry):
        start = pl.multiple_of(j * slots, slots)
        row_at = [
            rows_smem.at[pl.ds(i, (owners - 1) * slots + 1)][start] for i in range(slots)
        ]
        pieces = []
        for g in range(slots // 4):
            pair = []
            for h in range(2):
                s = 4 * g + 2 * h
                first = res_sc[pl.ds(row_at[s] + 8, 8), :]
                second = res_sc[pl.ds(row_at[s + 1] + 4, 8), :]
                pair.append(jnp.where(half, first, second))
            pieces.append(jnp.concatenate(pair, axis=0).astype(BF16))
        taps = jnp.concatenate(pieces, axis=0)
        row = row_sc[pl.ds(j, 1), :]
        cod = code_sc[pl.ds(j, 1), :]
        wgt = wi_sc[pl.ds(j, 1), :]
        visit = jnp.floor(row * (1.0 / rows))
        y = coord(row - visit * rows, ccd, rows, ccd_devs)
        ty = cheb_rows(jnp.broadcast_to(y, (ORDER, wide)), ORDER)
        ty = ty * jnp.where(cod < float(P_DEV), wgt, 0.0)
        lhs = [jnp.where(cod == kid, wgt, 0.0)]
        for v in range(vis):
            lhs.append(jnp.where(visit == float(v), ty, 0.0))
        lhs = jnp.concatenate(lhs, axis=0).astype(BF16)
        sums = dot(lhs, taps)
        t_ref[pl.ds(pl.multiple_of(j * P_DEV, P_DEV), P_DEV), :] = sums[:P_DEV]
        q_ref[...] += sums[P_DEV:]
        live = live_ref[pl.ds(j, 1), :]
        member = jnp.where((pid_ref[pl.ds(j, 1), :] == kid_s) & (live > 0), 1.0, 0.0)
        h_sc[pl.ds(pl.multiple_of(j * P_DEV, P_DEV), P_DEV), :] = member.astype(BF16)
        return carry

    lax.fori_loop(0, owners, body, 0, unroll=UNROLL)
    c_hi, c_lo = split(cxt_ref[...], 2)
    t_hi, t_lo = split(t_ref[...], 2)
    proj = dot_t(jnp.concatenate([c_hi, c_lo], axis=0), t_hi)
    proj = proj[:ORDER] + proj[ORDER:] + dot_t(c_hi, t_lo)
    counts = dot_t(jnp.ones((8, slots), BF16), h_sc[...])
    blocks = owners * P_DEV // 128
    sub = iota((8, 128), 0)
    rows_out = [proj[:, 128 * q : 128 * (q + 1)] for q in range(blocks)]
    tail = jnp.zeros((8, 128), F32)
    for q in range(blocks):
        tail = jnp.where(sub == q, counts[0:1, 128 * q : 128 * (q + 1)], tail)
    block = jnp.concatenate(rows_out + [tail], axis=0).astype(BF16)
    for i in range(owners):
        pay_ref[i] = block


def design_kernel(
    ccd_devs, rows, srow_ref, pid_ref, live_ref, q_ref, cxt_ref,
    mt_ref, qb_ref, sy_ref, mw_ref, mtw_ref, m_sc,
):
    owners, slots = srow_ref.shape
    vis = q_ref.shape[0] // ORDER
    n = vis * ORDER
    ccd = lax.axis_index("ccd")
    kid = iota((P_DEV, slots), 0)
    m_sc[...] = jnp.zeros_like(m_sc)

    def body(j, acc):
        srow = srow_ref[pl.ds(j, 1), :]
        live = live_ref[pl.ds(j, 1), :]
        pid = pid_ref[pl.ds(j, 1), :]
        visit = srow // rows
        y = coord((srow - visit * rows).astype(F32), ccd, rows, ccd_devs)
        ty = cheb_rows(jnp.broadcast_to(y, (ORDER, slots)), ORDER)
        member = jnp.where((pid == kid) & (live > 0), 1.0, 0.0).astype(BF16)
        vt = jnp.concatenate(
            [jnp.where((visit == v) & (live > 0), ty, 0.0) for v in range(vis)], axis=0
        )
        parts = jnp.concatenate([p.astype(F32) for p in split(ty, 3)] + [jnp.zeros_like(ty)], axis=0)
        left = jnp.concatenate([member, parts.astype(BF16)], axis=0)
        both = None
        for piece in split(vt, 3):
            part = dot_t(left, piece)
            both = part if both is None else both + part
        m_sc[pl.ds(pl.multiple_of(j * P_DEV, P_DEV), P_DEV), 0:n] = both[:P_DEV]
        return acc + both[P_DEV:]

    sy = lax.fori_loop(0, owners, body, jnp.zeros((4 * ORDER, n), F32), unroll=4)
    sy = sy[:ORDER] + sy[ORDER : 2 * ORDER] + sy[2 * ORDER : 3 * ORDER]
    sy_ref[...] = jnp.concatenate([sy, jnp.zeros((ORDER, 128 - n), F32)], axis=1)
    m_hi, m_lo = split(m_sc[...], 2)
    mt = m_sc[...].T[:n]
    mt_ref[...] = mt
    mt_hi, mt_lo = split(mt, 2)
    mtw_ref[...] = jnp.concatenate([mt_hi, mt_hi, mt_lo, jnp.zeros_like(mt_hi)], axis=0)
    mw_ref[0] = m_hi
    mw_ref[1] = m_lo
    qb_ref[...] = blocks_of(dot_t(q_ref[...], tile_rows(cxt_ref[...], 128 // ORDER), HI), vis)


def tile_rows(x, times):
    return jnp.concatenate([x] * times, axis=0)


def blocks_of(full, vis):
    lane = iota((ORDER, full.shape[1]), 1) // ORDER
    out = jnp.zeros((ORDER, full.shape[1]), F32)
    for v in range(vis):
        out = out + jnp.where(lane == v, full[v * ORDER : (v + 1) * ORDER], 0.0)
    return out


def moments_block(mt, back, q, vis):
    full = None
    for i, piece in enumerate(back):
        part = dot_t(mt[:, 128 * i : 128 * (i + 1)], tile_rows(piece, 128 // ORDER), HI)
        full = part if full is None else full + part
    return q - blocks_of(full, vis)


def senders_sum(ref, lo, hi):
    total = ref[0, lo:hi].astype(F32)
    for i in range(1, ref.shape[0]):
        total = total + ref[i, lo:hi].astype(F32)
    return total


def first_kernel(arr_ref, mt_ref, qb_ref, sy_ref, b_ref, den_ref, pay_ref):
    blocks = b_ref.shape[1] // 128
    vis = mt_ref.shape[0] // ORDER
    total = senders_sum(arr_ref, 0, arr_ref.shape[1])
    back = []
    for q in range(blocks):
        den = total[ORDER * blocks + q : ORDER * blocks + q + 1] + 1.0
        den = jnp.broadcast_to(den, (ORDER, 128))
        piece = total[ORDER * q : ORDER * (q + 1)] / den
        den_ref[:, 128 * q : 128 * (q + 1)] = den
        b_ref[:, 128 * q : 128 * (q + 1)] = piece
        back.append(piece)
    mom = moments_block(mt_ref[...], back, qb_ref[...], vis)
    block = jnp.concatenate([mom, sy_ref[...]], axis=0)
    for i in range(pay_ref.shape[0]):
        pay_ref[i] = block


def solve(mom, sy, lam, vis):
    n = vis * ORDER
    rows, lanes = iota((n, ORDER * 128), 0), iota((n, ORDER * 128), 1)
    pos = lanes % 128
    pick = (rows // ORDER == pos // ORDER) & (rows % ORDER == lanes // 128)
    spread = dot(sy[:, :n], jnp.where(pick, 1.0, 0.0), HI)
    sub = iota((ORDER, 128), 0)
    mat = [
        spread[:, 128 * b : 128 * (b + 1)] * lam + jnp.where(sub == b, RIDGE, 0.0)
        for b in range(ORDER)
    ]
    rhs = [mom[b : b + 1] for b in range(ORDER)]
    for p in range(ORDER):
        inv = 1.0 / mat[p][p : p + 1]
        mat[p] = mat[p] * inv
        rhs[p] = rhs[p] * inv
        for b in range(ORDER):
            if b != p:
                factor = mat[b][p : p + 1]
                mat[b] = mat[b] - factor * mat[p]
                rhs[b] = rhs[b] - factor * rhs[p]
    out = jnp.zeros((ORDER, 128), F32)
    for b in range(ORDER):
        out = jnp.where(sub == b, rhs[b], out)
    return jnp.where(iota((ORDER, 128), 1) < n, out, 0.0)


def block_diag_t(z, vis):
    n = vis * ORDER
    tiled = tile_rows(z, vis)
    keep = iota((n, 128), 0) // ORDER == iota((n, 128), 1) // ORDER
    return jnp.where(keep, tiled, 0.0).T[:n]


def model_kernel(arr_ref, lam_ref, mtw_ref, mw_ref, t_ref, cxt_ref, sy_ref, pay_ref):
    vis = mtw_ref.shape[0] // (4 * ORDER)
    n = vis * ORDER
    total = arr_ref[0]
    for i in range(1, arr_ref.shape[0]):
        total = total + arr_ref[i]
    sy_ref[...] = total[ORDER:]
    z = solve(total[:ORDER], total[ORDER:], lam_ref[0:1], vis)
    diag = block_diag_t(z, vis)
    weights = diag[:ORDER]
    for v in range(1, vis):
        weights = weights + diag[v * ORDER : (v + 1) * ORDER]
    w_hi, w_lo = split(weights, 2)
    model = (
        dot(w_hi, mtw_ref[0:n])
        + dot(w_lo, mtw_ref[n : 2 * n])
        + dot(w_hi, mtw_ref[2 * n : 3 * n])
    )
    surface = lax.dot_general(
        weights, cxt_ref[...], (((0,), (0,)), ((), ())), precision=HI, preferred_element_type=F32
    )
    surface = jnp.concatenate([surface, jnp.zeros((128 - n, 128), F32)], axis=0)
    s_hi, s_lo = split(surface, 2)
    corrected = t_ref[...] - (dot(mw_ref[0], s_hi) + dot(mw_ref[0], s_lo) + dot(mw_ref[1], s_hi))
    blocks = model.shape[1] // 128
    block = jnp.concatenate(
        [model[:, 128 * q : 128 * (q + 1)] for q in range(blocks)], axis=0
    ).astype(BF16)
    rows = ORDER * blocks
    for i in range(pay_ref.shape[0]):
        pay_ref[i, 0:rows] = block
        pay_ref[i, rows : rows + P_DEV] = corrected[P_DEV * i : P_DEV * (i + 1)].astype(BF16)


def second_kernel(arr_ref, b_ref, den_ref, mt_ref, qb_ref, lam_ref, pay_ref):
    blocks = b_ref.shape[1] // 128
    vis = mt_ref.shape[0] // ORDER
    total = senders_sum(arr_ref, 0, ORDER * blocks)
    lam = lam_ref[:, 0:1]
    back = []
    for q in range(blocks):
        cols = slice(128 * q, 128 * (q + 1))
        model = total[ORDER * q : ORDER * (q + 1)]
        back.append(b_ref[:, cols] - lam * model / den_ref[:, cols])
    mom = moments_block(mt_ref[...], back, qb_ref[...], vis)
    for i in range(pay_ref.shape[0]):
        pay_ref[i] = mom


def background_kernel(arr_ref, den_ref, out_ref):
    rows = arr_ref.shape[1] - P_DEV
    sums = senders_sum(arr_ref, rows, rows + P_DEV)
    own = lax.axis_index("visit") * P_DEV
    width = den_ref.shape[1]
    pick = iota((P_DEV, width), 1) == iota((P_DEV, width), 0) + own
    den = dot_t(jnp.where(pick, 1.0, 0.0), den_ref[...], HI)
    out_ref[...] = sums / den[:, 0:1]


def final_kernel(arr_ref, sy_ref, lam_ref, rot_ref, out_ref):
    vis = out_ref.shape[0]
    n = vis * ORDER
    total = arr_ref[0]
    for i in range(1, arr_ref.shape[0]):
        total = total + arr_ref[i]
    z = solve(total, sy_ref[...], lam_ref[0:1], vis)
    flat = tile_rows(z, ORDER).T[:n] * tile_rows(rot_ref[...], vis)
    for v in range(vis):
        out_ref[v : v + 1] = jnp.sum(flat[v * ORDER : (v + 1) * ORDER], axis=0, keepdims=True)


def call(kernel, out_shape, scratch=(), n_in=1, hbm=(), plain=()):
    fn = pl.pallas_call(
        kernel,
        out_shape=out_shape,
        in_specs=[HBM if i in hbm else VMEM for i in range(n_in)],
        out_specs=jax.tree.map(lambda _: VMEM, out_shape),
        scratch_shapes=list(scratch),
    )

    def run(*args):
        return fn(
            *(
                x if i in plain or i in hbm else pltpu.with_memory_space_constraint(x, pltpu.VMEM)
                for i, x in enumerate(args)
            )
        )

    return run


def shape(dims, dtype=F32):
    return pltpu.VMEM(dims, dtype)


def result(dims, dtype=F32):
    return jax.ShapeDtypeStruct(dims, dtype)


def exchange(x, axis):
    return lax.all_to_all(x, axis, split_axis=0, concat_axis=0, tiled=True)


def per_device(raw_rows, resample, slot_row, tap_weight, patch_id, live_mask):
    owners = lax.axis_size("visit")
    ccd_devs = lax.axis_size("ccd")
    vis, rows, pix = raw_rows.shape
    slots = slot_row.shape[3]
    patches = owners * P_DEV
    blocks = patches // 128
    nvb = vis * ORDER
    lam, rot, cxt = constants(pix)
    lam_lane = np.zeros((8, 128))
    lam_lane[0, :nvb] = np.tile(lam, vis)
    lam_sub = np.broadcast_to(lam[:, None], (8, 128))
    lam_lane, lam_sub = jnp.asarray(lam_lane, F32), jnp.asarray(lam_sub, F32)
    cxt = jnp.asarray(cxt, F32)
    rot = jnp.asarray(np.repeat(rot.T, ORDER, axis=1), F32)
    srow, pid, live = slot_row[0, 0], patch_id[0, 0], live_mask[0, 0]
    weights = tap_weight[:, 0, 0]
    pay_rows = ORDER * blocks + P_DEV

    pay1, tsum, qsum = call(
        functools.partial(gather_kernel, ccd_devs),
        (
            shape((owners, ORDER * blocks + 8, 128), BF16),
            shape((patches, pix)),
            shape((nvb, pix)),
        ),
        scratch=(
            pltpu.VMEM((vis * rows + 16, pix), F32),
            pltpu.VMEM((owners, slots * TAPS), F32),
            pltpu.VMEM((owners, slots * TAPS), F32),
            pltpu.VMEM((owners, slots * TAPS), F32),
            pltpu.VMEM((patches, slots), BF16),
            pltpu.SMEM((owners * slots,), jnp.int32),
            pltpu.VMEM(raw_rows.shape, BF16),
            pltpu.VMEM(resample.shape, BF16),
            pltpu.VMEM((owners, slots), jnp.int32),
            pltpu.VMEM((TAPS, owners, slots), F32),
            pltpu.VMEM((owners, slots), jnp.int32),
            pltpu.VMEM((owners, slots), jnp.int32),
            pltpu.VMEM((ORDER, pix), F32),
            pltpu.SemaphoreType.DMA((7 + vis,)),
        ),
        n_in=8,
        hbm=range(8),
    )(srow.reshape(-1), raw_rows, resample, srow, weights, pid, live, cxt)
    arr1 = exchange(pay1, "visit")
    mt, qb, sy, mw, mtw = call(
        functools.partial(design_kernel, ccd_devs, rows),
        (
            shape((nvb, patches)),
            shape((ORDER, 128)),
            shape((ORDER, 128)),
            shape((2, patches, 128), BF16),
            shape((4 * nvb, patches), BF16),
        ),
        scratch=(pltpu.VMEM((patches, 128), F32),),
        n_in=5,
        plain=(0, 1, 2, 4),
    )(srow, pid, live, qsum, cxt)
    back, den, pay2 = call(
        first_kernel,
        (
            shape((ORDER, patches)),
            shape((ORDER, patches)),
            shape((ccd_devs, 2 * ORDER, 128)),
        ),
        n_in=4,
    )(arr1, mt, qb, sy)
    arr2 = exchange(pay2, "ccd")
    sy_all, pay3 = call(
        model_kernel,
        (shape((ORDER, 128)), shape((owners, pay_rows, 128), BF16)),
        n_in=6,
    )(arr2, lam_lane, mtw, mw, tsum, cxt)
    arr3 = exchange(pay3, "visit")
    pay4 = call(
        second_kernel,
        shape((ccd_devs, ORDER, 128)),
        n_in=6,
    )(arr3, back, den, mt, qb, lam_sub)
    arr4 = exchange(pay4, "ccd")
    background = call(background_kernel, result((P_DEV, pix)), n_in=2)(arr3, den)
    offsets = call(final_kernel, result((vis, ORDER * ORDER)), n_in=4)(
        arr4, sy_all, lam_lane, rot
    )
    return offsets, background


def solution(mesh):
    in_specs = (
        P("visit", "ccd", None),
        P("visit", None, None),
        P("visit", "ccd", None, None),
        P(None, "visit", "ccd", None, None),
        P("visit", "ccd", None, None),
        P("visit", "ccd", None, None),
    )
    out_specs = (P("visit", None), P(("visit", "ccd"), None))
    return jax.shard_map(
        per_device, mesh=mesh, in_specs=in_specs, out_specs=out_specs, check_vma=False
    )
```

```python
import functools

import jax
import jax.numpy as jnp
import numpy as np
from jax import lax
from jax.experimental import pallas as pl
from jax.experimental.pallas import tpu as pltpu
from jax.sharding import PartitionSpec as P

ORDER = 8
TAPS = 4
P_DEV = 16
RIDGE = 1.0
UNROLL = 8
CXT, LAM_LANE, LAM_SUB, ROT = (slice(8 * i, 8 * (i + 1)) for i in range(4))
HI = lax.Precision.HIGHEST
F32 = jnp.float32
BF16 = jnp.bfloat16
VMEM = pl.BlockSpec(memory_space=pltpu.VMEM)
HBM = pl.BlockSpec(memory_space=pl.ANY)


def constants(pixels):
    x = (2 * np.arange(pixels) + 1) / pixels - 1.0
    cx = [np.ones_like(x), x]
    for _ in range(2, ORDER):
        cx.append(2 * x * cx[-1] - cx[-2])
    cx = np.stack(cx)
    lam, rot = np.linalg.eigh(cx @ cx.T)
    return lam, rot, rot.T @ cx


def dot(a, b, precision=None):
    return lax.dot_general(
        a, b, (((1,), (0,)), ((), ())), precision=precision, preferred_element_type=F32
    )


def dot_t(a, b, precision=None):
    return lax.dot_general(
        a, b, (((1,), (1,)), ((), ())), precision=precision, preferred_element_type=F32
    )


def split(x, parts):
    out = []
    for _ in range(parts):
        out.append(x.astype(BF16))
        x = x - out[-1].astype(F32)
    return out


def iota(shape, dim):
    return lax.broadcasted_iota(jnp.int32, shape, dim)


def cheb_rows(y, count):
    sub = iota(y.shape, 0)
    prev, cur = jnp.ones_like(y), y
    out = jnp.where(sub == 0, prev, cur)
    for k in range(2, count):
        prev, cur = cur, 2.0 * y * cur - prev
        out = jnp.where(sub == k, cur, out)
    return out


def coord(b_pos, ccd, rows_local, ccd_devs):
    base = (ccd * rows_local).astype(F32)
    return (2.0 * (base + b_pos) + float(TAPS)) / float(rows_local * ccd_devs) - 1.0


def gather_kernel(
    ccd_devs, rows_hbm, raw_hbm, res_hbm, srow_hbm, w_hbm, pid_hbm, live_hbm, cxt_hbm,
    pay_ref, t_ref, q_ref, res_sc, row_sc, code_sc, wi_sc, h_sc,
    rows_smem, raw_ref, res_ref, srow_ref, w_ref, pid_ref, live_ref, cxt_ref, sems,
):
    vis, rows, pix = raw_ref.shape
    owners, slots = srow_ref.shape
    wide = slots * TAPS
    ccd = lax.axis_index("ccd")
    small = [
        pltpu.make_async_copy(src, dst, sems.at[n])
        for n, (src, dst) in enumerate(
            ((srow_hbm, srow_ref), (pid_hbm, pid_ref), (live_hbm, live_ref), (w_hbm, w_ref))
        )
    ]
    index = pltpu.make_async_copy(rows_hbm, rows_smem, sems.at[4])
    warp = pltpu.make_async_copy(res_hbm, res_ref, sems.at[5])
    proj_copy = pltpu.make_async_copy(cxt_hbm.at[CXT], cxt_ref, sems.at[6 + vis])
    raw = [
        pltpu.make_async_copy(raw_hbm.at[v], raw_ref.at[v], sems.at[6 + v]) for v in range(vis)
    ]
    for copy in small + [warp] + raw + [index, proj_copy]:
        copy.start()
    for copy in small:
        copy.wait()
    off = iota((slots, wide), 1) - TAPS * iota((slots, wide), 0)
    rep = jnp.where((off >= 0) & (off < TAPS), 1.0, 0.0).astype(BF16)
    srow = srow_ref[...]
    code = pid_ref[...] + P_DEV * (1 - live_ref[...])
    high, low = srow >> 8, srow & 255
    whole = jnp.concatenate([high, low, code], axis=0).astype(F32).astype(BF16)
    whole = dot(whole, rep)
    row_sc[...] = 256.0 * whole[:owners] + whole[owners : 2 * owners]
    code_sc[...] = whole[2 * owners :]
    wi = None
    for t in range(TAPS):
        pick = jnp.where(off == t, 1.0, 0.0).astype(BF16)
        part = dot(w_ref[t].astype(BF16), pick)
        wi = part if wi is None else wi + part
    wi_sc[...] = wi
    q_ref[...] = jnp.zeros_like(q_ref)
    half = iota((8, pix), 0) < TAPS
    kid = iota((P_DEV, wide), 0).astype(F32)
    kid_s = iota((P_DEV, slots), 0)
    for copy in [warp] + raw + [index, proj_copy]:
        copy.wait()
    zero = jnp.zeros((pix, pix), BF16)
    for v in range(0, vis, 2):
        pair = jnp.concatenate([raw_ref[v], raw_ref[v + 1]], axis=1)
        diag = jnp.concatenate(
            [
                jnp.concatenate([res_ref[v], zero], axis=1),
                jnp.concatenate([zero, res_ref[v + 1]], axis=1),
            ],
            axis=0,
        )
        both = dot(pair, diag)
        res_sc[pl.ds(8 + v * rows, rows), :] = both[:, :pix]
        res_sc[pl.ds(8 + (v + 1) * rows, rows), :] = both[:, pix:]

    def body(j, carry):
        start = pl.multiple_of(j * slots, slots)
        row_at = [
            rows_smem.at[pl.ds(i, (owners - 1) * slots + 1)][start] for i in range(slots)
        ]
        pieces = []
        for g in range(slots // 4):
            pair = []
            for h in range(2):
                s = 4 * g + 2 * h
                first = res_sc[pl.ds(row_at[s] + 8, 8), :]
                second = res_sc[pl.ds(row_at[s + 1] + 4, 8), :]
                pair.append(jnp.where(half, first, second))
            pieces.append(jnp.concatenate(pair, axis=0).astype(BF16))
        taps = jnp.concatenate(pieces, axis=0)
        row = row_sc[pl.ds(j, 1), :]
        cod = code_sc[pl.ds(j, 1), :]
        wgt = wi_sc[pl.ds(j, 1), :]
        visit = jnp.floor(row * (1.0 / rows))
        y = coord(row - visit * rows, ccd, rows, ccd_devs)
        ty = cheb_rows(jnp.broadcast_to(y, (ORDER, wide)), ORDER)
        ty = ty * jnp.where(cod < float(P_DEV), wgt, 0.0)
        lhs = [jnp.where(cod == kid, wgt, 0.0)]
        for v in range(vis):
            lhs.append(jnp.where(visit == float(v), ty, 0.0))
        lhs = jnp.concatenate(lhs, axis=0).astype(BF16)
        sums = dot(lhs, taps)
        t_ref[pl.ds(pl.multiple_of(j * P_DEV, P_DEV), P_DEV), :] = sums[:P_DEV]
        q_ref[...] += sums[P_DEV:]
        live = live_ref[pl.ds(j, 1), :]
        member = jnp.where((pid_ref[pl.ds(j, 1), :] == kid_s) & (live > 0), 1.0, 0.0)
        h_sc[pl.ds(pl.multiple_of(j * P_DEV, P_DEV), P_DEV), :] = member.astype(BF16)
        return carry

    lax.fori_loop(0, owners, body, 0, unroll=UNROLL)
    c_hi, c_lo = split(cxt_ref[...], 2)
    t_hi, t_lo = split(t_ref[...], 2)
    proj = dot_t(jnp.concatenate([c_hi, c_lo], axis=0), t_hi)
    proj = proj[:ORDER] + proj[ORDER:] + dot_t(c_hi, t_lo)
    counts = dot_t(jnp.ones((8, slots), BF16), h_sc[...])
    blocks = owners * P_DEV // 128
    sub = iota((8, 128), 0)
    rows_out = [proj[:, 128 * q : 128 * (q + 1)] for q in range(blocks)]
    tail = jnp.zeros((8, 128), F32)
    for q in range(blocks):
        tail = jnp.where(sub == q, counts[0:1, 128 * q : 128 * (q + 1)], tail)
    block = jnp.concatenate(rows_out + [tail], axis=0).astype(BF16)
    for i in range(owners):
        pay_ref[i] = block


def design_kernel(
    ccd_devs, rows, srow_ref, pid_ref, live_ref, q_ref, const_ref,
    qb_ref, sy_ref, mw_ref, mtw_ref, keep_ref, m_sc,
):
    owners, slots = srow_ref.shape
    vis = q_ref.shape[0] // ORDER
    n = vis * ORDER
    ccd = lax.axis_index("ccd")
    kid = iota((P_DEV, slots), 0)
    m_sc[...] = jnp.zeros_like(m_sc)

    def body(j, acc):
        srow = srow_ref[pl.ds(j, 1), :]
        live = live_ref[pl.ds(j, 1), :]
        pid = pid_ref[pl.ds(j, 1), :]
        visit = srow // rows
        y = coord((srow - visit * rows).astype(F32), ccd, rows, ccd_devs)
        ty = cheb_rows(jnp.broadcast_to(y, (ORDER, slots)), ORDER)
        member = jnp.where((pid == kid) & (live > 0), 1.0, 0.0).astype(BF16)
        vt = jnp.concatenate(
            [jnp.where((visit == v) & (live > 0), ty, 0.0) for v in range(vis)], axis=0
        )
        parts = jnp.concatenate([p.astype(F32) for p in split(ty, 3)] + [jnp.zeros_like(ty)], axis=0)
        left = jnp.concatenate([member, parts.astype(BF16)], axis=0)
        both = None
        for piece in split(vt, 3):
            part = dot_t(left, piece)
            both = part if both is None else both + part
        m_sc[pl.ds(pl.multiple_of(j * P_DEV, P_DEV), P_DEV), 0:n] = both[:P_DEV]
        return acc + both[P_DEV:]

    sy = lax.fori_loop(0, owners, body, jnp.zeros((4 * ORDER, n), F32), unroll=4)
    sy = sy[:ORDER] + sy[ORDER : 2 * ORDER] + sy[2 * ORDER : 3 * ORDER]
    sy_ref[...] = widen(sy)
    m_hi, m_lo = split(m_sc[...], 2)
    mtw_ref[...] = jnp.concatenate(split(m_sc[...].T[:n], 2), axis=0)
    keep_ref[...] = const_ref[...]
    mw_ref[0] = m_hi
    mw_ref[1] = m_lo
    full = dot_t(q_ref[...], tile_rows(const_ref[CXT], vis), HI)
    qb_ref[...] = widen(blocks_of(full, vis))


def tile_rows(x, times):
    return jnp.concatenate([x] * times, axis=0)


def blocks_of(full, vis):
    lane = iota((ORDER, full.shape[1]), 1) // ORDER
    out = jnp.zeros((ORDER, full.shape[1]), F32)
    for v in range(vis):
        out = out + jnp.where(lane == v, full[v * ORDER : (v + 1) * ORDER], 0.0)
    return out


def widen(x):
    return jnp.concatenate([x, jnp.zeros((x.shape[0], 128 - x.shape[1]), F32)], axis=1)


def moments_block(mtw_ref, back, q):
    n = mtw_ref.shape[0] // 2
    vis = n // ORDER
    b_hi, b_lo = split(back, 2)
    b_hi, b_lo = (tile_rows(x.astype(F32), vis).astype(BF16) for x in (b_hi, b_lo))
    full = dot_t(mtw_ref[...], b_hi)
    full = full[:n] + full[n:] + dot_t(mtw_ref[0:n], b_lo)
    return q - widen(blocks_of(full, vis))


def senders_sum(ref, lo, hi):
    total = ref[0, lo:hi].astype(F32)
    for i in range(1, ref.shape[0]):
        total = total + ref[i, lo:hi].astype(F32)
    return total


def first_kernel(arr_ref, mtw_ref, qb_ref, sy_ref, b_ref, den_ref, pay_ref):
    blocks = b_ref.shape[1] // 128
    total = senders_sum(arr_ref, 0, arr_ref.shape[1])
    back, dens = [], []
    for q in range(blocks):
        den = total[ORDER * blocks + q : ORDER * blocks + q + 1] + 1.0
        dens.append(jnp.broadcast_to(den, (ORDER, 128)))
        back.append(total[ORDER * q : ORDER * (q + 1)] / dens[-1])
    back = jnp.concatenate(back, axis=1)
    den_ref[...] = jnp.concatenate(dens, axis=1)
    b_ref[...] = back
    mom = moments_block(mtw_ref, back, qb_ref[...])
    block = jnp.concatenate([mom, sy_ref[...]], axis=0)
    for i in range(pay_ref.shape[0]):
        pay_ref[i] = block


def systems(sy, lam, vis):
    n = vis * ORDER
    rows, lanes = iota((n, ORDER * 128), 0), iota((n, ORDER * 128), 1)
    pos = lanes % 128
    pick = (rows // ORDER == pos // ORDER) & (rows % ORDER == lanes // 128)
    spread = dot(sy[:, :n], jnp.where(pick, 1.0, 0.0), HI)
    sub = iota((ORDER, 128), 0)
    return [
        spread[:, 128 * b : 128 * (b + 1)] * lam + jnp.where(sub == b, RIDGE, 0.0)
        for b in range(ORDER)
    ]


def eliminate(mat, rhs):
    mat, rhs = list(mat), list(rhs)
    for p in range(ORDER):
        inv = 1.0 / mat[p][p : p + 1]
        mat[p] = mat[p] * inv
        rhs[p] = rhs[p] * inv
        for b in range(ORDER):
            if b != p:
                factor = mat[b][p : p + 1]
                mat[b] = mat[b] - factor * mat[p]
                rhs[b] = rhs[b] - factor * rhs[p]
    return rhs


def solve(mom, sy, lam, vis):
    rhs = eliminate(systems(sy, lam, vis), [mom[b : b + 1] for b in range(ORDER)])
    sub = iota((ORDER, 128), 0)
    out = jnp.zeros((ORDER, 128), F32)
    for b in range(ORDER):
        out = jnp.where(sub == b, rhs[b], out)
    return jnp.where(iota((ORDER, 128), 1) < vis * ORDER, out, 0.0)


def block_diag_t(z, vis):
    n = vis * ORDER
    tiled = tile_rows(z, vis)
    keep = iota((n, 128), 0) // ORDER == iota((n, 128), 1) // ORDER
    return jnp.where(keep, tiled, 0.0).T[:n]


def model_kernel(arr_ref, const_ref, mtw_ref, mw_ref, t_ref, sy_ref, pay_ref):
    vis = mtw_ref.shape[0] // (2 * ORDER)
    n = vis * ORDER
    total = arr_ref[0]
    for i in range(1, arr_ref.shape[0]):
        total = total + arr_ref[i]
    sy_ref[...] = total[ORDER:]
    z = solve(total[:ORDER], total[ORDER:], const_ref[LAM_LANE], vis)
    diag = block_diag_t(z, vis)
    weights = diag[:ORDER]
    for v in range(1, vis):
        weights = weights + diag[v * ORDER : (v + 1) * ORDER]
    w_hi, w_lo = split(weights, 2)
    model = (
        dot(w_hi, mtw_ref[0:n]) + dot(w_lo, mtw_ref[0:n]) + dot(w_hi, mtw_ref[n : 2 * n])
    )
    surface = lax.dot_general(
        weights, const_ref[CXT], (((0,), (0,)), ((), ())), precision=HI, preferred_element_type=F32
    )
    surface = jnp.concatenate([surface, jnp.zeros((128 - n, 128), F32)], axis=0)
    s_hi, s_lo = split(surface, 2)
    corrected = t_ref[...] - (dot(mw_ref[0], s_hi) + dot(mw_ref[0], s_lo) + dot(mw_ref[1], s_hi))
    blocks = model.shape[1] // 128
    block = jnp.concatenate(
        [model[:, 128 * q : 128 * (q + 1)] for q in range(blocks)], axis=0
    ).astype(BF16)
    rows = ORDER * blocks
    for i in range(pay_ref.shape[0]):
        pay_ref[i, 0:rows] = block
        pay_ref[i, rows : rows + P_DEV] = corrected[P_DEV * i : P_DEV * (i + 1)].astype(BF16)


def second_kernel(arr_ref, b_ref, den_ref, mtw_ref, qb_ref, const_ref, pay_ref):
    blocks = b_ref.shape[1] // 128
    total = senders_sum(arr_ref, 0, ORDER * blocks)
    model = jnp.concatenate(
        [total[ORDER * q : ORDER * (q + 1)] for q in range(blocks)], axis=1
    )
    lam = const_ref[LAM_SUB][:, 0:1]
    mom = moments_block(mtw_ref, b_ref[...] - lam * model / den_ref[...], qb_ref[...])
    for i in range(pay_ref.shape[0]):
        pay_ref[i] = mom


def background_kernel(vis, arr_ref, den_ref, sy_ref, const_ref, out_ref, inv_ref):
    rows = arr_ref.shape[1] - P_DEV
    sums = senders_sum(arr_ref, rows, rows + P_DEV)
    own = lax.axis_index("visit") * P_DEV
    width = den_ref.shape[1]
    pick = iota((P_DEV, width), 1) == iota((P_DEV, width), 0) + own
    den = dot_t(jnp.where(pick, 1.0, 0.0), den_ref[...], HI)
    out_ref[...] = sums / den[:, 0:1]
    sub = iota((ORDER, 128), 0)
    unit = [jnp.where(sub == b, 1.0, 0.0) for b in range(ORDER)]
    inverse = eliminate(systems(sy_ref[...], const_ref[LAM_LANE], vis), unit)
    for b in range(ORDER):
        inv_ref[b] = inverse[b]


def final_kernel(arr_ref, inv_ref, const_ref, out_ref):
    vis = out_ref.shape[0]
    n = vis * ORDER
    total = arr_ref[0]
    for i in range(1, arr_ref.shape[0]):
        total = total + arr_ref[i]
    z = inv_ref[0] * total[0:1]
    for d in range(1, ORDER):
        z = z + inv_ref[d] * total[d : d + 1]
    flat = tile_rows(z, ORDER).T[:n] * tile_rows(const_ref[ROT][:, : ORDER * ORDER], vis)
    for v in range(vis):
        out_ref[v : v + 1] = jnp.sum(flat[v * ORDER : (v + 1) * ORDER], axis=0, keepdims=True)


def call(kernel, out_shape, scratch=(), n_in=1, hbm=(), plain=()):
    fn = pl.pallas_call(
        kernel,
        out_shape=out_shape,
        in_specs=[HBM if i in hbm else VMEM for i in range(n_in)],
        out_specs=jax.tree.map(lambda _: VMEM, out_shape),
        scratch_shapes=list(scratch),
    )

    def run(*args):
        return fn(
            *(
                x if i in plain or i in hbm else pltpu.with_memory_space_constraint(x, pltpu.VMEM)
                for i, x in enumerate(args)
            )
        )

    return run


def shape(dims, dtype=F32):
    return pltpu.VMEM(dims, dtype)


def result(dims, dtype=F32):
    return jax.ShapeDtypeStruct(dims, dtype)


def exchange(x, axis):
    return lax.all_to_all(x, axis, split_axis=0, concat_axis=0, tiled=True)


def per_device(raw_rows, resample, slot_row, tap_weight, patch_id, live_mask):
    owners = lax.axis_size("visit")
    ccd_devs = lax.axis_size("ccd")
    vis, rows, pix = raw_rows.shape
    slots = slot_row.shape[3]
    patches = owners * P_DEV
    blocks = patches // 128
    nvb = vis * ORDER
    lam, rot, cxt = constants(pix)
    const = np.zeros((32, 128))
    const[CXT] = cxt
    const[LAM_LANE, :nvb] = np.tile(lam, vis)
    const[LAM_SUB] = lam[:, None]
    const[ROT, : ORDER * ORDER] = np.repeat(rot.T, ORDER, axis=1)
    const = jnp.asarray(const, F32)
    srow, pid, live = slot_row[0, 0], patch_id[0, 0], live_mask[0, 0]
    weights = tap_weight[:, 0, 0]
    pay_rows = ORDER * blocks + P_DEV

    pay1, tsum, qsum = call(
        functools.partial(gather_kernel, ccd_devs),
        (
            shape((owners, ORDER * blocks + 8, 128), BF16),
            shape((patches, pix)),
            shape((nvb, pix)),
        ),
        scratch=(
            pltpu.VMEM((vis * rows + 16, pix), F32),
            pltpu.VMEM((owners, slots * TAPS), F32),
            pltpu.VMEM((owners, slots * TAPS), F32),
            pltpu.VMEM((owners, slots * TAPS), F32),
            pltpu.VMEM((patches, slots), BF16),
            pltpu.SMEM((owners * slots,), jnp.int32),
            pltpu.VMEM(raw_rows.shape, BF16),
            pltpu.VMEM(resample.shape, BF16),
            pltpu.VMEM((owners, slots), jnp.int32),
            pltpu.VMEM((TAPS, owners, slots), F32),
            pltpu.VMEM((owners, slots), jnp.int32),
            pltpu.VMEM((owners, slots), jnp.int32),
            pltpu.VMEM((ORDER, pix), F32),
            pltpu.SemaphoreType.DMA((7 + vis,)),
        ),
        n_in=8,
        hbm=range(8),
    )(srow.reshape(-1), raw_rows, resample, srow, weights, pid, live, const)
    arr1 = exchange(pay1, "visit")
    qb, sy, mw, mtw, const = call(
        functools.partial(design_kernel, ccd_devs, rows),
        (
            shape((ORDER, 128)),
            shape((ORDER, 128)),
            shape((2, patches, 128), BF16),
            shape((2 * nvb, patches), BF16),
            shape(const.shape),
        ),
        scratch=(pltpu.VMEM((patches, 128), F32),),
        n_in=5,
        plain=(0, 1, 2, 4),
    )(srow, pid, live, qsum, const)
    back, den, pay2 = call(
        first_kernel,
        (
            shape((ORDER, patches)),
            shape((ORDER, patches)),
            shape((ccd_devs, 2 * ORDER, 128)),
        ),
        n_in=4,
    )(arr1, mtw, qb, sy)
    arr2 = exchange(pay2, "ccd")
    sy_all, pay3 = call(
        model_kernel,
        (shape((ORDER, 128)), shape((owners, pay_rows, 128), BF16)),
        n_in=5,
    )(arr2, const, mtw, mw, tsum)
    arr3 = exchange(pay3, "visit")
    pay4 = call(second_kernel, shape((ccd_devs, ORDER, 128)), n_in=6)(
        arr3, back, den, mtw, qb, const
    )
    arr4 = exchange(pay4, "ccd")
    background, inverse = call(
        functools.partial(background_kernel, vis),
        (result((P_DEV, pix)), shape((ORDER, ORDER, 128))),
        n_in=4,
    )(arr3, den, sy_all, const)
    offsets = call(final_kernel, result((vis, ORDER * ORDER)), n_in=3)(arr4, inverse, const)
    return offsets, background


def solution(mesh):
    in_specs = (
        P("visit", "ccd", None),
        P("visit", None, None),
        P("visit", "ccd", None, None),
        P(None, "visit", "ccd", None, None),
        P("visit", "ccd", None, None),
        P("visit", "ccd", None, None),
    )
    out_specs = (P("visit", None), P(("visit", "ccd"), None))
    return jax.shard_map(
        per_device, mesh=mesh, in_specs=in_specs, out_specs=out_specs, check_vma=False
    )
```

```python
import functools

import jax
import jax.numpy as jnp
import numpy as np
from jax import lax
from jax.experimental import pallas as pl
from jax.experimental.pallas import tpu as pltpu
from jax.sharding import PartitionSpec as P

ORDER = 8
TAPS = 4
P_DEV = 16
RIDGE = 1.0
UNROLL = 16
CXT, LAM_LANE, LAM_SUB, ROT = (slice(8 * i, 8 * (i + 1)) for i in range(4))
HI = lax.Precision.HIGHEST
F32 = jnp.float32
BF16 = jnp.bfloat16
VMEM = pl.BlockSpec(memory_space=pltpu.VMEM)
HBM = pl.BlockSpec(memory_space=pl.ANY)


def constants(pixels):
    x = (2 * np.arange(pixels) + 1) / pixels - 1.0
    cx = [np.ones_like(x), x]
    for _ in range(2, ORDER):
        cx.append(2 * x * cx[-1] - cx[-2])
    cx = np.stack(cx)
    lam, rot = np.linalg.eigh(cx @ cx.T)
    return lam, rot, rot.T @ cx


def dot(a, b, precision=None):
    return lax.dot_general(
        a, b, (((1,), (0,)), ((), ())), precision=precision, preferred_element_type=F32
    )


def dot_t(a, b, precision=None):
    return lax.dot_general(
        a, b, (((1,), (1,)), ((), ())), precision=precision, preferred_element_type=F32
    )


def split(x, parts):
    out = []
    for _ in range(parts):
        out.append(x.astype(BF16))
        x = x - out[-1].astype(F32)
    return out


def iota(shape, dim):
    return lax.broadcasted_iota(jnp.int32, shape, dim)


def cheb_rows(y, count):
    sub = iota(y.shape, 0)
    prev, cur = jnp.ones_like(y), y
    out = jnp.where(sub == 0, prev, cur)
    for k in range(2, count):
        prev, cur = cur, 2.0 * y * cur - prev
        out = jnp.where(sub == k, cur, out)
    return out


def coord(b_pos, ccd, rows_local, ccd_devs):
    base = (ccd * rows_local).astype(F32)
    return (2.0 * (base + b_pos) + float(TAPS)) / float(rows_local * ccd_devs) - 1.0


def gather_kernel(
    ccd_devs, rows_hbm, raw_hbm, res_hbm, srow_hbm, w_hbm, pid_hbm, live_hbm, cxt_hbm,
    pay_ref, t_ref, q_ref, res_sc, row_sc, code_sc, wi_sc, h_sc,
    rows_smem, raw_ref, res_ref, srow_ref, w_ref, pid_ref, live_ref, cxt_ref, sems,
):
    vis, rows, pix = raw_ref.shape
    owners, slots = srow_ref.shape
    wide = slots * TAPS
    ccd = lax.axis_index("ccd")
    small = [
        pltpu.make_async_copy(src, dst, sems.at[n])
        for n, (src, dst) in enumerate(
            ((srow_hbm, srow_ref), (pid_hbm, pid_ref), (live_hbm, live_ref), (w_hbm, w_ref))
        )
    ]
    index = pltpu.make_async_copy(rows_hbm, rows_smem, sems.at[4])
    warp = pltpu.make_async_copy(res_hbm, res_ref, sems.at[5])
    proj_copy = pltpu.make_async_copy(cxt_hbm.at[CXT], cxt_ref, sems.at[6 + vis])
    raw = [
        pltpu.make_async_copy(raw_hbm.at[v], raw_ref.at[v], sems.at[6 + v]) for v in range(vis)
    ]
    for copy in small + [warp] + raw + [index, proj_copy]:
        copy.start()
    for copy in small:
        copy.wait()
    off = iota((slots, wide), 1) - TAPS * iota((slots, wide), 0)
    rep = jnp.where((off >= 0) & (off < TAPS), 1.0, 0.0).astype(BF16)
    srow = srow_ref[...]
    code = pid_ref[...] + P_DEV * (1 - live_ref[...])
    high, low = srow >> 8, srow & 255
    whole = jnp.concatenate([high, low, code], axis=0).astype(F32).astype(BF16)
    whole = dot(whole, rep)
    row_sc[...] = 256.0 * whole[:owners] + whole[owners : 2 * owners]
    code_sc[...] = whole[2 * owners :]
    wi = None
    for t in range(TAPS):
        pick = jnp.where(off == t, 1.0, 0.0).astype(BF16)
        part = dot(w_ref[t].astype(BF16), pick)
        wi = part if wi is None else wi + part
    wi_sc[...] = wi
    q_ref[...] = jnp.zeros_like(q_ref)
    half = iota((8, pix), 0) < TAPS
    kid = iota((P_DEV, wide), 0).astype(F32)
    kid_s = iota((P_DEV, slots), 0)
    for copy in [warp] + raw + [index, proj_copy]:
        copy.wait()
    zero = jnp.zeros((pix, pix), BF16)
    for v in range(0, vis, 2):
        pair = jnp.concatenate([raw_ref[v], raw_ref[v + 1]], axis=1)
        diag = jnp.concatenate(
            [
                jnp.concatenate([res_ref[v], zero], axis=1),
                jnp.concatenate([zero, res_ref[v + 1]], axis=1),
            ],
            axis=0,
        )
        both = dot(pair, diag)
        res_sc[pl.ds(8 + v * rows, rows), :] = both[:, :pix]
        res_sc[pl.ds(8 + (v + 1) * rows, rows), :] = both[:, pix:]

    def body(j, carry):
        start = pl.multiple_of(j * slots, slots)
        row_at = [
            rows_smem.at[pl.ds(i, (owners - 1) * slots + 1)][start] for i in range(slots)
        ]
        pieces = []
        for g in range(slots // 4):
            pair = []
            for h in range(2):
                s = 4 * g + 2 * h
                first = res_sc[pl.ds(row_at[s] + 8, 8), :]
                second = res_sc[pl.ds(row_at[s + 1] + 4, 8), :]
                pair.append(jnp.where(half, first, second))
            pieces.append(jnp.concatenate(pair, axis=0).astype(BF16))
        taps = jnp.concatenate(pieces, axis=0)
        row = row_sc[pl.ds(j, 1), :]
        cod = code_sc[pl.ds(j, 1), :]
        wgt = wi_sc[pl.ds(j, 1), :]
        visit = jnp.floor(row * (1.0 / rows))
        y = coord(row - visit * rows, ccd, rows, ccd_devs)
        ty = cheb_rows(jnp.broadcast_to(y, (ORDER, wide)), ORDER)
        ty = ty * jnp.where(cod < float(P_DEV), wgt, 0.0)
        lhs = [jnp.where(cod == kid, wgt, 0.0)]
        for v in range(vis):
            lhs.append(jnp.where(visit == float(v), ty, 0.0))
        lhs = jnp.concatenate(lhs, axis=0).astype(BF16)
        sums = dot(lhs, taps)
        t_ref[pl.ds(pl.multiple_of(j * P_DEV, P_DEV), P_DEV), :] = sums[:P_DEV]
        q_ref[...] += sums[P_DEV:]
        live = live_ref[pl.ds(j, 1), :]
        member = jnp.where((pid_ref[pl.ds(j, 1), :] == kid_s) & (live > 0), 1.0, 0.0)
        h_sc[pl.ds(pl.multiple_of(j * P_DEV, P_DEV), P_DEV), :] = member.astype(BF16)
        return carry

    lax.fori_loop(0, owners, body, 0, unroll=UNROLL)
    c_hi, c_lo = split(cxt_ref[...], 2)
    t_hi, t_lo = split(t_ref[...], 2)
    proj = dot_t(jnp.concatenate([c_hi, c_lo], axis=0), t_hi)
    proj = proj[:ORDER] + proj[ORDER:] + dot_t(c_hi, t_lo)
    counts = dot_t(jnp.ones((8, slots), BF16), h_sc[...])
    blocks = owners * P_DEV // 128
    sub = iota((8, 128), 0)
    rows_out = [proj[:, 128 * q : 128 * (q + 1)] for q in range(blocks)]
    tail = jnp.zeros((8, 128), F32)
    for q in range(blocks):
        tail = jnp.where(sub == q, counts[0:1, 128 * q : 128 * (q + 1)], tail)
    block = jnp.concatenate(rows_out + [tail], axis=0).astype(BF16)
    for i in range(owners):
        pay_ref[i] = block


def design_kernel(
    ccd_devs, rows, srow_ref, pid_ref, live_ref, q_ref, const_ref,
    qb_ref, sy_ref, mw_ref, mtw_ref, keep_ref, m_sc,
):
    owners, slots = srow_ref.shape
    vis = q_ref.shape[0] // ORDER
    n = vis * ORDER
    ccd = lax.axis_index("ccd")
    kid = iota((P_DEV, slots), 0)
    m_sc[...] = jnp.zeros_like(m_sc)

    def body(j, acc):
        srow = srow_ref[pl.ds(j, 1), :]
        live = live_ref[pl.ds(j, 1), :]
        pid = pid_ref[pl.ds(j, 1), :]
        visit = srow // rows
        y = coord((srow - visit * rows).astype(F32), ccd, rows, ccd_devs)
        ty = cheb_rows(jnp.broadcast_to(y, (ORDER, slots)), ORDER)
        member = jnp.where((pid == kid) & (live > 0), 1.0, 0.0).astype(BF16)
        vt = jnp.concatenate(
            [jnp.where((visit == v) & (live > 0), ty, 0.0) for v in range(vis)], axis=0
        )
        parts = jnp.concatenate([p.astype(F32) for p in split(ty, 3)] + [jnp.zeros_like(ty)], axis=0)
        left = jnp.concatenate([member, parts.astype(BF16)], axis=0)
        both = None
        for piece in split(vt, 3):
            part = dot_t(left, piece)
            both = part if both is None else both + part
        m_sc[pl.ds(pl.multiple_of(j * P_DEV, P_DEV), P_DEV), 0:n] = both[:P_DEV]
        return acc + both[P_DEV:]

    sy = lax.fori_loop(0, owners, body, jnp.zeros((4 * ORDER, n), F32), unroll=4)
    sy = sy[:ORDER] + sy[ORDER : 2 * ORDER] + sy[2 * ORDER : 3 * ORDER]
    sy_ref[...] = widen(sy)
    m_hi, m_lo = split(m_sc[...], 2)
    mtw_ref[...] = jnp.concatenate(split(m_sc[...].T[:n], 2), axis=0)
    keep_ref[...] = const_ref[...]
    m_hi, m_lo = m_hi.astype(F32), m_lo.astype(F32)
    wide = m_hi + pltpu.roll(m_hi, n, 1) + pltpu.roll(m_lo, 2 * n, 1)
    mw_ref[...] = wide.astype(BF16)
    full = dot_t(q_ref[...], tile_rows(const_ref[CXT], vis), HI)
    qb_ref[...] = widen(blocks_of(full, vis))


def tile_rows(x, times):
    return jnp.concatenate([x] * times, axis=0)


def blocks_of(full, vis):
    lane = iota((ORDER, full.shape[1]), 1) // ORDER
    out = jnp.zeros((ORDER, full.shape[1]), F32)
    for v in range(vis):
        out = out + jnp.where(lane == v, full[v * ORDER : (v + 1) * ORDER], 0.0)
    return out


def widen(x):
    return jnp.concatenate([x, jnp.zeros((x.shape[0], 128 - x.shape[1]), F32)], axis=1)


def pack(x):
    turned = [x] + [pltpu.roll(x, 32 * g, 1) for g in range(1, 4)]
    out = []
    for r in range(ORDER // 4):
        row = turned[0][4 * r : 4 * r + 1]
        for g in range(1, 4):
            row = row + turned[g][4 * r + g : 4 * r + g + 1]
        out.append(row)
    return out


def unpack(x):
    out = []
    for row in x:
        row = jnp.broadcast_to(row, (ORDER, 128))
        out.append(row[0:1])
        for g in range(1, 4):
            out.append(pltpu.roll(row, 128 - 32 * g, 1)[0:1])
    return out


def stack(rows):
    sub = iota((8, 128), 0)
    out = jnp.broadcast_to(rows[0], (8, 128))
    for i in range(1, len(rows)):
        out = jnp.where(sub == i, rows[i], out)
    return out


def moments_block(mtw_ref, back, q):
    n = mtw_ref.shape[0] // 2
    vis = n // ORDER
    b_hi, b_lo = split(back, 2)
    b_hi, b_lo = (tile_rows(x.astype(F32), vis).astype(BF16) for x in (b_hi, b_lo))
    full = dot_t(mtw_ref[...], b_hi)
    full = full[:n] + full[n:] + dot_t(mtw_ref[0:n], b_lo)
    return q - widen(blocks_of(full, vis))


def senders_sum(ref, lo, hi):
    total = ref[0, lo:hi].astype(F32)
    for i in range(1, ref.shape[0]):
        total = total + ref[i, lo:hi].astype(F32)
    return total


def first_kernel(arr_ref, mtw_ref, qb_ref, sy_ref, b_ref, den_ref, pay_ref):
    blocks = b_ref.shape[1] // 128
    total = senders_sum(arr_ref, 0, arr_ref.shape[1])
    back, dens = [], []
    for q in range(blocks):
        den = total[ORDER * blocks + q : ORDER * blocks + q + 1] + 1.0
        dens.append(jnp.broadcast_to(den, (ORDER, 128)))
        back.append(total[ORDER * q : ORDER * (q + 1)] / dens[-1])
    back = jnp.concatenate(back, axis=1)
    den_ref[...] = jnp.concatenate(dens, axis=1)
    b_ref[...] = back
    mom = moments_block(mtw_ref, back, qb_ref[...])
    block = stack(pack(mom) + pack(sy_ref[...]))[: pay_ref.shape[1]]
    for i in range(pay_ref.shape[0]):
        pay_ref[i] = block


def systems(sy, lam, vis):
    n = vis * ORDER
    rows, lanes = iota((n, ORDER * 128), 0), iota((n, ORDER * 128), 1)
    pos = lanes % 128
    pick = (rows // ORDER == pos // ORDER) & (rows % ORDER == lanes // 128)
    spread = dot(sy[:, :n], jnp.where(pick, 1.0, 0.0), HI)
    sub = iota((ORDER, 128), 0)
    return [
        spread[:, 128 * b : 128 * (b + 1)] * lam + jnp.where(sub == b, RIDGE, 0.0)
        for b in range(ORDER)
    ]


def eliminate(mat, rhs):
    mat, rhs = list(mat), list(rhs)
    for p in range(ORDER):
        inv = 1.0 / mat[p][p : p + 1]
        mat[p] = mat[p] * inv
        rhs[p] = rhs[p] * inv
        for b in range(ORDER):
            if b != p:
                factor = mat[b][p : p + 1]
                mat[b] = mat[b] - factor * mat[p]
                rhs[b] = rhs[b] - factor * rhs[p]
    return rhs


def solve(mom, sy, lam, vis):
    out = stack(eliminate(systems(sy, lam, vis), mom))
    return jnp.where(iota((ORDER, 128), 1) < vis * ORDER, out, 0.0)


def block_diag_t(z, vis):
    n = vis * ORDER
    tiled = tile_rows(z, vis)
    keep = iota((n, 128), 0) // ORDER == iota((n, 128), 1) // ORDER
    return jnp.where(keep, tiled, 0.0).T[:n]


def model_kernel(arr_ref, const_ref, mtw_ref, mw_ref, t_ref, sy_ref, pay_ref):
    vis = mtw_ref.shape[0] // (2 * ORDER)
    n = vis * ORDER
    total = arr_ref[0]
    for i in range(1, arr_ref.shape[0]):
        total = total + arr_ref[i]
    rows = ORDER // 4
    sy = stack(unpack([total[i : i + 1] for i in range(rows, 2 * rows)]))
    sy_ref[...] = sy
    mom = unpack([total[i : i + 1] for i in range(rows)])
    z = solve(mom, sy, const_ref[LAM_LANE], vis)
    diag = block_diag_t(z, vis)
    weights = diag[:ORDER]
    for v in range(1, vis):
        weights = weights + diag[v * ORDER : (v + 1) * ORDER]
    w_hi, w_lo = split(weights, 2)
    model = (
        dot(w_hi, mtw_ref[0:n]) + dot(w_lo, mtw_ref[0:n]) + dot(w_hi, mtw_ref[n : 2 * n])
    )
    surface = lax.dot_general(
        weights, const_ref[CXT], (((0,), (0,)), ((), ())), precision=HI, preferred_element_type=F32
    )
    s_hi, s_lo = split(surface, 2)
    surface = jnp.concatenate([s_hi, s_lo, s_hi, jnp.zeros((128 - 3 * n, 128), BF16)], axis=0)
    corrected = t_ref[...] - dot(mw_ref[...], surface)
    blocks = model.shape[1] // 128
    block = jnp.concatenate(
        [model[:, 128 * q : 128 * (q + 1)] for q in range(blocks)], axis=0
    ).astype(BF16)
    rows = ORDER * blocks
    for i in range(pay_ref.shape[0]):
        pay_ref[i, 0:rows] = block
        pay_ref[i, rows : rows + P_DEV] = corrected[P_DEV * i : P_DEV * (i + 1)].astype(BF16)


def second_kernel(arr_ref, b_ref, den_ref, mtw_ref, qb_ref, const_ref, pay_ref):
    blocks = b_ref.shape[1] // 128
    total = senders_sum(arr_ref, 0, ORDER * blocks)
    model = jnp.concatenate(
        [total[ORDER * q : ORDER * (q + 1)] for q in range(blocks)], axis=1
    )
    lam = const_ref[LAM_SUB][:, 0:1]
    mom = moments_block(mtw_ref, b_ref[...] - lam * model / den_ref[...], qb_ref[...])
    block = stack(pack(mom))[: pay_ref.shape[1]]
    for i in range(pay_ref.shape[0]):
        pay_ref[i] = block


def background_kernel(vis, arr_ref, den_ref, sy_ref, const_ref, out_ref, inv_ref):
    rows = arr_ref.shape[1] - P_DEV
    sums = senders_sum(arr_ref, rows, rows + P_DEV)
    own = lax.axis_index("visit") * P_DEV
    width = den_ref.shape[1]
    pick = iota((P_DEV, width), 1) == iota((P_DEV, width), 0) + own
    den = dot_t(jnp.where(pick, 1.0, 0.0), den_ref[...], HI)
    out_ref[...] = sums / den[:, 0:1]
    sub = iota((ORDER, 128), 0)
    unit = [jnp.where(sub == b, 1.0, 0.0) for b in range(ORDER)]
    inverse = eliminate(systems(sy_ref[...], const_ref[LAM_LANE], vis), unit)
    for b in range(ORDER):
        inv_ref[b] = inverse[b]


def final_kernel(arr_ref, inv_ref, const_ref, out_ref):
    vis = out_ref.shape[0]
    n = vis * ORDER
    total = arr_ref[0]
    for i in range(1, arr_ref.shape[0]):
        total = total + arr_ref[i]
    mom = unpack([total[i : i + 1] for i in range(ORDER // 4)])
    z = inv_ref[0] * mom[0]
    for d in range(1, ORDER):
        z = z + inv_ref[d] * mom[d]
    flat = tile_rows(z, ORDER).T[:n] * tile_rows(const_ref[ROT][:, : ORDER * ORDER], vis)
    for v in range(vis):
        out_ref[v : v + 1] = jnp.sum(flat[v * ORDER : (v + 1) * ORDER], axis=0, keepdims=True)


def call(kernel, out_shape, scratch=(), n_in=1, hbm=(), plain=()):
    fn = pl.pallas_call(
        kernel,
        out_shape=out_shape,
        in_specs=[HBM if i in hbm else VMEM for i in range(n_in)],
        out_specs=jax.tree.map(lambda _: VMEM, out_shape),
        scratch_shapes=list(scratch),
    )

    def run(*args):
        return fn(
            *(
                x if i in plain or i in hbm else pltpu.with_memory_space_constraint(x, pltpu.VMEM)
                for i, x in enumerate(args)
            )
        )

    return run


def shape(dims, dtype=F32):
    return pltpu.VMEM(dims, dtype)


def result(dims, dtype=F32):
    return jax.ShapeDtypeStruct(dims, dtype)


def exchange(x, axis):
    return lax.all_to_all(x, axis, split_axis=0, concat_axis=0, tiled=True)


def per_device(raw_rows, resample, slot_row, tap_weight, patch_id, live_mask):
    owners = lax.axis_size("visit")
    ccd_devs = lax.axis_size("ccd")
    vis, rows, pix = raw_rows.shape
    slots = slot_row.shape[3]
    patches = owners * P_DEV
    blocks = patches // 128
    nvb = vis * ORDER
    lam, rot, cxt = constants(pix)
    const = np.zeros((32, 128))
    const[CXT] = cxt
    const[LAM_LANE, :nvb] = np.tile(lam, vis)
    const[LAM_SUB] = lam[:, None]
    const[ROT, : ORDER * ORDER] = np.repeat(rot.T, ORDER, axis=1)
    const = jnp.asarray(const, F32)
    srow, pid, live = slot_row[0, 0], patch_id[0, 0], live_mask[0, 0]
    weights = tap_weight[:, 0, 0]
    pay_rows = ORDER * blocks + P_DEV

    pay1, tsum, qsum = call(
        functools.partial(gather_kernel, ccd_devs),
        (
            shape((owners, ORDER * blocks + 8, 128), BF16),
            shape((patches, pix)),
            shape((nvb, pix)),
        ),
        scratch=(
            pltpu.VMEM((vis * rows + 16, pix), F32),
            pltpu.VMEM((owners, slots * TAPS), F32),
            pltpu.VMEM((owners, slots * TAPS), F32),
            pltpu.VMEM((owners, slots * TAPS), F32),
            pltpu.VMEM((patches, slots), BF16),
            pltpu.SMEM((owners * slots,), jnp.int32),
            pltpu.VMEM(raw_rows.shape, BF16),
            pltpu.VMEM(resample.shape, BF16),
            pltpu.VMEM((owners, slots), jnp.int32),
            pltpu.VMEM((TAPS, owners, slots), F32),
            pltpu.VMEM((owners, slots), jnp.int32),
            pltpu.VMEM((owners, slots), jnp.int32),
            pltpu.VMEM((ORDER, pix), F32),
            pltpu.SemaphoreType.DMA((7 + vis,)),
        ),
        n_in=8,
        hbm=range(8),
    )(srow.reshape(-1), raw_rows, resample, srow, weights, pid, live, const)
    arr1 = exchange(pay1, "visit")
    qb, sy, mw, mtw, const = call(
        functools.partial(design_kernel, ccd_devs, rows),
        (
            shape((ORDER, 128)),
            shape((ORDER, 128)),
            shape((patches, 128), BF16),
            shape((2 * nvb, patches), BF16),
            shape(const.shape),
        ),
        scratch=(pltpu.VMEM((patches, 128), F32),),
        n_in=5,
        plain=(0, 1, 2, 4),
    )(srow, pid, live, qsum, const)
    back, den, pay2 = call(
        first_kernel,
        (
            shape((ORDER, patches)),
            shape((ORDER, patches)),
            shape((ccd_devs, ORDER // 2, 128)),
        ),
        n_in=4,
    )(arr1, mtw, qb, sy)
    arr2 = exchange(pay2, "ccd")
    sy_all, pay3 = call(
        model_kernel,
        (shape((ORDER, 128)), shape((owners, pay_rows, 128), BF16)),
        n_in=5,
    )(arr2, const, mtw, mw, tsum)
    arr3 = exchange(pay3, "visit")
    pay4 = call(second_kernel, shape((ccd_devs, ORDER // 4, 128)), n_in=6)(
        arr3, back, den, mtw, qb, const
    )
    arr4 = exchange(pay4, "ccd")
    background, inverse = call(
        functools.partial(background_kernel, vis),
        (result((P_DEV, pix)), shape((ORDER, ORDER, 128))),
        n_in=4,
    )(arr3, den, sy_all, const)
    offsets = call(final_kernel, result((vis, ORDER * ORDER)), n_in=3)(arr4, inverse, const)
    return offsets, background


def solution(mesh):
    in_specs = (
        P("visit", "ccd", None),
        P("visit", None, None),
        P("visit", "ccd", None, None),
        P(None, "visit", "ccd", None, None),
        P("visit", "ccd", None, None),
        P("visit", "ccd", None, None),
    )
    out_specs = (P("visit", None), P(("visit", "ccd"), None))
    return jax.shard_map(
        per_device, mesh=mesh, in_specs=in_specs, out_specs=out_specs, check_vma=False
    )
```

```python
import functools

import jax
import jax.numpy as jnp
import numpy as np
from jax import lax
from jax.experimental import pallas as pl
from jax.experimental.pallas import tpu as pltpu
from jax.sharding import PartitionSpec as P

ORDER = 8
TAPS = 4
P_DEV = 16
RIDGE = 1.0
UNROLL = 8
CXT, LAM_LANE, LAM_SUB, ROT = (slice(8 * i, 8 * (i + 1)) for i in range(4))
HI = lax.Precision.HIGHEST
F32 = jnp.float32
BF16 = jnp.bfloat16
VMEM = pl.BlockSpec(memory_space=pltpu.VMEM)
HBM = pl.BlockSpec(memory_space=pl.ANY)
SMEM = pl.BlockSpec(memory_space=pltpu.SMEM)


def constants(pixels):
    x = (2 * np.arange(pixels) + 1) / pixels - 1.0
    cx = [np.ones_like(x), x]
    for _ in range(2, ORDER):
        cx.append(2 * x * cx[-1] - cx[-2])
    cx = np.stack(cx)
    lam, rot = np.linalg.eigh(cx @ cx.T)
    return lam, rot, rot.T @ cx


def dot(a, b, precision=None):
    return lax.dot_general(
        a, b, (((1,), (0,)), ((), ())), precision=precision, preferred_element_type=F32
    )


def dot_t(a, b, precision=None):
    return lax.dot_general(
        a, b, (((1,), (1,)), ((), ())), precision=precision, preferred_element_type=F32
    )


def split(x, parts):
    out = []
    for _ in range(parts):
        out.append(x.astype(BF16))
        x = x - out[-1].astype(F32)
    return out


def iota(shape, dim):
    return lax.broadcasted_iota(jnp.int32, shape, dim)


def cheb_rows(y, count):
    sub = iota(y.shape, 0)
    prev, cur = jnp.ones_like(y), y
    out = jnp.where(sub == 0, prev, cur)
    for k in range(2, count):
        prev, cur = cur, 2.0 * y * cur - prev
        out = jnp.where(sub == k, cur, out)
    return out


def coord(b_pos, ccd, rows_local, ccd_devs):
    base = (ccd * rows_local).astype(F32)
    return (2.0 * (base + b_pos) + float(TAPS)) / float(rows_local * ccd_devs) - 1.0


def project_kernel(
    srow_hbm, raw_hbm, res_hbm, w_hbm, pid_hbm, live_hbm, const_hbm,
    pay_ref, srow_ref, raw_ref, res_ref, w_ref, pid_ref, live_ref, const_ref,
    hi_sc, lo_sc, code_sc, acc_sc, sems,
):
    vis, rows, pix = raw_ref.shape
    owners, slots = srow_ref.shape
    blocks = owners * P_DEV // 128
    group = owners // blocks
    small = (
        (srow_hbm, srow_ref), (w_hbm, w_ref), (pid_hbm, pid_ref), (live_hbm, live_ref),
        (const_hbm, const_ref), (res_hbm, res_ref),
    )
    copies = [pltpu.make_async_copy(a, b, sems.at[n]) for n, (a, b) in enumerate(small)]
    raw_copy = pltpu.make_async_copy(raw_hbm, raw_ref, sems.at[len(small)])
    for copy in copies + [raw_copy]:
        copy.start()
    for copy in copies:
        copy.wait()
    span = 128 - TAPS + 1
    srow = srow_ref[...].astype(F32)
    high = jnp.floor((srow + 0.5) * (1.0 / span))
    hi_sc[...] = high
    lo_sc[...] = srow - span * high
    place = P_DEV * (iota((owners, slots), 0) % group) + pid_ref[...]
    code_sc[...] = jnp.where(live_ref[...] > 0, place, -1).astype(F32)
    c_parts = jnp.concatenate(split(const_ref[CXT], 2), axis=0)
    kernels = []
    for v in range(vis):
        both = dot_t(c_parts, res_ref[v])
        kernels.append(jnp.concatenate(split(both[:ORDER] + both[ORDER:], 2), axis=0))
    raw_copy.wait()
    pieces = []
    for v in range(vis):
        both = dot_t(kernels[v], raw_ref[v])
        pieces.append(both[:ORDER] + both[ORDER:])
    table = jnp.concatenate(pieces, axis=1)
    tiles = vis * rows // 128
    lane = iota((ORDER, 128), 1)
    windows = []
    for k in range(-(-(vis * rows - TAPS + 1) // span)):
        start = span * k
        first, shift = start // 128, start % 128
        a = table[:, 128 * first : 128 * (first + 1)]
        if shift:
            nxt = min(first + 1, tiles - 1)
            b = table[:, 128 * nxt : 128 * (nxt + 1)]
            a = jnp.where(
                lane < 128 - shift, pltpu.roll(a, 128 - shift, 1), pltpu.roll(b, 128 - shift, 1)
            )
        windows.append(a)
    if len(windows) % 2:
        windows.append(jnp.zeros((ORDER, 128), F32))
    left = jnp.concatenate(windows, axis=0).astype(BF16)
    ids = iota((128, slots), 0).astype(F32).astype(BF16)
    ones = jnp.ones((ORDER, slots), BF16)
    unit = jnp.ones((128, slots), BF16)

    def pair_sums(m):
        taps, his = [], []
        for h in range(2):
            j = 2 * m + h
            low = lo_sc[pl.ds(j, 1), :]
            one = jnp.zeros((128, slots), BF16)
            for t in range(TAPS):
                hit = ids == (low + float(t)).astype(BF16)
                one = jnp.where(hit, w_ref[t, pl.ds(j, 1), :].astype(BF16), one)
            taps.append(one)
            his.append(jnp.broadcast_to(hi_sc[pl.ds(j, 1), :], (ORDER, slots)))
        vals = dot(left, jnp.concatenate(taps, axis=1))
        left_sums, members = [], []
        for h in range(2):
            got = jnp.zeros((ORDER, slots), F32)
            for k in range(len(windows)):
                part = vals[ORDER * k : ORDER * (k + 1), slots * h : slots * (h + 1)]
                got = jnp.where(his[h] == float(k), part, got)
            left_sums.append(jnp.concatenate(split(got, 2) + [ones, ones], axis=0))
            code = code_sc[pl.ds(2 * m + h, 1), :].astype(BF16)
            members.append(jnp.where(ids == code, unit, jnp.zeros_like(unit)))
        return dot_t(jnp.concatenate(left_sums, axis=1), jnp.concatenate(members, axis=1))

    def body(q, carry):
        pairs = group // 2
        total = pair_sums(q * pairs)
        for m in range(1, pairs):
            total = total + pair_sums(q * pairs + m)
        acc_sc[q] = total
        return carry

    lax.fori_loop(0, blocks, body, 0)
    sub = iota((8, 128), 0)
    tail = jnp.zeros((8, 128), F32)
    rows_out = []
    for q in range(blocks):
        rows_out.append(acc_sc[q, 0:ORDER] + acc_sc[q, ORDER : 2 * ORDER])
        tail = jnp.where(sub == q, acc_sc[q, 2 * ORDER : 3 * ORDER], tail)
    block = jnp.concatenate(rows_out + [tail], axis=0).astype(BF16)
    for i in range(owners):
        pay_ref[i] = block


def gather_kernel(
    ccd_devs, rows_smem, raw_ref, res_ref, srow_ref, w_ref, pid_ref, live_ref, const_ref,
    t_ref, qb_ref, sy_ref, mw_ref, mtw_ref,
    res_sc, row_sc, code_sc, wi_sc, q_sc, m_sc,
):
    vis, rows, pix = raw_ref.shape
    owners, slots = srow_ref.shape
    wide = slots * TAPS
    n = vis * ORDER
    ccd = lax.axis_index("ccd")
    off = iota((slots, wide), 1) - TAPS * iota((slots, wide), 0)
    rep = jnp.where((off >= 0) & (off < TAPS), 1.0, 0.0).astype(BF16)
    srow = srow_ref[...]
    code = pid_ref[...] + P_DEV * (1 - live_ref[...])
    high, low = srow >> 8, srow & 255
    whole = jnp.concatenate([high, low, code], axis=0).astype(F32).astype(BF16)
    whole = dot(whole, rep)
    row_sc[...] = 256.0 * whole[:owners] + whole[owners : 2 * owners]
    code_sc[...] = whole[2 * owners :]
    wi = None
    for t in range(TAPS):
        pick = jnp.where(off == t, 1.0, 0.0).astype(BF16)
        part = dot(w_ref[t].astype(BF16), pick)
        wi = part if wi is None else wi + part
    wi_sc[...] = wi
    q_sc[...] = jnp.zeros_like(q_sc)
    m_sc[...] = jnp.zeros_like(m_sc)
    half = iota((8, pix), 0) < TAPS
    kid = iota((P_DEV, wide), 0).astype(F32)
    kid_s = iota((P_DEV, slots), 0)
    zero = jnp.zeros((pix, pix), BF16)
    for v in range(0, vis, 2):
        pair = jnp.concatenate([raw_ref[v], raw_ref[v + 1]], axis=1)
        diag = jnp.concatenate(
            [
                jnp.concatenate([res_ref[v], zero], axis=1),
                jnp.concatenate([zero, res_ref[v + 1]], axis=1),
            ],
            axis=0,
        )
        both = dot(pair, diag)
        res_sc[pl.ds(8 + v * rows, rows), :] = both[:, :pix]
        res_sc[pl.ds(8 + (v + 1) * rows, rows), :] = both[:, pix:]

    def design(j):
        srow = srow_ref[pl.ds(j, 1), :]
        live = live_ref[pl.ds(j, 1), :]
        pid = pid_ref[pl.ds(j, 1), :]
        visit = srow // rows
        y = coord((srow - visit * rows).astype(F32), ccd, rows, ccd_devs)
        ty = cheb_rows(jnp.broadcast_to(y, (ORDER, slots)), ORDER)
        member = jnp.where((pid == kid_s) & (live > 0), 1.0, 0.0).astype(BF16)
        vt = jnp.concatenate(
            [jnp.where((visit == v) & (live > 0), ty, 0.0) for v in range(vis)], axis=0
        )
        parts = jnp.concatenate([p.astype(F32) for p in split(ty, 3)] + [jnp.zeros_like(ty)], axis=0)
        left = jnp.concatenate([member, parts.astype(BF16)], axis=0)
        both = None
        for piece in split(vt, 3):
            part = dot_t(left, piece)
            both = part if both is None else both + part
        m_sc[pl.ds(pl.multiple_of(j * P_DEV, P_DEV), P_DEV), 0:n] = both[:P_DEV]
        return both[P_DEV:]

    def body(j, acc):
        start = pl.multiple_of(j * slots, slots)
        row_at = [
            rows_smem.at[pl.ds(i, (owners - 1) * slots + 1)][start] for i in range(slots)
        ]
        pieces = []
        for g in range(slots // 4):
            pair = []
            for h in range(2):
                s = 4 * g + 2 * h
                first = res_sc[pl.ds(row_at[s] + 8, 8), :]
                second = res_sc[pl.ds(row_at[s + 1] + 4, 8), :]
                pair.append(jnp.where(half, first, second))
            pieces.append(jnp.concatenate(pair, axis=0).astype(BF16))
        taps = jnp.concatenate(pieces, axis=0)
        row = row_sc[pl.ds(j, 1), :]
        cod = code_sc[pl.ds(j, 1), :]
        wgt = wi_sc[pl.ds(j, 1), :]
        visit = jnp.floor(row * (1.0 / rows))
        y = coord(row - visit * rows, ccd, rows, ccd_devs)
        ty = cheb_rows(jnp.broadcast_to(y, (ORDER, wide)), ORDER)
        ty = ty * jnp.where(cod < float(P_DEV), wgt, 0.0)
        lhs = [jnp.where(cod == kid, wgt, 0.0)]
        for v in range(vis):
            lhs.append(jnp.where(visit == float(v), ty, 0.0))
        lhs = jnp.concatenate(lhs, axis=0).astype(BF16)
        sums = dot(lhs, taps)
        t_ref[pl.ds(pl.multiple_of(j * P_DEV, P_DEV), P_DEV), :] = sums[:P_DEV]
        q_sc[...] += sums[P_DEV:]
        return acc + design(j)

    sy = lax.fori_loop(0, owners, body, jnp.zeros((4 * ORDER, n), F32), unroll=UNROLL)
    sy = sy[:ORDER] + sy[ORDER : 2 * ORDER] + sy[2 * ORDER : 3 * ORDER]
    sy_ref[...] = widen(sy)
    m_hi, m_lo = split(m_sc[...], 2)
    mtw_ref[...] = jnp.concatenate(split(m_sc[...].T[:n], 2), axis=0)
    m_hi, m_lo = m_hi.astype(F32), m_lo.astype(F32)
    wide_m = m_hi + pltpu.roll(m_hi, n, 1) + pltpu.roll(m_lo, 2 * n, 1)
    mw_ref[...] = wide_m.astype(BF16)
    full = dot_t(q_sc[...], tile_rows(const_ref[CXT], vis), HI)
    qb_ref[...] = widen(blocks_of(full, vis))


def tile_rows(x, times):
    return jnp.concatenate([x] * times, axis=0)


def blocks_of(full, vis):
    lane = iota((ORDER, full.shape[1]), 1) // ORDER
    out = jnp.zeros((ORDER, full.shape[1]), F32)
    for v in range(vis):
        out = out + jnp.where(lane == v, full[v * ORDER : (v + 1) * ORDER], 0.0)
    return out


def widen(x):
    return jnp.concatenate([x, jnp.zeros((x.shape[0], 128 - x.shape[1]), F32)], axis=1)


def pack(x):
    turned = [x] + [pltpu.roll(x, 32 * g, 1) for g in range(1, 4)]
    out = []
    for r in range(ORDER // 4):
        row = turned[0][4 * r : 4 * r + 1]
        for g in range(1, 4):
            row = row + turned[g][4 * r + g : 4 * r + g + 1]
        out.append(row)
    return out


def unpack(x):
    out = []
    for row in x:
        row = jnp.broadcast_to(row, (ORDER, 128))
        out.append(row[0:1])
        for g in range(1, 4):
            out.append(pltpu.roll(row, 128 - 32 * g, 1)[0:1])
    return out


def stack(rows):
    sub = iota((8, 128), 0)
    out = jnp.broadcast_to(rows[0], (8, 128))
    for i in range(1, len(rows)):
        out = jnp.where(sub == i, rows[i], out)
    return out


def moments_block(mtw_ref, back, q):
    n = mtw_ref.shape[0] // 2
    vis = n // ORDER
    b_hi, b_lo = split(back, 2)
    b_hi, b_lo = (tile_rows(x.astype(F32), vis).astype(BF16) for x in (b_hi, b_lo))
    full = dot_t(mtw_ref[...], b_hi)
    full = full[:n] + full[n:] + dot_t(mtw_ref[0:n], b_lo)
    return q - widen(blocks_of(full, vis))


def senders_sum(ref, lo, hi):
    total = ref[0, lo:hi].astype(F32)
    for i in range(1, ref.shape[0]):
        total = total + ref[i, lo:hi].astype(F32)
    return total


def first_kernel(arr_ref, mtw_ref, qb_ref, sy_ref, b_ref, den_ref, pay_ref):
    blocks = b_ref.shape[1] // 128
    total = senders_sum(arr_ref, 0, arr_ref.shape[1])
    back, dens = [], []
    for q in range(blocks):
        den = total[ORDER * blocks + q : ORDER * blocks + q + 1] + 1.0
        dens.append(jnp.broadcast_to(den, (ORDER, 128)))
        back.append(total[ORDER * q : ORDER * (q + 1)] / dens[-1])
    back = jnp.concatenate(back, axis=1)
    den_ref[...] = jnp.concatenate(dens, axis=1)
    b_ref[...] = back
    mom = moments_block(mtw_ref, back, qb_ref[...])
    block = stack(pack(mom) + pack(sy_ref[...]))[: pay_ref.shape[1]]
    for i in range(pay_ref.shape[0]):
        pay_ref[i] = block


def systems(sy, lam, vis):
    n = vis * ORDER
    rows, lanes = iota((n, ORDER * 128), 0), iota((n, ORDER * 128), 1)
    pos = lanes % 128
    pick = (rows // ORDER == pos // ORDER) & (rows % ORDER == lanes // 128)
    spread = dot(sy[:, :n], jnp.where(pick, 1.0, 0.0), HI)
    sub = iota((ORDER, 128), 0)
    return [
        spread[:, 128 * b : 128 * (b + 1)] * lam + jnp.where(sub == b, RIDGE, 0.0)
        for b in range(ORDER)
    ]


def eliminate(mat, rhs):
    mat, rhs = list(mat), list(rhs)
    for p in range(ORDER):
        inv = 1.0 / mat[p][p : p + 1]
        mat[p] = mat[p] * inv
        rhs[p] = rhs[p] * inv
        for b in range(ORDER):
            if b != p:
                factor = mat[b][p : p + 1]
                mat[b] = mat[b] - factor * mat[p]
                rhs[b] = rhs[b] - factor * rhs[p]
    return rhs


def solve(mom, sy, lam, vis):
    out = stack(eliminate(systems(sy, lam, vis), mom))
    return jnp.where(iota((ORDER, 128), 1) < vis * ORDER, out, 0.0)


def block_diag_t(z, vis):
    n = vis * ORDER
    tiled = tile_rows(z, vis)
    keep = iota((n, 128), 0) // ORDER == iota((n, 128), 1) // ORDER
    return jnp.where(keep, tiled, 0.0).T[:n]


def model_kernel(arr_ref, const_ref, mtw_ref, mw_ref, t_ref, sy_ref, pay_ref):
    vis = mtw_ref.shape[0] // (2 * ORDER)
    n = vis * ORDER
    total = arr_ref[0]
    for i in range(1, arr_ref.shape[0]):
        total = total + arr_ref[i]
    rows = ORDER // 4
    sy = stack(unpack([total[i : i + 1] for i in range(rows, 2 * rows)]))
    sy_ref[...] = sy
    mom = unpack([total[i : i + 1] for i in range(rows)])
    z = solve(mom, sy, const_ref[LAM_LANE], vis)
    diag = block_diag_t(z, vis)
    weights = diag[:ORDER]
    for v in range(1, vis):
        weights = weights + diag[v * ORDER : (v + 1) * ORDER]
    w_hi, w_lo = split(weights, 2)
    model = (
        dot(w_hi, mtw_ref[0:n]) + dot(w_lo, mtw_ref[0:n]) + dot(w_hi, mtw_ref[n : 2 * n])
    )
    surface = lax.dot_general(
        weights, const_ref[CXT], (((0,), (0,)), ((), ())), precision=HI, preferred_element_type=F32
    )
    s_hi, s_lo = split(surface, 2)
    surface = jnp.concatenate([s_hi, s_lo, s_hi, jnp.zeros((128 - 3 * n, 128), BF16)], axis=0)
    corrected = t_ref[...] - dot(mw_ref[...], surface)
    blocks = model.shape[1] // 128
    block = jnp.concatenate(
        [model[:, 128 * q : 128 * (q + 1)] for q in range(blocks)], axis=0
    ).astype(BF16)
    rows = ORDER * blocks
    for i in range(pay_ref.shape[0]):
        pay_ref[i, 0:rows] = block
        pay_ref[i, rows : rows + P_DEV] = corrected[P_DEV * i : P_DEV * (i + 1)].astype(BF16)


def second_kernel(arr_ref, b_ref, den_ref, mtw_ref, qb_ref, const_ref, pay_ref):
    blocks = b_ref.shape[1] // 128
    total = senders_sum(arr_ref, 0, ORDER * blocks)
    model = jnp.concatenate(
        [total[ORDER * q : ORDER * (q + 1)] for q in range(blocks)], axis=1
    )
    lam = const_ref[LAM_SUB][:, 0:1]
    mom = moments_block(mtw_ref, b_ref[...] - lam * model / den_ref[...], qb_ref[...])
    block = stack(pack(mom))[: pay_ref.shape[1]]
    for i in range(pay_ref.shape[0]):
        pay_ref[i] = block


def background_kernel(vis, arr_ref, den_ref, sy_ref, const_ref, out_ref, inv_ref):
    rows = arr_ref.shape[1] - P_DEV
    sums = senders_sum(arr_ref, rows, rows + P_DEV)
    own = lax.axis_index("visit") * P_DEV
    width = den_ref.shape[1]
    pick = iota((P_DEV, width), 1) == iota((P_DEV, width), 0) + own
    den = dot_t(jnp.where(pick, 1.0, 0.0), den_ref[...], HI)
    out_ref[...] = sums / den[:, 0:1]
    sub = iota((ORDER, 128), 0)
    unit = [jnp.where(sub == b, 1.0, 0.0) for b in range(ORDER)]
    inverse = eliminate(systems(sy_ref[...], const_ref[LAM_LANE], vis), unit)
    for b in range(ORDER):
        inv_ref[b] = inverse[b]


def final_kernel(arr_ref, inv_ref, const_ref, out_ref):
    vis = out_ref.shape[0]
    n = vis * ORDER
    total = arr_ref[0]
    for i in range(1, arr_ref.shape[0]):
        total = total + arr_ref[i]
    mom = unpack([total[i : i + 1] for i in range(ORDER // 4)])
    z = inv_ref[0] * mom[0]
    for d in range(1, ORDER):
        z = z + inv_ref[d] * mom[d]
    flat = tile_rows(z, ORDER).T[:n] * tile_rows(const_ref[ROT][:, : ORDER * ORDER], vis)
    for v in range(vis):
        out_ref[v : v + 1] = jnp.sum(flat[v * ORDER : (v + 1) * ORDER], axis=0, keepdims=True)


def call(kernel, out_shape, scratch=(), n_in=1, hbm=(), smem=()):
    spec = {i: HBM for i in hbm} | {i: SMEM for i in smem}
    fn = pl.pallas_call(
        kernel,
        out_shape=out_shape,
        in_specs=[spec.get(i, VMEM) for i in range(n_in)],
        out_specs=jax.tree.map(lambda _: VMEM, out_shape),
        scratch_shapes=list(scratch),
    )

    def run(*args):
        return fn(
            *(
                x if i in spec else pltpu.with_memory_space_constraint(x, pltpu.VMEM)
                for i, x in enumerate(args)
            )
        )

    return run


def shape(dims, dtype=F32):
    return pltpu.VMEM(dims, dtype)


def result(dims, dtype=F32):
    return jax.ShapeDtypeStruct(dims, dtype)


def exchange(x, axis):
    return lax.all_to_all(x, axis, split_axis=0, concat_axis=0, tiled=True)


def per_device(raw_rows, resample, slot_row, tap_weight, patch_id, live_mask):
    owners = lax.axis_size("visit")
    ccd_devs = lax.axis_size("ccd")
    vis, rows, pix = raw_rows.shape
    slots = slot_row.shape[3]
    patches = owners * P_DEV
    blocks = patches // 128
    nvb = vis * ORDER
    lam, rot, cxt = constants(pix)
    const = np.zeros((32, 128))
    const[CXT] = cxt
    const[LAM_LANE, :nvb] = np.tile(lam, vis)
    const[LAM_SUB] = lam[:, None]
    const[ROT, : ORDER * ORDER] = np.repeat(rot.T, ORDER, axis=1)
    const = jnp.asarray(const, F32)
    srow, pid, live = slot_row[0, 0], patch_id[0, 0], live_mask[0, 0]
    weights = tap_weight[:, 0, 0]
    pay_rows = ORDER * blocks + P_DEV

    ints = shape((owners, slots), jnp.int32)
    pay1, srow_v, raw_v, res_v, w_v, pid_v, live_v, const = call(
        project_kernel,
        (
            shape((owners, ORDER * blocks + 8, 128), BF16),
            ints,
            shape(raw_rows.shape, BF16),
            shape(resample.shape, BF16),
            shape((TAPS, owners, slots)),
            ints,
            ints,
            shape(const.shape),
        ),
        scratch=(
            pltpu.VMEM((owners, slots), F32),
            pltpu.VMEM((owners, slots), F32),
            pltpu.VMEM((owners, slots), F32),
            pltpu.VMEM((blocks, 4 * ORDER, 128), F32),
            pltpu.SemaphoreType.DMA((7,)),
        ),
        n_in=7,
        hbm=range(7),
    )(srow, raw_rows, resample, weights, pid, live, const)
    arr1 = exchange(pay1, "visit")
    tsum, qb, sy, mw, mtw = call(
        functools.partial(gather_kernel, ccd_devs),
        (
            shape((patches, pix)),
            shape((ORDER, 128)),
            shape((ORDER, 128)),
            shape((patches, 128), BF16),
            shape((2 * nvb, patches), BF16),
        ),
        scratch=(
            pltpu.VMEM((vis * rows + 16, pix), F32),
            pltpu.VMEM((owners, slots * TAPS), F32),
            pltpu.VMEM((owners, slots * TAPS), F32),
            pltpu.VMEM((owners, slots * TAPS), F32),
            pltpu.VMEM((nvb, pix), F32),
            pltpu.VMEM((patches, 128), F32),
        ),
        n_in=8,
        smem=(0,),
    )(srow.reshape(-1), raw_v, res_v, srow_v, w_v, pid_v, live_v, const)
    back, den, pay2 = call(
        first_kernel,
        (
            shape((ORDER, patches)),
            shape((ORDER, patches)),
            shape((ccd_devs, ORDER // 2, 128)),
        ),
        n_in=4,
    )(arr1, mtw, qb, sy)
    arr2 = exchange(pay2, "ccd")
    sy_all, pay3 = call(
        model_kernel,
        (shape((ORDER, 128)), shape((owners, pay_rows, 128), BF16)),
        n_in=5,
    )(arr2, const, mtw, mw, tsum)
    arr3 = exchange(pay3, "visit")
    pay4 = call(second_kernel, shape((ccd_devs, ORDER // 4, 128)), n_in=6)(
        arr3, back, den, mtw, qb, const
    )
    arr4 = exchange(pay4, "ccd")
    background, inverse = call(
        functools.partial(background_kernel, vis),
        (result((P_DEV, pix)), shape((ORDER, ORDER, 128))),
        n_in=4,
    )(arr3, den, sy_all, const)
    offsets = call(final_kernel, result((vis, ORDER * ORDER)), n_in=3)(arr4, inverse, const)
    return offsets, background


def solution(mesh):
    in_specs = (
        P("visit", "ccd", None),
        P("visit", None, None),
        P("visit", "ccd", None, None),
        P(None, "visit", "ccd", None, None),
        P("visit", "ccd", None, None),
        P("visit", "ccd", None, None),
    )
    out_specs = (P("visit", None), P(("visit", "ccd"), None))
    return jax.shard_map(
        per_device, mesh=mesh, in_specs=in_specs, out_specs=out_specs, check_vma=False
    )
```

```python
import functools

import jax
import jax.numpy as jnp
import numpy as np
from jax import lax
from jax.experimental import pallas as pl
from jax.experimental.pallas import tpu as pltpu
from jax.sharding import PartitionSpec as P

ORDER = 8
TAPS = 4
P_DEV = 16
RIDGE = 1.0
UNROLL = 8
CXT, LAM_LANE, LAM_SUB, ROT = (slice(8 * i, 8 * (i + 1)) for i in range(4))
HI = lax.Precision.HIGHEST
F32 = jnp.float32
BF16 = jnp.bfloat16
VMEM = pl.BlockSpec(memory_space=pltpu.VMEM)
HBM = pl.BlockSpec(memory_space=pl.ANY)
SMEM = pl.BlockSpec(memory_space=pltpu.SMEM)


def constants(pixels):
    x = (2 * np.arange(pixels) + 1) / pixels - 1.0
    cx = [np.ones_like(x), x]
    for _ in range(2, ORDER):
        cx.append(2 * x * cx[-1] - cx[-2])
    cx = np.stack(cx)
    lam, rot = np.linalg.eigh(cx @ cx.T)
    return lam, rot, rot.T @ cx


def dot(a, b, precision=None):
    return lax.dot_general(
        a, b, (((1,), (0,)), ((), ())), precision=precision, preferred_element_type=F32
    )


def dot_t(a, b, precision=None):
    return lax.dot_general(
        a, b, (((1,), (1,)), ((), ())), precision=precision, preferred_element_type=F32
    )


def split(x, parts):
    out = []
    for _ in range(parts):
        out.append(x.astype(BF16))
        x = x - out[-1].astype(F32)
    return out


def iota(shape, dim):
    return lax.broadcasted_iota(jnp.int32, shape, dim)


def cheb_rows(y, count):
    sub = iota(y.shape, 0)
    prev, cur = jnp.ones_like(y), y
    out = jnp.where(sub == 0, prev, cur)
    for k in range(2, count):
        prev, cur = cur, 2.0 * y * cur - prev
        out = jnp.where(sub == k, cur, out)
    return out


def coord(b_pos, ccd, rows_local, ccd_devs):
    base = (ccd * rows_local).astype(F32)
    return (2.0 * (base + b_pos) + float(TAPS)) / float(rows_local * ccd_devs) - 1.0


def project_kernel(
    srow_hbm, raw_hbm, res_hbm, w_hbm, pid_hbm, live_hbm, const_hbm,
    pay_ref, srow_ref, raw_ref, res_ref, w_ref, pid_ref, live_ref, const_ref,
    hi_sc, lo_sc, code_sc, acc_sc, sems,
):
    vis, rows, pix = raw_ref.shape
    owners, slots = srow_ref.shape
    blocks = owners * P_DEV // 128
    group = owners // blocks
    small = (
        (srow_hbm, srow_ref), (w_hbm, w_ref), (pid_hbm, pid_ref), (live_hbm, live_ref),
        (const_hbm, const_ref), (res_hbm, res_ref),
    )
    copies = [pltpu.make_async_copy(a, b, sems.at[n]) for n, (a, b) in enumerate(small)]
    raw_copy = pltpu.make_async_copy(raw_hbm, raw_ref, sems.at[len(small)])
    for copy in copies + [raw_copy]:
        copy.start()
    for copy in copies:
        copy.wait()
    wide = 256
    span = wide - TAPS + 1
    srow = srow_ref[...].astype(F32)
    high = jnp.floor((srow + 0.5) * (1.0 / span))
    hi_sc[...] = high
    lo_sc[...] = srow - span * high
    place = P_DEV * (iota((owners, slots), 0) % group) + pid_ref[...]
    code_sc[...] = jnp.where(live_ref[...] > 0, place, -1).astype(F32)
    c_parts = jnp.concatenate(split(const_ref[CXT], 2), axis=0)
    kernels = []
    for v in range(vis):
        both = dot_t(c_parts, res_ref[v])
        kernels.append(jnp.concatenate(split(both[:ORDER] + both[ORDER:], 2), axis=0))
    raw_copy.wait()
    pieces = []
    for v in range(vis):
        both = dot_t(kernels[v], raw_ref[v])
        pieces.append(both[:ORDER] + both[ORDER:])
    table = jnp.concatenate(pieces, axis=1)
    tiles = vis * rows // 128
    lane = iota((ORDER, 128), 1)

    def window(start):
        first, shift = start // 128, start % 128
        a, b = (
            table[:, 128 * t : 128 * (t + 1)]
            for t in (min(first, tiles - 1), min(first + 1, tiles - 1))
        )
        if not shift:
            return a
        a, b = pltpu.roll(a, 128 - shift, 1), pltpu.roll(b, 128 - shift, 1)
        return jnp.where(lane < 128 - shift, a, b)

    windows = []
    for k in range(-(-(vis * rows - TAPS + 1) // span)):
        parts = [window(span * k + c) for c in range(0, wide, 128)]
        windows.append(jnp.concatenate(parts, axis=1))
    if len(windows) % 2:
        windows.append(jnp.zeros((ORDER, wide), F32))
    left = jnp.concatenate(windows, axis=0).astype(BF16)
    rid = iota((wide, slots), 0).astype(F32).astype(BF16)
    ids = rid[:128]
    ones = jnp.ones((ORDER, slots), BF16)
    unit = jnp.ones((128, slots), BF16)

    def pair_sums(m):
        taps, his = [], []
        for h in range(2):
            j = 2 * m + h
            low = lo_sc[pl.ds(j, 1), :]
            one = jnp.zeros((wide, slots), BF16)
            for t in range(TAPS):
                hit = rid == (low + float(t)).astype(BF16)
                one = jnp.where(hit, w_ref[t, pl.ds(j, 1), :].astype(BF16), one)
            taps.append(one)
            his.append(jnp.broadcast_to(hi_sc[pl.ds(j, 1), :], (ORDER, slots)))
        vals = dot(left, jnp.concatenate(taps, axis=1))
        left_sums, members = [], []
        for h in range(2):
            got = jnp.zeros((ORDER, slots), F32)
            for k in range(len(windows)):
                part = vals[ORDER * k : ORDER * (k + 1), slots * h : slots * (h + 1)]
                got = jnp.where(his[h] == float(k), part, got)
            left_sums.append(jnp.concatenate(split(got, 2) + [ones, ones], axis=0))
            code = code_sc[pl.ds(2 * m + h, 1), :].astype(BF16)
            members.append(jnp.where(ids == code, unit, jnp.zeros_like(unit)))
        return dot_t(jnp.concatenate(left_sums, axis=1), jnp.concatenate(members, axis=1))

    def body(q, carry):
        pairs = group // 2
        total = pair_sums(q * pairs)
        for m in range(1, pairs):
            total = total + pair_sums(q * pairs + m)
        acc_sc[q] = total
        return carry

    lax.fori_loop(0, blocks, body, 0, unroll=2)
    sub = iota((8, 128), 0)
    tail = jnp.zeros((8, 128), F32)
    rows_out = []
    for q in range(blocks):
        rows_out.append(acc_sc[q, 0:ORDER] + acc_sc[q, ORDER : 2 * ORDER])
        tail = jnp.where(sub == q, acc_sc[q, 2 * ORDER : 3 * ORDER], tail)
    block = jnp.concatenate(rows_out + [tail], axis=0).astype(BF16)
    for i in range(owners):
        pay_ref[i] = block


def gather_kernel(
    ccd_devs, rows_smem, raw_ref, res_ref, srow_ref, w_ref, pid_ref, live_ref, const_ref,
    t_ref, qb_ref, sy_ref, mw_ref, mtw_ref,
    res_sc, row_sc, code_sc, wi_sc, q_sc, m_sc,
):
    vis, rows, pix = raw_ref.shape
    owners, slots = srow_ref.shape
    wide = slots * TAPS
    n = vis * ORDER
    ccd = lax.axis_index("ccd")
    off = iota((slots, wide), 1) - TAPS * iota((slots, wide), 0)
    rep = jnp.where((off >= 0) & (off < TAPS), 1.0, 0.0).astype(BF16)
    srow = srow_ref[...]
    code = pid_ref[...] + P_DEV * (1 - live_ref[...])
    high, low = srow >> 8, srow & 255
    whole = jnp.concatenate([high, low, code], axis=0).astype(F32).astype(BF16)
    whole = dot(whole, rep)
    row_sc[...] = 256.0 * whole[:owners] + whole[owners : 2 * owners]
    code_sc[...] = whole[2 * owners :]
    wi = None
    for t in range(TAPS):
        pick = jnp.where(off == t, 1.0, 0.0).astype(BF16)
        part = dot(w_ref[t].astype(BF16), pick)
        wi = part if wi is None else wi + part
    wi_sc[...] = wi
    q_sc[...] = jnp.zeros_like(q_sc)
    m_sc[...] = jnp.zeros_like(m_sc)
    half = iota((8, pix), 0) < TAPS
    kid = iota((P_DEV, wide), 0).astype(F32)
    kid_s = iota((P_DEV, slots), 0)
    zero = jnp.zeros((pix, pix), BF16)
    for v in range(0, vis, 2):
        pair = jnp.concatenate([raw_ref[v], raw_ref[v + 1]], axis=1)
        diag = jnp.concatenate(
            [
                jnp.concatenate([res_ref[v], zero], axis=1),
                jnp.concatenate([zero, res_ref[v + 1]], axis=1),
            ],
            axis=0,
        )
        both = dot(pair, diag)
        res_sc[pl.ds(8 + v * rows, rows), :] = both[:, :pix]
        res_sc[pl.ds(8 + (v + 1) * rows, rows), :] = both[:, pix:]

    def design(j):
        srow = srow_ref[pl.ds(j, 1), :]
        live = live_ref[pl.ds(j, 1), :]
        pid = pid_ref[pl.ds(j, 1), :]
        visit = srow // rows
        y = coord((srow - visit * rows).astype(F32), ccd, rows, ccd_devs)
        ty = cheb_rows(jnp.broadcast_to(y, (ORDER, slots)), ORDER)
        member = jnp.where((pid == kid_s) & (live > 0), 1.0, 0.0).astype(BF16)
        vt = jnp.concatenate(
            [jnp.where((visit == v) & (live > 0), ty, 0.0) for v in range(vis)], axis=0
        )
        parts = jnp.concatenate([p.astype(F32) for p in split(ty, 3)] + [jnp.zeros_like(ty)], axis=0)
        left = jnp.concatenate([member, parts.astype(BF16)], axis=0)
        both = None
        for piece in split(vt, 3):
            part = dot_t(left, piece)
            both = part if both is None else both + part
        m_sc[pl.ds(pl.multiple_of(j * P_DEV, P_DEV), P_DEV), 0:n] = both[:P_DEV]
        return both[P_DEV:]

    def body(j, acc):
        start = pl.multiple_of(j * slots, slots)
        row_at = [
            rows_smem.at[pl.ds(i, (owners - 1) * slots + 1)][start] for i in range(slots)
        ]
        pieces = []
        for g in range(slots // 4):
            pair = []
            for h in range(2):
                s = 4 * g + 2 * h
                first = res_sc[pl.ds(row_at[s] + 8, 8), :]
                second = res_sc[pl.ds(row_at[s + 1] + 4, 8), :]
                pair.append(jnp.where(half, first, second))
            pieces.append(jnp.concatenate(pair, axis=0).astype(BF16))
        taps = jnp.concatenate(pieces, axis=0)
        row = row_sc[pl.ds(j, 1), :]
        cod = code_sc[pl.ds(j, 1), :]
        wgt = wi_sc[pl.ds(j, 1), :]
        visit = jnp.floor(row * (1.0 / rows))
        y = coord(row - visit * rows, ccd, rows, ccd_devs)
        ty = cheb_rows(jnp.broadcast_to(y, (ORDER, wide)), ORDER)
        ty = ty * jnp.where(cod < float(P_DEV), wgt, 0.0)
        lhs = [jnp.where(cod == kid, wgt, 0.0)]
        for v in range(vis):
            lhs.append(jnp.where(visit == float(v), ty, 0.0))
        lhs = jnp.concatenate(lhs, axis=0).astype(BF16)
        sums = dot(lhs, taps)
        t_ref[pl.ds(pl.multiple_of(j * P_DEV, P_DEV), P_DEV), :] = sums[:P_DEV]
        q_sc[...] += sums[P_DEV:]
        return acc + design(j)

    sy = lax.fori_loop(0, owners, body, jnp.zeros((4 * ORDER, n), F32), unroll=UNROLL)
    sy = sy[:ORDER] + sy[ORDER : 2 * ORDER] + sy[2 * ORDER : 3 * ORDER]
    sy_ref[...] = widen(sy)
    m_hi, m_lo = split(m_sc[...], 2)
    mtw_ref[...] = jnp.concatenate(split(m_sc[...].T[:n], 2), axis=0)
    m_hi, m_lo = m_hi.astype(F32), m_lo.astype(F32)
    wide_m = m_hi + pltpu.roll(m_hi, n, 1) + pltpu.roll(m_lo, 2 * n, 1)
    mw_ref[...] = wide_m.astype(BF16)
    full = dot_t(q_sc[...], tile_rows(const_ref[CXT], vis), HI)
    qb_ref[...] = widen(blocks_of(full, vis))


def tile_rows(x, times):
    return jnp.concatenate([x] * times, axis=0)


def blocks_of(full, vis):
    lane = iota((ORDER, full.shape[1]), 1) // ORDER
    out = jnp.zeros((ORDER, full.shape[1]), F32)
    for v in range(vis):
        out = out + jnp.where(lane == v, full[v * ORDER : (v + 1) * ORDER], 0.0)
    return out


def widen(x):
    return jnp.concatenate([x, jnp.zeros((x.shape[0], 128 - x.shape[1]), F32)], axis=1)


def pack(x):
    turned = [x] + [pltpu.roll(x, 32 * g, 1) for g in range(1, 4)]
    out = []
    for r in range(ORDER // 4):
        row = turned[0][4 * r : 4 * r + 1]
        for g in range(1, 4):
            row = row + turned[g][4 * r + g : 4 * r + g + 1]
        out.append(row)
    return out


def unpack(x):
    out = []
    for row in x:
        row = jnp.broadcast_to(row, (ORDER, 128))
        out.append(row[0:1])
        for g in range(1, 4):
            out.append(pltpu.roll(row, 128 - 32 * g, 1)[0:1])
    return out


def stack(rows):
    sub = iota((8, 128), 0)
    out = jnp.broadcast_to(rows[0], (8, 128))
    for i in range(1, len(rows)):
        out = jnp.where(sub == i, rows[i], out)
    return out


def moments_block(mtw_ref, back, q):
    n = mtw_ref.shape[0] // 2
    vis = n // ORDER
    b_hi, b_lo = split(back, 2)
    b_hi, b_lo = (tile_rows(x.astype(F32), vis).astype(BF16) for x in (b_hi, b_lo))
    full = dot_t(mtw_ref[...], b_hi)
    full = full[:n] + full[n:] + dot_t(mtw_ref[0:n], b_lo)
    return q - widen(blocks_of(full, vis))


def senders_sum(ref, lo, hi):
    total = ref[0, lo:hi].astype(F32)
    for i in range(1, ref.shape[0]):
        total = total + ref[i, lo:hi].astype(F32)
    return total


def first_kernel(arr_ref, mtw_ref, qb_ref, sy_ref, b_ref, den_ref, pay_ref):
    blocks = b_ref.shape[1] // 128
    total = senders_sum(arr_ref, 0, arr_ref.shape[1])
    back, dens = [], []
    for q in range(blocks):
        den = total[ORDER * blocks + q : ORDER * blocks + q + 1] + 1.0
        dens.append(jnp.broadcast_to(den, (ORDER, 128)))
        back.append(total[ORDER * q : ORDER * (q + 1)] / dens[-1])
    back = jnp.concatenate(back, axis=1)
    den_ref[...] = jnp.concatenate(dens, axis=1)
    b_ref[...] = back
    mom = moments_block(mtw_ref, back, qb_ref[...])
    block = stack(pack(mom) + pack(sy_ref[...]))[: pay_ref.shape[1]]
    for i in range(pay_ref.shape[0]):
        pay_ref[i] = block


def systems(sy, lam, vis):
    sub = iota((ORDER, 128), 0)
    base = iota((ORDER, 128), 1) // ORDER * ORDER
    return [
        jnp.take_along_axis(sy, base + b, axis=1, mode="promise_in_bounds") * lam
        + jnp.where(sub == b, RIDGE, 0.0)
        for b in range(ORDER)
    ]


def eliminate(mat, rhs):
    mat, rhs = list(mat), list(rhs)
    for p in range(ORDER):
        inv = 1.0 / mat[p][p : p + 1]
        mat[p] = mat[p] * inv
        rhs[p] = rhs[p] * inv
        for b in range(ORDER):
            if b != p:
                factor = mat[b][p : p + 1]
                mat[b] = mat[b] - factor * mat[p]
                rhs[b] = rhs[b] - factor * rhs[p]
    return rhs


def solve(mom, sy, lam, vis):
    out = stack(eliminate(systems(sy, lam, vis), mom))
    return jnp.where(iota((ORDER, 128), 1) < vis * ORDER, out, 0.0)


def block_diag(z, vis):
    n = vis * ORDER
    keep = iota((n, 128), 0) // ORDER == iota((n, 128), 1) // ORDER
    return jnp.where(keep, tile_rows(z, vis), 0.0)


def model_kernel(arr_ref, const_ref, mtw_ref, mw_ref, t_ref, sy_ref, pay_ref):
    vis = mtw_ref.shape[0] // (2 * ORDER)
    n = vis * ORDER
    total = arr_ref[0]
    for i in range(1, arr_ref.shape[0]):
        total = total + arr_ref[i]
    rows = ORDER // 4
    sy = stack(unpack([total[i : i + 1] for i in range(rows, 2 * rows)]))
    sy_ref[...] = sy
    mom = unpack([total[i : i + 1] for i in range(rows)])
    z = solve(mom, sy, const_ref[LAM_LANE], vis)
    square = block_diag(z, vis)
    diag = square.T[:n]
    weights = diag[:ORDER]
    for v in range(1, vis):
        weights = weights + diag[v * ORDER : (v + 1) * ORDER]
    w_hi, w_lo = split(weights, 2)
    model = (
        dot(w_hi, mtw_ref[0:n]) + dot(w_lo, mtw_ref[0:n]) + dot(w_hi, mtw_ref[n : 2 * n])
    )
    z_hi, z_lo = split(square, 2)
    c_hi, c_lo = split(tile_rows(const_ref[CXT], 128 // ORDER), 2)
    surface = dot(jnp.concatenate([z_hi, z_lo], axis=0), c_hi)
    surface = surface[:n] + surface[n:] + dot(z_hi, c_lo)
    s_hi, s_lo = split(surface, 2)
    surface = jnp.concatenate([s_hi, s_lo, s_hi, jnp.zeros((128 - 3 * n, 128), BF16)], axis=0)
    corrected = t_ref[...] - dot(mw_ref[...], surface)
    blocks = model.shape[1] // 128
    block = jnp.concatenate(
        [model[:, 128 * q : 128 * (q + 1)] for q in range(blocks)], axis=0
    ).astype(BF16)
    rows = ORDER * blocks
    for i in range(pay_ref.shape[0]):
        pay_ref[i, 0:rows] = block
        pay_ref[i, rows : rows + P_DEV] = corrected[P_DEV * i : P_DEV * (i + 1)].astype(BF16)


def second_kernel(arr_ref, b_ref, den_ref, mtw_ref, qb_ref, const_ref, pay_ref):
    blocks = b_ref.shape[1] // 128
    total = senders_sum(arr_ref, 0, ORDER * blocks)
    model = jnp.concatenate(
        [total[ORDER * q : ORDER * (q + 1)] for q in range(blocks)], axis=1
    )
    lam = const_ref[LAM_SUB][:, 0:1]
    mom = moments_block(mtw_ref, b_ref[...] - lam * model / den_ref[...], qb_ref[...])
    block = stack(pack(mom))[: pay_ref.shape[1]]
    for i in range(pay_ref.shape[0]):
        pay_ref[i] = block


def background_kernel(vis, arr_ref, den_ref, sy_ref, const_ref, out_ref, inv_ref):
    rows = arr_ref.shape[1] - P_DEV
    sums = senders_sum(arr_ref, rows, rows + P_DEV)
    own = lax.axis_index("visit") * P_DEV
    width = den_ref.shape[1]
    pick = iota((P_DEV, width), 1) == iota((P_DEV, width), 0) + own
    den = dot_t(jnp.where(pick, 1.0, 0.0), den_ref[...], HI)
    out_ref[...] = sums / den[:, 0:1]
    sub = iota((ORDER, 128), 0)
    unit = [jnp.where(sub == b, 1.0, 0.0) for b in range(ORDER)]
    inverse = eliminate(systems(sy_ref[...], const_ref[LAM_LANE], vis), unit)
    for b in range(ORDER):
        inv_ref[b] = inverse[b]


def final_kernel(arr_ref, inv_ref, const_ref, out_ref):
    vis = out_ref.shape[0]
    n = vis * ORDER
    total = arr_ref[0]
    for i in range(1, arr_ref.shape[0]):
        total = total + arr_ref[i]
    mom = unpack([total[i : i + 1] for i in range(ORDER // 4)])
    z = inv_ref[0] * mom[0]
    for d in range(1, ORDER):
        z = z + inv_ref[d] * mom[d]
    flat = tile_rows(z, ORDER).T[:n] * tile_rows(const_ref[ROT][:, : ORDER * ORDER], vis)
    for v in range(vis):
        out_ref[v : v + 1] = jnp.sum(flat[v * ORDER : (v + 1) * ORDER], axis=0, keepdims=True)


def call(kernel, out_shape, scratch=(), n_in=1, hbm=(), smem=()):
    spec = {i: HBM for i in hbm} | {i: SMEM for i in smem}
    fn = pl.pallas_call(
        kernel,
        out_shape=out_shape,
        in_specs=[spec.get(i, VMEM) for i in range(n_in)],
        out_specs=jax.tree.map(lambda _: VMEM, out_shape),
        scratch_shapes=list(scratch),
    )

    def run(*args):
        return fn(
            *(
                x if i in spec else pltpu.with_memory_space_constraint(x, pltpu.VMEM)
                for i, x in enumerate(args)
            )
        )

    return run


def shape(dims, dtype=F32):
    return pltpu.VMEM(dims, dtype)


def result(dims, dtype=F32):
    return jax.ShapeDtypeStruct(dims, dtype)


def exchange(x, axis):
    return lax.all_to_all(x, axis, split_axis=0, concat_axis=0, tiled=True)


def per_device(raw_rows, resample, slot_row, tap_weight, patch_id, live_mask):
    owners = lax.axis_size("visit")
    ccd_devs = lax.axis_size("ccd")
    vis, rows, pix = raw_rows.shape
    slots = slot_row.shape[3]
    patches = owners * P_DEV
    blocks = patches // 128
    nvb = vis * ORDER
    lam, rot, cxt = constants(pix)
    const = np.zeros((32, 128))
    const[CXT] = cxt
    const[LAM_LANE, :nvb] = np.tile(lam, vis)
    const[LAM_SUB] = lam[:, None]
    const[ROT, : ORDER * ORDER] = np.repeat(rot.T, ORDER, axis=1)
    const = jnp.asarray(const, F32)
    srow, pid, live = slot_row[0, 0], patch_id[0, 0], live_mask[0, 0]
    weights = tap_weight[:, 0, 0]
    pay_rows = ORDER * blocks + P_DEV

    ints = shape((owners, slots), jnp.int32)
    pay1, srow_v, raw_v, res_v, w_v, pid_v, live_v, const = call(
        project_kernel,
        (
            shape((owners, ORDER * blocks + 8, 128), BF16),
            ints,
            shape(raw_rows.shape, BF16),
            shape(resample.shape, BF16),
            shape((TAPS, owners, slots)),
            ints,
            ints,
            shape(const.shape),
        ),
        scratch=(
            pltpu.VMEM((owners, slots), F32),
            pltpu.VMEM((owners, slots), F32),
            pltpu.VMEM((owners, slots), F32),
            pltpu.VMEM((blocks, 4 * ORDER, 128), F32),
            pltpu.SemaphoreType.DMA((7,)),
        ),
        n_in=7,
        hbm=range(7),
    )(srow, raw_rows, resample, weights, pid, live, const)
    arr1 = exchange(pay1, "visit")
    tsum, qb, sy, mw, mtw = call(
        functools.partial(gather_kernel, ccd_devs),
        (
            shape((patches, pix)),
            shape((ORDER, 128)),
            shape((ORDER, 128)),
            shape((patches, 128), BF16),
            shape((2 * nvb, patches), BF16),
        ),
        scratch=(
            pltpu.VMEM((vis * rows + 16, pix), F32),
            pltpu.VMEM((owners, slots * TAPS), F32),
            pltpu.VMEM((owners, slots * TAPS), F32),
            pltpu.VMEM((owners, slots * TAPS), F32),
            pltpu.VMEM((nvb, pix), F32),
            pltpu.VMEM((patches, 128), F32),
        ),
        n_in=8,
        smem=(0,),
    )(srow.reshape(-1), raw_v, res_v, srow_v, w_v, pid_v, live_v, const)
    back, den, pay2 = call(
        first_kernel,
        (
            shape((ORDER, patches)),
            shape((ORDER, patches)),
            shape((ccd_devs, ORDER // 2, 128)),
        ),
        n_in=4,
    )(arr1, mtw, qb, sy)
    arr2 = exchange(pay2, "ccd")
    sy_all, pay3 = call(
        model_kernel,
        (shape((ORDER, 128)), shape((owners, pay_rows, 128), BF16)),
        n_in=5,
    )(arr2, const, mtw, mw, tsum)
    arr3 = exchange(pay3, "visit")
    pay4 = call(second_kernel, shape((ccd_devs, ORDER // 4, 128)), n_in=6)(
        arr3, back, den, mtw, qb, const
    )
    arr4 = exchange(pay4, "ccd")
    background, inverse = call(
        functools.partial(background_kernel, vis),
        (result((P_DEV, pix)), shape((ORDER, ORDER, 128))),
        n_in=4,
    )(arr3, den, sy_all, const)
    offsets = call(final_kernel, result((vis, ORDER * ORDER)), n_in=3)(arr4, inverse, const)
    return offsets, background


def solution(mesh):
    in_specs = (
        P("visit", "ccd", None),
        P("visit", None, None),
        P("visit", "ccd", None, None),
        P(None, "visit", "ccd", None, None),
        P("visit", "ccd", None, None),
        P("visit", "ccd", None, None),
    )
    out_specs = (P("visit", None), P(("visit", "ccd"), None))
    return jax.shard_map(
        per_device, mesh=mesh, in_specs=in_specs, out_specs=out_specs, check_vma=False
    )
```

```python
import functools

import jax
import jax.numpy as jnp
import numpy as np
from jax import lax
from jax.experimental import pallas as pl
from jax.experimental.pallas import tpu as pltpu
from jax.sharding import PartitionSpec as P

ORDER = 8
TAPS = 4
P_DEV = 16
RIDGE = 1.0
UNROLL = 8
UNROLL_W = 2
CXT, LAM_LANE, LAM_SUB, ROT = (slice(8 * i, 8 * (i + 1)) for i in range(4))
HI = lax.Precision.HIGHEST
F32 = jnp.float32
BF16 = jnp.bfloat16
VMEM = pl.BlockSpec(memory_space=pltpu.VMEM)
HBM = pl.BlockSpec(memory_space=pl.ANY)
SMEM = pl.BlockSpec(memory_space=pltpu.SMEM)


def constants(pixels):
    x = (2 * np.arange(pixels) + 1) / pixels - 1.0
    cx = [np.ones_like(x), x]
    for _ in range(2, ORDER):
        cx.append(2 * x * cx[-1] - cx[-2])
    cx = np.stack(cx)
    lam, rot = np.linalg.eigh(cx @ cx.T)
    return lam, rot, rot.T @ cx


def dot(a, b, precision=None):
    return lax.dot_general(
        a, b, (((1,), (0,)), ((), ())), precision=precision, preferred_element_type=F32
    )


def dot_t(a, b, precision=None):
    return lax.dot_general(
        a, b, (((1,), (1,)), ((), ())), precision=precision, preferred_element_type=F32
    )


def split(x, parts):
    out = []
    for _ in range(parts):
        out.append(x.astype(BF16))
        x = x - out[-1].astype(F32)
    return out


def iota(shape, dim):
    return lax.broadcasted_iota(jnp.int32, shape, dim)


def cheb_rows(y, count):
    sub = iota(y.shape, 0)
    prev, cur = jnp.ones_like(y), y
    out = jnp.where(sub == 0, prev, cur)
    for k in range(2, count):
        prev, cur = cur, 2.0 * y * cur - prev
        out = jnp.where(sub == k, cur, out)
    return out


def coord(b_pos, ccd, rows_local, ccd_devs):
    base = (ccd * rows_local).astype(F32)
    return (2.0 * (base + b_pos) + float(TAPS)) / float(rows_local * ccd_devs) - 1.0


def project_kernel(
    srow_hbm, raw_hbm, res_hbm, w_hbm, pid_hbm, live_hbm, const_hbm,
    pay_ref, srow_ref, raw_ref, res_ref, w_ref, pid_ref, live_ref, const_ref,
    hi_sc, lo_sc, code_sc, hot_sc, member_sc, acc_sc, sems,
):
    vis, rows, pix = raw_ref.shape
    owners, slots = srow_ref.shape
    blocks = owners * P_DEV // 128
    group = owners // blocks
    small = (
        (srow_hbm, srow_ref), (w_hbm, w_ref), (pid_hbm, pid_ref), (live_hbm, live_ref),
        (const_hbm, const_ref), (res_hbm, res_ref),
    )
    copies = [pltpu.make_async_copy(a, b, sems.at[n]) for n, (a, b) in enumerate(small)]
    raw_copies = [
        pltpu.make_async_copy(raw_hbm.at[v], raw_ref.at[v], sems.at[len(small) + v])
        for v in range(vis)
    ]
    for copy in copies + raw_copies:
        copy.start()
    for copy in copies:
        copy.wait()
    wide = 256
    span = wide - TAPS + 1
    srow = srow_ref[...].astype(F32)
    high = jnp.floor((srow + 0.5) * (1.0 / span))
    hi_sc[...] = high
    lo_sc[...] = srow - span * high
    place = P_DEV * (iota((owners, slots), 0) % group) + pid_ref[...]
    code_sc[...] = jnp.where(live_ref[...] > 0, place, -1).astype(F32)
    c_parts = jnp.concatenate(split(const_ref[CXT], 2), axis=0)
    kernels = []
    for v in range(vis):
        both = dot_t(c_parts, res_ref[v])
        kernels.append(jnp.concatenate(split(both[:ORDER] + both[ORDER:], 2), axis=0))
    rid = iota((wide, slots), 0).astype(F32).astype(BF16)
    ids = rid[:128]
    unit = jnp.ones((128, slots), BF16)
    def operands(j):
        low = lo_sc[pl.ds(j, 1), :]
        one = jnp.zeros((wide, slots), BF16)
        for t in range(TAPS):
            hit = rid == (low + float(t)).astype(BF16)
            one = jnp.where(hit, w_ref[t, pl.ds(j, 1), :].astype(BF16), one)
        code = code_sc[pl.ds(j, 1), :].astype(BF16)
        return one, jnp.where(ids == code, unit, jnp.zeros_like(unit))

    def build(j, carry):
        hot_sc[j], member_sc[j] = operands(j)
        return carry

    early = blocks // 2
    lax.fori_loop(0, early * group, build, 0, unroll=UNROLL_W)
    for copy in raw_copies:
        copy.wait()
    pieces = []
    for v in range(vis):
        both = dot_t(kernels[v], raw_ref[v])
        pieces.append(both[:ORDER] + both[ORDER:])
    table = jnp.concatenate(pieces, axis=1)
    tiles = vis * rows // 128
    lane = iota((ORDER, 128), 1)

    def window(start):
        first, shift = start // 128, start % 128
        a, b = (
            table[:, 128 * t : 128 * (t + 1)]
            for t in (min(first, tiles - 1), min(first + 1, tiles - 1))
        )
        if not shift:
            return a
        a, b = pltpu.roll(a, 128 - shift, 1), pltpu.roll(b, 128 - shift, 1)
        return jnp.where(lane < 128 - shift, a, b)

    windows = []
    for k in range(-(-(vis * rows - TAPS + 1) // span)):
        parts = [window(span * k + c) for c in range(0, wide, 128)]
        windows.append(jnp.concatenate(parts, axis=1))
    if len(windows) % 2:
        windows.append(jnp.zeros((ORDER, wide), F32))
    left = jnp.concatenate(windows, axis=0).astype(BF16)
    ones = jnp.ones((ORDER, slots), BF16)

    def pair_sums(m, made):
        both = [2 * m, 2 * m + 1]
        pairs = [(hot_sc[j], member_sc[j]) if made else operands(j) for j in both]
        vals = dot(left, jnp.concatenate([p[0] for p in pairs], axis=1))
        left_sums = []
        for h, j in enumerate(both):
            high = jnp.broadcast_to(hi_sc[pl.ds(j, 1), :], (ORDER, slots))
            got = jnp.zeros((ORDER, slots), F32)
            for k in range(len(windows)):
                part = vals[ORDER * k : ORDER * (k + 1), slots * h : slots * (h + 1)]
                got = jnp.where(high == float(k), part, got)
            left_sums.append(jnp.concatenate(split(got, 2) + [ones, ones], axis=0))
        members = jnp.concatenate([p[1] for p in pairs], axis=1)
        return dot_t(jnp.concatenate(left_sums, axis=1), members)

    def body(made, q, carry):
        pairs = group // 2
        total = pair_sums(q * pairs, made)
        for m in range(1, pairs):
            total = total + pair_sums(q * pairs + m, made)
        acc_sc[q] = total
        return carry

    lax.fori_loop(0, early, functools.partial(body, True), 0, unroll=True)
    lax.fori_loop(early, blocks, functools.partial(body, False), 0, unroll=True)
    sub = iota((8, 128), 0)
    tail = jnp.zeros((8, 128), F32)
    rows_out = []
    for q in range(blocks):
        rows_out.append(acc_sc[q, 0:ORDER] + acc_sc[q, ORDER : 2 * ORDER])
        tail = jnp.where(sub == q, acc_sc[q, 2 * ORDER : 3 * ORDER], tail)
    block = jnp.concatenate(rows_out + [tail], axis=0).astype(BF16)
    for i in range(owners):
        pay_ref[i] = block


def gather_kernel(
    ccd_devs, rows_smem, raw_ref, res_ref, srow_ref, w_ref, pid_ref, live_ref, const_ref,
    t_ref, qb_ref, sy_ref, mw_ref, mtw_ref,
    res_sc, row_sc, code_sc, wi_sc, q_sc, m_sc,
):
    vis, rows, pix = raw_ref.shape
    owners, slots = srow_ref.shape
    wide = slots * TAPS
    n = vis * ORDER
    ccd = lax.axis_index("ccd")
    off = iota((slots, wide), 1) - TAPS * iota((slots, wide), 0)
    rep = jnp.where((off >= 0) & (off < TAPS), 1.0, 0.0).astype(BF16)
    srow = srow_ref[...]
    code = pid_ref[...] + P_DEV * (1 - live_ref[...])
    high, low = srow >> 8, srow & 255
    whole = jnp.concatenate([high, low, code], axis=0).astype(F32).astype(BF16)
    whole = dot(whole, rep)
    row_sc[...] = 256.0 * whole[:owners] + whole[owners : 2 * owners]
    code_sc[...] = whole[2 * owners :]
    wi = None
    for t in range(TAPS):
        pick = jnp.where(off == t, 1.0, 0.0).astype(BF16)
        part = dot(w_ref[t].astype(BF16), pick)
        wi = part if wi is None else wi + part
    wi_sc[...] = wi
    q_sc[...] = jnp.zeros_like(q_sc)
    m_sc[...] = jnp.zeros_like(m_sc)
    half = iota((8, pix), 0) < TAPS
    kid = iota((P_DEV, wide), 0).astype(F32)
    kid_s = iota((P_DEV, slots), 0)
    zero = jnp.zeros((pix, pix), BF16)
    for v in range(0, vis, 2):
        pair = jnp.concatenate([raw_ref[v], raw_ref[v + 1]], axis=1)
        diag = jnp.concatenate(
            [
                jnp.concatenate([res_ref[v], zero], axis=1),
                jnp.concatenate([zero, res_ref[v + 1]], axis=1),
            ],
            axis=0,
        )
        both = dot(pair, diag)
        res_sc[pl.ds(8 + v * rows, rows), :] = both[:, :pix]
        res_sc[pl.ds(8 + (v + 1) * rows, rows), :] = both[:, pix:]

    def design(j):
        srow = srow_ref[pl.ds(j, 1), :]
        live = live_ref[pl.ds(j, 1), :]
        pid = pid_ref[pl.ds(j, 1), :]
        visit = srow // rows
        y = coord((srow - visit * rows).astype(F32), ccd, rows, ccd_devs)
        ty = cheb_rows(jnp.broadcast_to(y, (ORDER, slots)), ORDER)
        member = jnp.where((pid == kid_s) & (live > 0), 1.0, 0.0).astype(BF16)
        vt = jnp.concatenate(
            [jnp.where((visit == v) & (live > 0), ty, 0.0) for v in range(vis)], axis=0
        )
        parts = jnp.concatenate([p.astype(F32) for p in split(ty, 3)] + [jnp.zeros_like(ty)], axis=0)
        left = jnp.concatenate([member, parts.astype(BF16)], axis=0)
        both = None
        for piece in split(vt, 3):
            part = dot_t(left, piece)
            both = part if both is None else both + part
        m_sc[pl.ds(pl.multiple_of(j * P_DEV, P_DEV), P_DEV), 0:n] = both[:P_DEV]
        return both[P_DEV:]

    def body(j, acc):
        start = pl.multiple_of(j * slots, slots)
        row_at = [
            rows_smem.at[pl.ds(i, (owners - 1) * slots + 1)][start] for i in range(slots)
        ]
        pieces = []
        for g in range(slots // 4):
            pair = []
            for h in range(2):
                s = 4 * g + 2 * h
                first = res_sc[pl.ds(row_at[s] + 8, 8), :]
                second = res_sc[pl.ds(row_at[s + 1] + 4, 8), :]
                pair.append(jnp.where(half, first, second))
            pieces.append(jnp.concatenate(pair, axis=0).astype(BF16))
        taps = jnp.concatenate(pieces, axis=0)
        row = row_sc[pl.ds(j, 1), :]
        cod = code_sc[pl.ds(j, 1), :]
        wgt = wi_sc[pl.ds(j, 1), :]
        visit = jnp.floor(row * (1.0 / rows))
        y = coord(row - visit * rows, ccd, rows, ccd_devs)
        ty = cheb_rows(jnp.broadcast_to(y, (ORDER, wide)), ORDER)
        ty = ty * jnp.where(cod < float(P_DEV), wgt, 0.0)
        lhs = [jnp.where(cod == kid, wgt, 0.0)]
        for v in range(vis):
            lhs.append(jnp.where(visit == float(v), ty, 0.0))
        lhs = jnp.concatenate(lhs, axis=0).astype(BF16)
        sums = dot(lhs, taps)
        t_ref[pl.ds(pl.multiple_of(j * P_DEV, P_DEV), P_DEV), :] = sums[:P_DEV]
        q_sc[...] += sums[P_DEV:]
        return acc + design(j)

    sy = lax.fori_loop(0, owners, body, jnp.zeros((4 * ORDER, n), F32), unroll=UNROLL)
    sy = sy[:ORDER] + sy[ORDER : 2 * ORDER] + sy[2 * ORDER : 3 * ORDER]
    sy_ref[...] = widen(sy)
    m_hi, m_lo = split(m_sc[...], 2)
    mtw_ref[...] = jnp.concatenate(split(m_sc[...].T[:n], 2), axis=0)
    m_hi, m_lo = m_hi.astype(F32), m_lo.astype(F32)
    wide_m = m_hi + pltpu.roll(m_hi, n, 1) + pltpu.roll(m_lo, 2 * n, 1)
    mw_ref[...] = wide_m.astype(BF16)
    full = dot_t(q_sc[...], tile_rows(const_ref[CXT], vis), HI)
    qb_ref[...] = widen(blocks_of(full, vis))


def tile_rows(x, times):
    return jnp.concatenate([x] * times, axis=0)


def blocks_of(full, vis):
    lane = iota((ORDER, full.shape[1]), 1) // ORDER
    out = jnp.zeros((ORDER, full.shape[1]), F32)
    for v in range(vis):
        out = out + jnp.where(lane == v, full[v * ORDER : (v + 1) * ORDER], 0.0)
    return out


def widen(x):
    return jnp.concatenate([x, jnp.zeros((x.shape[0], 128 - x.shape[1]), F32)], axis=1)


def pack(x):
    turned = [x] + [pltpu.roll(x, 32 * g, 1) for g in range(1, 4)]
    out = []
    for r in range(ORDER // 4):
        row = turned[0][4 * r : 4 * r + 1]
        for g in range(1, 4):
            row = row + turned[g][4 * r + g : 4 * r + g + 1]
        out.append(row)
    return out


def unpack(x):
    out = []
    for row in x:
        row = jnp.broadcast_to(row, (ORDER, 128))
        out.append(row[0:1])
        for g in range(1, 4):
            out.append(pltpu.roll(row, 128 - 32 * g, 1)[0:1])
    return out


def stack(rows):
    sub = iota((8, 128), 0)
    out = jnp.broadcast_to(rows[0], (8, 128))
    for i in range(1, len(rows)):
        out = jnp.where(sub == i, rows[i], out)
    return out


def moments_block(mtw_ref, back, q):
    n = mtw_ref.shape[0] // 2
    vis = n // ORDER
    b_hi, b_lo = split(back, 2)
    b_hi, b_lo = (tile_rows(x.astype(F32), vis).astype(BF16) for x in (b_hi, b_lo))
    full = dot_t(mtw_ref[...], b_hi)
    full = full[:n] + full[n:] + dot_t(mtw_ref[0:n], b_lo)
    return q - widen(blocks_of(full, vis))


def senders_sum(ref, lo, hi):
    total = ref[0, lo:hi].astype(F32)
    for i in range(1, ref.shape[0]):
        total = total + ref[i, lo:hi].astype(F32)
    return total


def first_kernel(arr_ref, mtw_ref, qb_ref, sy_ref, b_ref, den_ref, pay_ref):
    blocks = b_ref.shape[1] // 128
    total = senders_sum(arr_ref, 0, arr_ref.shape[1])
    back, dens = [], []
    for q in range(blocks):
        den = total[ORDER * blocks + q : ORDER * blocks + q + 1] + 1.0
        dens.append(jnp.broadcast_to(den, (ORDER, 128)))
        back.append(total[ORDER * q : ORDER * (q + 1)] / dens[-1])
    back = jnp.concatenate(back, axis=1)
    den_ref[...] = jnp.concatenate(dens, axis=1)
    b_ref[...] = back
    mom = moments_block(mtw_ref, back, qb_ref[...])
    block = stack(pack(mom) + pack(sy_ref[...]))[: pay_ref.shape[1]]
    for i in range(pay_ref.shape[0]):
        pay_ref[i] = block


def systems(sy, lam, vis):
    sub = iota((ORDER, 128), 0)
    base = iota((ORDER, 128), 1) // ORDER * ORDER
    return [
        jnp.take_along_axis(sy, base + b, axis=1, mode="promise_in_bounds") * lam
        + jnp.where(sub == b, RIDGE, 0.0)
        for b in range(ORDER)
    ]


def eliminate(mat, rhs):
    mat, rhs = list(mat), list(rhs)
    for p in range(ORDER):
        inv = 1.0 / mat[p][p : p + 1]
        mat[p] = mat[p] * inv
        rhs[p] = rhs[p] * inv
        for b in range(ORDER):
            if b != p:
                factor = mat[b][p : p + 1]
                mat[b] = mat[b] - factor * mat[p]
                rhs[b] = rhs[b] - factor * rhs[p]
    return rhs


def solve(mom, sy, lam, vis):
    out = stack(eliminate(systems(sy, lam, vis), mom))
    return jnp.where(iota((ORDER, 128), 1) < vis * ORDER, out, 0.0)


def block_diag(z, vis):
    n = vis * ORDER
    keep = iota((n, 128), 0) // ORDER == iota((n, 128), 1) // ORDER
    return jnp.where(keep, tile_rows(z, vis), 0.0)


def model_kernel(arr_ref, const_ref, mtw_ref, mw_ref, t_ref, sy_ref, pay_ref):
    vis = mtw_ref.shape[0] // (2 * ORDER)
    n = vis * ORDER
    total = arr_ref[0]
    for i in range(1, arr_ref.shape[0]):
        total = total + arr_ref[i]
    rows = ORDER // 4
    sy = stack(unpack([total[i : i + 1] for i in range(rows, 2 * rows)]))
    sy_ref[...] = sy
    mom = unpack([total[i : i + 1] for i in range(rows)])
    z = solve(mom, sy, const_ref[LAM_LANE], vis)
    square = block_diag(z, vis)
    diag = square.T[:n]
    weights = diag[:ORDER]
    for v in range(1, vis):
        weights = weights + diag[v * ORDER : (v + 1) * ORDER]
    w_hi, w_lo = split(weights, 2)
    model = (
        dot(w_hi, mtw_ref[0:n]) + dot(w_lo, mtw_ref[0:n]) + dot(w_hi, mtw_ref[n : 2 * n])
    )
    z_hi, z_lo = split(square, 2)
    c_hi, c_lo = split(tile_rows(const_ref[CXT], 128 // ORDER), 2)
    surface = dot(jnp.concatenate([z_hi, z_lo], axis=0), c_hi)
    surface = surface[:n] + surface[n:] + dot(z_hi, c_lo)
    s_hi, s_lo = split(surface, 2)
    surface = jnp.concatenate([s_hi, s_lo, s_hi, jnp.zeros((128 - 3 * n, 128), BF16)], axis=0)
    corrected = t_ref[...] - dot(mw_ref[...], surface)
    blocks = model.shape[1] // 128
    block = jnp.concatenate(
        [model[:, 128 * q : 128 * (q + 1)] for q in range(blocks)], axis=0
    ).astype(BF16)
    rows = ORDER * blocks
    for i in range(pay_ref.shape[0]):
        pay_ref[i, 0:rows] = block
        pay_ref[i, rows : rows + P_DEV] = corrected[P_DEV * i : P_DEV * (i + 1)].astype(BF16)


def second_kernel(arr_ref, b_ref, den_ref, mtw_ref, qb_ref, const_ref, pay_ref):
    blocks = b_ref.shape[1] // 128
    total = senders_sum(arr_ref, 0, ORDER * blocks)
    model = jnp.concatenate(
        [total[ORDER * q : ORDER * (q + 1)] for q in range(blocks)], axis=1
    )
    lam = const_ref[LAM_SUB][:, 0:1]
    mom = moments_block(mtw_ref, b_ref[...] - lam * model / den_ref[...], qb_ref[...])
    block = stack(pack(mom))[: pay_ref.shape[1]]
    for i in range(pay_ref.shape[0]):
        pay_ref[i] = block


def background_kernel(vis, arr_ref, den_ref, sy_ref, const_ref, out_ref, inv_ref):
    rows = arr_ref.shape[1] - P_DEV
    sums = senders_sum(arr_ref, rows, rows + P_DEV)
    own = lax.axis_index("visit") * P_DEV
    width = den_ref.shape[1]
    pick = iota((P_DEV, width), 1) == iota((P_DEV, width), 0) + own
    den = dot_t(jnp.where(pick, 1.0, 0.0), den_ref[...], HI)
    out_ref[...] = sums / den[:, 0:1]
    sub = iota((ORDER, 128), 0)
    unit = [jnp.where(sub == b, 1.0, 0.0) for b in range(ORDER)]
    inverse = eliminate(systems(sy_ref[...], const_ref[LAM_LANE], vis), unit)
    for b in range(ORDER):
        inv_ref[b] = inverse[b]


def final_kernel(arr_ref, inv_ref, const_ref, out_ref):
    vis = out_ref.shape[0]
    n = vis * ORDER
    total = arr_ref[0]
    for i in range(1, arr_ref.shape[0]):
        total = total + arr_ref[i]
    mom = unpack([total[i : i + 1] for i in range(ORDER // 4)])
    z = inv_ref[0] * mom[0]
    for d in range(1, ORDER):
        z = z + inv_ref[d] * mom[d]
    flat = tile_rows(z, ORDER).T[:n] * tile_rows(const_ref[ROT][:, : ORDER * ORDER], vis)
    for v in range(vis):
        out_ref[v : v + 1] = jnp.sum(flat[v * ORDER : (v + 1) * ORDER], axis=0, keepdims=True)


def call(kernel, out_shape, scratch=(), n_in=1, hbm=(), smem=()):
    spec = {i: HBM for i in hbm} | {i: SMEM for i in smem}
    fn = pl.pallas_call(
        kernel,
        out_shape=out_shape,
        in_specs=[spec.get(i, VMEM) for i in range(n_in)],
        out_specs=jax.tree.map(lambda _: VMEM, out_shape),
        scratch_shapes=list(scratch),
    )

    def run(*args):
        return fn(
            *(
                x if i in spec else pltpu.with_memory_space_constraint(x, pltpu.VMEM)
                for i, x in enumerate(args)
            )
        )

    return run


def shape(dims, dtype=F32):
    return pltpu.VMEM(dims, dtype)


def result(dims, dtype=F32):
    return jax.ShapeDtypeStruct(dims, dtype)


def exchange(x, axis):
    return lax.all_to_all(x, axis, split_axis=0, concat_axis=0, tiled=True)


def per_device(raw_rows, resample, slot_row, tap_weight, patch_id, live_mask):
    owners = lax.axis_size("visit")
    ccd_devs = lax.axis_size("ccd")
    vis, rows, pix = raw_rows.shape
    slots = slot_row.shape[3]
    patches = owners * P_DEV
    blocks = patches // 128
    nvb = vis * ORDER
    lam, rot, cxt = constants(pix)
    const = np.zeros((32, 128))
    const[CXT] = cxt
    const[LAM_LANE, :nvb] = np.tile(lam, vis)
    const[LAM_SUB] = lam[:, None]
    const[ROT, : ORDER * ORDER] = np.repeat(rot.T, ORDER, axis=1)
    const = jnp.asarray(const, F32)
    srow, pid, live = slot_row[0, 0], patch_id[0, 0], live_mask[0, 0]
    weights = tap_weight[:, 0, 0]
    pay_rows = ORDER * blocks + P_DEV

    ints = shape((owners, slots), jnp.int32)
    pay1, srow_v, raw_v, res_v, w_v, pid_v, live_v, const = call(
        project_kernel,
        (
            shape((owners, ORDER * blocks + 8, 128), BF16),
            ints,
            shape(raw_rows.shape, BF16),
            shape(resample.shape, BF16),
            shape((TAPS, owners, slots)),
            ints,
            ints,
            shape(const.shape),
        ),
        scratch=(
            pltpu.VMEM((owners, slots), F32),
            pltpu.VMEM((owners, slots), F32),
            pltpu.VMEM((owners, slots), F32),
            pltpu.VMEM((owners // 2, 256, slots), BF16),
            pltpu.VMEM((owners // 2, 128, slots), BF16),
            pltpu.VMEM((blocks, 4 * ORDER, 128), F32),
            pltpu.SemaphoreType.DMA((6 + vis,)),
        ),
        n_in=7,
        hbm=range(7),
    )(srow, raw_rows, resample, weights, pid, live, const)
    arr1 = exchange(pay1, "visit")
    tsum, qb, sy, mw, mtw = call(
        functools.partial(gather_kernel, ccd_devs),
        (
            shape((patches, pix)),
            shape((ORDER, 128)),
            shape((ORDER, 128)),
            shape((patches, 128), BF16),
            shape((2 * nvb, patches), BF16),
        ),
        scratch=(
            pltpu.VMEM((vis * rows + 16, pix), F32),
            pltpu.VMEM((owners, slots * TAPS), F32),
            pltpu.VMEM((owners, slots * TAPS), F32),
            pltpu.VMEM((owners, slots * TAPS), F32),
            pltpu.VMEM((nvb, pix), F32),
            pltpu.VMEM((patches, 128), F32),
        ),
        n_in=8,
        smem=(0,),
    )(srow.reshape(-1), raw_v, res_v, srow_v, w_v, pid_v, live_v, const)
    back, den, pay2 = call(
        first_kernel,
        (
            shape((ORDER, patches)),
            shape((ORDER, patches)),
            shape((ccd_devs, ORDER // 2, 128)),
        ),
        n_in=4,
    )(arr1, mtw, qb, sy)
    arr2 = exchange(pay2, "ccd")
    sy_all, pay3 = call(
        model_kernel,
        (shape((ORDER, 128)), shape((owners, pay_rows, 128), BF16)),
        n_in=5,
    )(arr2, const, mtw, mw, tsum)
    arr3 = exchange(pay3, "visit")
    pay4 = call(second_kernel, shape((ccd_devs, ORDER // 4, 128)), n_in=6)(
        arr3, back, den, mtw, qb, const
    )
    arr4 = exchange(pay4, "ccd")
    background, inverse = call(
        functools.partial(background_kernel, vis),
        (result((P_DEV, pix)), shape((ORDER, ORDER, 128))),
        n_in=4,
    )(arr3, den, sy_all, const)
    offsets = call(final_kernel, result((vis, ORDER * ORDER)), n_in=3)(arr4, inverse, const)
    return offsets, background


def solution(mesh):
    in_specs = (
        P("visit", "ccd", None),
        P("visit", None, None),
        P("visit", "ccd", None, None),
        P(None, "visit", "ccd", None, None),
        P("visit", "ccd", None, None),
        P("visit", "ccd", None, None),
    )
    out_specs = (P("visit", None), P(("visit", "ccd"), None))
    return jax.shard_map(
        per_device, mesh=mesh, in_specs=in_specs, out_specs=out_specs, check_vma=False
    )
```

```python
import functools

import jax
import jax.numpy as jnp
import numpy as np
from jax import lax
from jax.experimental import pallas as pl
from jax.experimental.pallas import tpu as pltpu
from jax.sharding import PartitionSpec as P

ORDER = 8
TAPS = 4
P_DEV = 16
RIDGE = 1.0
UNROLL = 8
UNROLL_W = 2
CXT, LAM_LANE, LAM_SUB, ROT = (slice(8 * i, 8 * (i + 1)) for i in range(4))
HI = lax.Precision.HIGHEST
F32 = jnp.float32
BF16 = jnp.bfloat16
VMEM = pl.BlockSpec(memory_space=pltpu.VMEM)
HBM = pl.BlockSpec(memory_space=pl.ANY)
SMEM = pl.BlockSpec(memory_space=pltpu.SMEM)


def constants(pixels):
    x = (2 * np.arange(pixels) + 1) / pixels - 1.0
    cx = [np.ones_like(x), x]
    for _ in range(2, ORDER):
        cx.append(2 * x * cx[-1] - cx[-2])
    cx = np.stack(cx)
    lam, rot = np.linalg.eigh(cx @ cx.T)
    return lam, rot, rot.T @ cx


def dot(a, b, precision=None):
    return lax.dot_general(
        a, b, (((1,), (0,)), ((), ())), precision=precision, preferred_element_type=F32
    )


def dot_t(a, b, precision=None):
    return lax.dot_general(
        a, b, (((1,), (1,)), ((), ())), precision=precision, preferred_element_type=F32
    )


def split(x, parts):
    out = []
    for _ in range(parts):
        out.append(x.astype(BF16))
        x = x - out[-1].astype(F32)
    return out


def iota(shape, dim):
    return lax.broadcasted_iota(jnp.int32, shape, dim)


def cheb_rows(y, count):
    sub = iota(y.shape, 0)
    prev, cur = jnp.ones_like(y), y
    out = jnp.where(sub == 0, prev, cur)
    for k in range(2, count):
        prev, cur = cur, 2.0 * y * cur - prev
        out = jnp.where(sub == k, cur, out)
    return out


def coord(b_pos, ccd, rows_local, ccd_devs):
    base = (ccd * rows_local).astype(F32)
    return (2.0 * (base + b_pos) + float(TAPS)) / float(rows_local * ccd_devs) - 1.0


def project_kernel(
    srow_hbm, raw_hbm, res_hbm, w_hbm, pid_hbm, live_hbm, const_hbm,
    pay_ref, srow_ref, raw_ref, res_ref, w_ref, pid_ref, live_ref, const_ref,
    hi_sc, lo_sc, code_sc, hot_sc, member_sc, acc_sc, sems,
):
    vis, rows, pix = raw_ref.shape
    owners, slots = srow_ref.shape
    blocks = owners * P_DEV // 128
    group = owners // blocks
    small = (
        (srow_hbm, srow_ref), (w_hbm, w_ref), (pid_hbm, pid_ref), (live_hbm, live_ref),
        (const_hbm, const_ref), (res_hbm, res_ref),
    )
    copies = [pltpu.make_async_copy(a, b, sems.at[n]) for n, (a, b) in enumerate(small)]
    raw_copies = [
        pltpu.make_async_copy(raw_hbm.at[v], raw_ref.at[v], sems.at[len(small) + v])
        for v in range(vis)
    ]
    for copy in copies + raw_copies:
        copy.start()
    for copy in copies:
        copy.wait()
    wide = 256
    span = wide - TAPS + 1
    srow = srow_ref[...].astype(F32)
    high = jnp.floor((srow + 0.5) * (1.0 / span))
    hi_sc[...] = high
    lo_sc[...] = srow - span * high
    place = P_DEV * (iota((owners, slots), 0) % group) + pid_ref[...]
    code_sc[...] = jnp.where(live_ref[...] > 0, place, -1).astype(F32)
    c_parts = jnp.concatenate(split(const_ref[CXT], 2), axis=0)
    kernels = []
    for v in range(vis):
        both = dot_t(c_parts, res_ref[v])
        kernels.append(jnp.concatenate(split(both[:ORDER] + both[ORDER:], 2), axis=0))
    rid = iota((wide, slots), 0).astype(F32).astype(BF16)
    ids = rid[:128]
    unit = jnp.ones((128, slots), BF16)
    def operands(j):
        low = lo_sc[pl.ds(j, 1), :]
        one = jnp.zeros((wide, slots), BF16)
        for t in range(TAPS):
            hit = rid == (low + float(t)).astype(BF16)
            one = jnp.where(hit, w_ref[t, pl.ds(j, 1), :].astype(BF16), one)
        code = code_sc[pl.ds(j, 1), :].astype(BF16)
        return one, jnp.where(ids == code, unit, jnp.zeros_like(unit))

    def build(j, carry):
        hot_sc[j], member_sc[j] = operands(j)
        return carry

    early = blocks // 2
    lax.fori_loop(0, early * group, build, 0, unroll=UNROLL_W)
    for copy in raw_copies:
        copy.wait()
    pieces = []
    for v in range(vis):
        both = dot_t(kernels[v], raw_ref[v])
        pieces.append(both[:ORDER] + both[ORDER:])
    table = jnp.concatenate(pieces, axis=1)
    tiles = vis * rows // 128
    lane = iota((ORDER, 128), 1)

    def window(start):
        first, shift = start // 128, start % 128
        a, b = (
            table[:, 128 * t : 128 * (t + 1)]
            for t in (min(first, tiles - 1), min(first + 1, tiles - 1))
        )
        if not shift:
            return a
        a, b = pltpu.roll(a, 128 - shift, 1), pltpu.roll(b, 128 - shift, 1)
        return jnp.where(lane < 128 - shift, a, b)

    windows = []
    for k in range(-(-(vis * rows - TAPS + 1) // span)):
        parts = [window(span * k + c) for c in range(0, wide, 128)]
        windows.append(jnp.concatenate(parts, axis=1))
    if len(windows) % 2:
        windows.append(jnp.zeros((ORDER, wide), F32))
    left = jnp.concatenate(windows, axis=0).astype(BF16)
    ones = jnp.ones((ORDER, slots), BF16)

    def pair_sums(m, made):
        both = [2 * m, 2 * m + 1]
        pairs = [(hot_sc[j], member_sc[j]) if made else operands(j) for j in both]
        vals = dot(left, jnp.concatenate([p[0] for p in pairs], axis=1))
        left_sums = []
        for h, j in enumerate(both):
            high = jnp.broadcast_to(hi_sc[pl.ds(j, 1), :], (ORDER, slots))
            got = jnp.zeros((ORDER, slots), F32)
            for k in range(len(windows)):
                part = vals[ORDER * k : ORDER * (k + 1), slots * h : slots * (h + 1)]
                got = jnp.where(high == float(k), part, got)
            left_sums.append(jnp.concatenate(split(got, 2) + [ones, ones], axis=0))
        members = jnp.concatenate([p[1] for p in pairs], axis=1)
        return dot_t(jnp.concatenate(left_sums, axis=1), members)

    def body(made, q, carry):
        pairs = group // 2
        total = pair_sums(q * pairs, made)
        for m in range(1, pairs):
            total = total + pair_sums(q * pairs + m, made)
        acc_sc[q] = total
        return carry

    lax.fori_loop(0, early, functools.partial(body, True), 0, unroll=True)
    lax.fori_loop(early, blocks, functools.partial(body, False), 0, unroll=True)
    sub = iota((8, 128), 0)
    tail = jnp.zeros((8, 128), F32)
    rows_out = []
    for q in range(blocks):
        rows_out.append(acc_sc[q, 0:ORDER] + acc_sc[q, ORDER : 2 * ORDER])
        tail = jnp.where(sub == q, acc_sc[q, 2 * ORDER : 3 * ORDER], tail)
    block = jnp.concatenate(rows_out + [tail], axis=0).astype(BF16)
    for i in range(owners):
        pay_ref[i] = block


def gather_kernel(
    ccd_devs, rows_smem, raw_ref, res_ref, srow_ref, w_ref, pid_ref, live_ref, const_ref,
    t_ref, qb_ref, sy_ref, mw_ref, mtw_ref,
    res_sc, row_sc, code_sc, wi_sc, q_sc, m_sc,
):
    vis, rows, pix = raw_ref.shape
    owners, slots = srow_ref.shape
    wide = slots * TAPS
    n = vis * ORDER
    ccd = lax.axis_index("ccd")
    off = iota((slots, wide), 1) - TAPS * iota((slots, wide), 0)
    rep = jnp.where((off >= 0) & (off < TAPS), 1.0, 0.0).astype(BF16)
    srow = srow_ref[...]
    code = pid_ref[...] + P_DEV * (1 - live_ref[...])
    high, low = srow >> 8, srow & 255
    whole = jnp.concatenate([high, low, code], axis=0).astype(F32).astype(BF16)
    whole = dot(whole, rep)
    row_sc[...] = 256.0 * whole[:owners] + whole[owners : 2 * owners]
    code_sc[...] = whole[2 * owners :]
    wi = None
    for t in range(TAPS):
        pick = jnp.where(off == t, 1.0, 0.0).astype(BF16)
        part = dot(w_ref[t].astype(BF16), pick)
        wi = part if wi is None else wi + part
    wi_sc[...] = wi
    q_sc[...] = jnp.zeros_like(q_sc)
    m_sc[...] = jnp.zeros_like(m_sc)
    half = iota((8, pix), 0) < TAPS
    kid = iota((P_DEV, wide), 0).astype(F32)
    kid_s = iota((P_DEV, slots), 0)
    zero = jnp.zeros((pix, pix), BF16)
    for v in range(0, vis, 2):
        pair = jnp.concatenate([raw_ref[v], raw_ref[v + 1]], axis=1)
        diag = jnp.concatenate(
            [
                jnp.concatenate([res_ref[v], zero], axis=1),
                jnp.concatenate([zero, res_ref[v + 1]], axis=1),
            ],
            axis=0,
        )
        both = dot(pair, diag)
        res_sc[pl.ds(8 + v * rows, rows), :] = both[:, :pix]
        res_sc[pl.ds(8 + (v + 1) * rows, rows), :] = both[:, pix:]

    def design(j):
        srow = srow_ref[pl.ds(j, 1), :]
        live = live_ref[pl.ds(j, 1), :]
        pid = pid_ref[pl.ds(j, 1), :]
        visit = srow // rows
        y = coord((srow - visit * rows).astype(F32), ccd, rows, ccd_devs)
        ty = cheb_rows(jnp.broadcast_to(y, (ORDER, slots)), ORDER)
        member = jnp.where((pid == kid_s) & (live > 0), 1.0, 0.0).astype(BF16)
        vt = jnp.concatenate(
            [jnp.where((visit == v) & (live > 0), ty, 0.0) for v in range(vis)], axis=0
        )
        parts = jnp.concatenate([p.astype(F32) for p in split(ty, 3)] + [jnp.zeros_like(ty)], axis=0)
        left = jnp.concatenate([member, parts.astype(BF16)], axis=0)
        both = None
        for piece in split(vt, 3):
            part = dot_t(left, piece)
            both = part if both is None else both + part
        m_sc[pl.ds(pl.multiple_of(j * P_DEV, P_DEV), P_DEV), 0:n] = both[:P_DEV]
        return both[P_DEV:]

    def body(j, acc):
        start = pl.multiple_of(j * slots, slots)
        row_at = [
            rows_smem.at[pl.ds(i, (owners - 1) * slots + 1)][start] for i in range(slots)
        ]
        pieces = []
        for g in range(slots // 4):
            pair = []
            for h in range(2):
                s = 4 * g + 2 * h
                first = res_sc[pl.ds(row_at[s] + 8, 8), :]
                second = res_sc[pl.ds(row_at[s + 1] + 4, 8), :]
                pair.append(jnp.where(half, first, second))
            pieces.append(jnp.concatenate(pair, axis=0).astype(BF16))
        taps = jnp.concatenate(pieces, axis=0)
        row = row_sc[pl.ds(j, 1), :]
        cod = code_sc[pl.ds(j, 1), :]
        wgt = wi_sc[pl.ds(j, 1), :]
        visit = jnp.floor(row * (1.0 / rows))
        y = coord(row - visit * rows, ccd, rows, ccd_devs)
        ty = cheb_rows(jnp.broadcast_to(y, (ORDER, wide)), ORDER)
        ty = ty * jnp.where(cod < float(P_DEV), wgt, 0.0)
        lhs = [jnp.where(cod == kid, wgt, 0.0)]
        for v in range(vis):
            lhs.append(jnp.where(visit == float(v), ty, 0.0))
        lhs = jnp.concatenate(lhs, axis=0).astype(BF16)
        sums = dot(lhs, taps)
        t_ref[pl.ds(pl.multiple_of(j * P_DEV, P_DEV), P_DEV), :] = sums[:P_DEV]
        q_sc[...] += sums[P_DEV:]
        return acc + design(j)

    sy = lax.fori_loop(0, owners, body, jnp.zeros((4 * ORDER, n), F32), unroll=UNROLL)
    sy = sy[:ORDER] + sy[ORDER : 2 * ORDER] + sy[2 * ORDER : 3 * ORDER]
    sy_ref[...] = widen(sy)
    m_hi, m_lo = split(m_sc[...], 2)
    mtw_ref[...] = jnp.concatenate(split(m_sc[...].T[:n], 2), axis=0)
    m_hi, m_lo = m_hi.astype(F32), m_lo.astype(F32)
    wide_m = m_hi + pltpu.roll(m_hi, n, 1) + pltpu.roll(m_lo, 2 * n, 1)
    mw_ref[...] = wide_m.astype(BF16)
    full = dot_t(q_sc[...], tile_rows(const_ref[CXT], vis), HI)
    qb_ref[...] = widen(blocks_of(full, vis))


def tile_rows(x, times):
    return jnp.concatenate([x] * times, axis=0)


def blocks_of(full, vis):
    lane = iota((ORDER, full.shape[1]), 1) // ORDER
    out = jnp.zeros((ORDER, full.shape[1]), F32)
    for v in range(vis):
        out = out + jnp.where(lane == v, full[v * ORDER : (v + 1) * ORDER], 0.0)
    return out


def widen(x):
    return jnp.concatenate([x, jnp.zeros((x.shape[0], 128 - x.shape[1]), F32)], axis=1)


def pack(x):
    turned = [x] + [pltpu.roll(x, 32 * g, 1) for g in range(1, 4)]
    out = []
    for r in range(ORDER // 4):
        row = turned[0][4 * r : 4 * r + 1]
        for g in range(1, 4):
            row = row + turned[g][4 * r + g : 4 * r + g + 1]
        out.append(row)
    return out


def unpack(x):
    out = []
    for row in x:
        row = jnp.broadcast_to(row, (ORDER, 128))
        out.append(row[0:1])
        for g in range(1, 4):
            out.append(pltpu.roll(row, 128 - 32 * g, 1)[0:1])
    return out


def stack(rows):
    sub = iota((8, 128), 0)
    out = jnp.broadcast_to(rows[0], (8, 128))
    for i in range(1, len(rows)):
        out = jnp.where(sub == i, rows[i], out)
    return out


def moments_block(mtw_ref, back, q):
    n = mtw_ref.shape[0] // 2
    vis = n // ORDER
    b_hi, b_lo = split(back, 2)
    b_hi, b_lo = (tile_rows(x.astype(F32), vis).astype(BF16) for x in (b_hi, b_lo))
    full = dot_t(mtw_ref[...], b_hi)
    full = full[:n] + full[n:] + dot_t(mtw_ref[0:n], b_lo)
    return q - widen(blocks_of(full, vis))


def senders_sum(ref, lo, hi):
    total = ref[0, lo:hi].astype(F32)
    for i in range(1, ref.shape[0]):
        total = total + ref[i, lo:hi].astype(F32)
    return total


def first_kernel(arr_ref, mtw_ref, qb_ref, sy_ref, b_ref, den_ref, pay_ref):
    blocks = b_ref.shape[1] // 128
    total = senders_sum(arr_ref, 0, arr_ref.shape[1])
    back, dens = [], []
    for q in range(blocks):
        den = total[ORDER * blocks + q : ORDER * blocks + q + 1] + 1.0
        dens.append(jnp.broadcast_to(den, (ORDER, 128)))
        back.append(total[ORDER * q : ORDER * (q + 1)] / dens[-1])
    back = jnp.concatenate(back, axis=1)
    den_ref[...] = jnp.concatenate(dens, axis=1)
    b_ref[...] = back
    mom = moments_block(mtw_ref, back, qb_ref[...])
    block = stack(pack(mom) + pack(sy_ref[...]))[: pay_ref.shape[1]]
    for i in range(pay_ref.shape[0]):
        pay_ref[i] = block


def systems(sy, lam, vis):
    sub = iota((ORDER, 128), 0)
    base = iota((ORDER, 128), 1) // ORDER * ORDER
    return [
        jnp.take_along_axis(sy, base + b, axis=1, mode="promise_in_bounds") * lam
        + jnp.where(sub == b, RIDGE, 0.0)
        for b in range(ORDER)
    ]


def eliminate(mat, rhs):
    mat, rhs = list(mat), list(rhs)
    for p in range(ORDER):
        inv = 1.0 / mat[p][p : p + 1]
        mat[p] = mat[p] * inv
        rhs[p] = rhs[p] * inv
        for b in range(ORDER):
            if b != p:
                factor = mat[b][p : p + 1]
                mat[b] = mat[b] - factor * mat[p]
                rhs[b] = rhs[b] - factor * rhs[p]
    return rhs


def solve(mom, sy, lam, vis):
    out = stack(eliminate(systems(sy, lam, vis), mom))
    return jnp.where(iota((ORDER, 128), 1) < vis * ORDER, out, 0.0)


def block_diag(z, vis):
    n = vis * ORDER
    keep = iota((n, 128), 0) // ORDER == iota((n, 128), 1) // ORDER
    return jnp.where(keep, tile_rows(z, vis), 0.0)


def model_kernel(arr_ref, const_ref, mtw_ref, mw_ref, t_ref, sy_ref, pay_ref):
    vis = mtw_ref.shape[0] // (2 * ORDER)
    n = vis * ORDER
    total = arr_ref[0]
    for i in range(1, arr_ref.shape[0]):
        total = total + arr_ref[i]
    rows = ORDER // 4
    sy = stack(unpack([total[i : i + 1] for i in range(rows, 2 * rows)]))
    sy_ref[...] = sy
    mom = unpack([total[i : i + 1] for i in range(rows)])
    z = solve(mom, sy, const_ref[LAM_LANE], vis)
    square = block_diag(z, vis)
    diag = square.T[:n]
    weights = diag[:ORDER]
    for v in range(1, vis):
        weights = weights + diag[v * ORDER : (v + 1) * ORDER]
    w_hi, w_lo = split(weights, 2)
    model = (
        dot(w_hi, mtw_ref[0:n]) + dot(w_lo, mtw_ref[0:n]) + dot(w_hi, mtw_ref[n : 2 * n])
    )
    z_hi, z_lo = split(square, 2)
    c_hi, c_lo = split(tile_rows(const_ref[CXT], 128 // ORDER), 2)
    surface = dot(jnp.concatenate([z_hi, z_lo], axis=0), c_hi)
    surface = surface[:n] + surface[n:] + dot(z_hi, c_lo)
    s_hi, s_lo = split(surface, 2)
    surface = jnp.concatenate([s_hi, s_lo, s_hi, jnp.zeros((128 - 3 * n, 128), BF16)], axis=0)
    corrected = t_ref[...] - dot(mw_ref[...], surface)
    blocks = model.shape[1] // 128
    block = jnp.concatenate(
        [model[:, 128 * q : 128 * (q + 1)] for q in range(blocks)], axis=0
    ).astype(BF16)
    rows = ORDER * blocks
    for i in range(pay_ref.shape[0]):
        pay_ref[i, 0:rows] = block
        pay_ref[i, rows : rows + P_DEV] = corrected[P_DEV * i : P_DEV * (i + 1)].astype(BF16)


def second_kernel(arr_ref, b_ref, den_ref, mtw_ref, qb_ref, const_ref, pay_ref, lam_ref):
    blocks = b_ref.shape[1] // 128
    total = senders_sum(arr_ref, 0, ORDER * blocks)
    model = jnp.concatenate(
        [total[ORDER * q : ORDER * (q + 1)] for q in range(blocks)], axis=1
    )
    lam = const_ref[LAM_SUB][:, 0:1]
    mom = moments_block(mtw_ref, b_ref[...] - lam * model / den_ref[...], qb_ref[...])
    lam_ref[...] = const_ref[LAM_LANE]
    block = stack(pack(mom))[: pay_ref.shape[1]]
    for i in range(pay_ref.shape[0]):
        pay_ref[i] = block


def final_kernel(
    arr_ref, sums_ref, den_ref, sy_ref, const_ref, lam_ref, out_ref, back_ref
):
    vis = out_ref.shape[0]
    n = vis * ORDER
    total = arr_ref[0]
    for i in range(1, arr_ref.shape[0]):
        total = total + arr_ref[i]
    mom = unpack([total[i : i + 1] for i in range(ORDER // 4)])
    z = solve(mom, sy_ref[...], lam_ref[...], vis)
    flat = tile_rows(z, ORDER).T[:n] * tile_rows(const_ref[ROT][:, : ORDER * ORDER], vis)
    for v in range(vis):
        out_ref[v : v + 1] = jnp.sum(flat[v * ORDER : (v + 1) * ORDER], axis=0, keepdims=True)
    rows = sums_ref.shape[1] - P_DEV
    sums = senders_sum(sums_ref, rows, rows + P_DEV)
    own = lax.axis_index("visit") * P_DEV
    width = den_ref.shape[1]
    pick = iota((P_DEV, width), 1) == iota((P_DEV, width), 0) + own
    d_hi, d_lo = split(den_ref[...], 2)
    pick = jnp.where(pick, 1.0, 0.0).astype(BF16)
    den = dot_t(pick, d_hi) + dot_t(pick, d_lo)
    back_ref[...] = sums / den[:, 0:1]


def call(kernel, out_shape, scratch=(), n_in=1, hbm=(), smem=()):
    spec = {i: HBM for i in hbm} | {i: SMEM for i in smem}
    fn = pl.pallas_call(
        kernel,
        out_shape=out_shape,
        in_specs=[spec.get(i, VMEM) for i in range(n_in)],
        out_specs=jax.tree.map(lambda _: VMEM, out_shape),
        scratch_shapes=list(scratch),
    )

    def run(*args):
        return fn(
            *(
                x if i in spec else pltpu.with_memory_space_constraint(x, pltpu.VMEM)
                for i, x in enumerate(args)
            )
        )

    return run


def shape(dims, dtype=F32):
    return pltpu.VMEM(dims, dtype)


def result(dims, dtype=F32):
    return jax.ShapeDtypeStruct(dims, dtype)


def exchange(x, axis):
    return lax.all_to_all(x, axis, split_axis=0, concat_axis=0, tiled=True)


def per_device(raw_rows, resample, slot_row, tap_weight, patch_id, live_mask):
    owners = lax.axis_size("visit")
    ccd_devs = lax.axis_size("ccd")
    vis, rows, pix = raw_rows.shape
    slots = slot_row.shape[3]
    patches = owners * P_DEV
    blocks = patches // 128
    nvb = vis * ORDER
    lam, rot, cxt = constants(pix)
    const = np.zeros((32, 128))
    const[CXT] = cxt
    const[LAM_LANE, :nvb] = np.tile(lam, vis)
    const[LAM_SUB] = lam[:, None]
    const[ROT, : ORDER * ORDER] = np.repeat(rot.T, ORDER, axis=1)
    const = jnp.asarray(const, F32)
    srow, pid, live = slot_row[0, 0], patch_id[0, 0], live_mask[0, 0]
    weights = tap_weight[:, 0, 0]
    pay_rows = ORDER * blocks + P_DEV

    ints = shape((owners, slots), jnp.int32)
    pay1, srow_v, raw_v, res_v, w_v, pid_v, live_v, const = call(
        project_kernel,
        (
            shape((owners, ORDER * blocks + 8, 128), BF16),
            ints,
            shape(raw_rows.shape, BF16),
            shape(resample.shape, BF16),
            shape((TAPS, owners, slots)),
            ints,
            ints,
            shape(const.shape),
        ),
        scratch=(
            pltpu.VMEM((owners, slots), F32),
            pltpu.VMEM((owners, slots), F32),
            pltpu.VMEM((owners, slots), F32),
            pltpu.VMEM((owners // 2, 256, slots), BF16),
            pltpu.VMEM((owners // 2, 128, slots), BF16),
            pltpu.VMEM((blocks, 4 * ORDER, 128), F32),
            pltpu.SemaphoreType.DMA((6 + vis,)),
        ),
        n_in=7,
        hbm=range(7),
    )(srow, raw_rows, resample, weights, pid, live, const)
    arr1 = exchange(pay1, "visit")
    tsum, qb, sy, mw, mtw = call(
        functools.partial(gather_kernel, ccd_devs),
        (
            shape((patches, pix)),
            shape((ORDER, 128)),
            shape((ORDER, 128)),
            shape((patches, 128), BF16),
            shape((2 * nvb, patches), BF16),
        ),
        scratch=(
            pltpu.VMEM((vis * rows + 16, pix), F32),
            pltpu.VMEM((owners, slots * TAPS), F32),
            pltpu.VMEM((owners, slots * TAPS), F32),
            pltpu.VMEM((owners, slots * TAPS), F32),
            pltpu.VMEM((nvb, pix), F32),
            pltpu.VMEM((patches, 128), F32),
        ),
        n_in=8,
        smem=(0,),
    )(srow.reshape(-1), raw_v, res_v, srow_v, w_v, pid_v, live_v, const)
    back, den, pay2 = call(
        first_kernel,
        (
            shape((ORDER, patches)),
            shape((ORDER, patches)),
            shape((ccd_devs, ORDER // 2, 128)),
        ),
        n_in=4,
    )(arr1, mtw, qb, sy)
    arr2 = exchange(pay2, "ccd")
    sy_all, pay3 = call(
        model_kernel,
        (shape((ORDER, 128)), shape((owners, pay_rows, 128), BF16)),
        n_in=5,
    )(arr2, const, mtw, mw, tsum)
    arr3 = exchange(pay3, "visit")
    pay4, lam = call(
        second_kernel, (shape((ccd_devs, ORDER // 4, 128)), shape((ORDER, 128))), n_in=6
    )(
        arr3, back, den, mtw, qb, const
    )
    arr4 = exchange(pay4, "ccd")
    offsets, background = call(
        final_kernel, (result((vis, ORDER * ORDER)), result((P_DEV, pix))), n_in=6
    )(arr4, arr3, den, sy_all, const, lam)
    return offsets, background


def solution(mesh):
    in_specs = (
        P("visit", "ccd", None),
        P("visit", None, None),
        P("visit", "ccd", None, None),
        P(None, "visit", "ccd", None, None),
        P("visit", "ccd", None, None),
        P("visit", "ccd", None, None),
    )
    out_specs = (P("visit", None), P(("visit", "ccd"), None))
    return jax.shard_map(
        per_device, mesh=mesh, in_specs=in_specs, out_specs=out_specs, check_vma=False
    )
```

```python
import functools

import jax
import jax.numpy as jnp
import numpy as np
from jax import lax
from jax.experimental import pallas as pl
from jax.experimental.pallas import tpu as pltpu
from jax.sharding import PartitionSpec as P

ORDER = 8
TAPS = 4
P_DEV = 16
RIDGE = 1.0
UNROLL = 8
UNROLL_W = 2
CXT, LAM_LANE, LAM_SUB, ROT = (slice(8 * i, 8 * (i + 1)) for i in range(4))
HI = lax.Precision.HIGHEST
F32 = jnp.float32
BF16 = jnp.bfloat16
VMEM = pl.BlockSpec(memory_space=pltpu.VMEM)
HBM = pl.BlockSpec(memory_space=pl.ANY)
SMEM = pl.BlockSpec(memory_space=pltpu.SMEM)


def constants(pixels):
    x = (2 * np.arange(pixels) + 1) / pixels - 1.0
    cx = [np.ones_like(x), x]
    for _ in range(2, ORDER):
        cx.append(2 * x * cx[-1] - cx[-2])
    cx = np.stack(cx)
    lam, rot = np.linalg.eigh(cx @ cx.T)
    return lam, rot, rot.T @ cx


def dot(a, b, precision=None):
    return lax.dot_general(
        a, b, (((1,), (0,)), ((), ())), precision=precision, preferred_element_type=F32
    )


def dot_t(a, b, precision=None):
    return lax.dot_general(
        a, b, (((1,), (1,)), ((), ())), precision=precision, preferred_element_type=F32
    )


def split(x, parts):
    out = []
    for _ in range(parts):
        out.append(x.astype(BF16))
        x = x - out[-1].astype(F32)
    return out


def iota(shape, dim):
    return lax.broadcasted_iota(jnp.int32, shape, dim)


def cheb_rows(y, count):
    sub = iota(y.shape, 0)
    prev, cur = jnp.ones_like(y), y
    out = jnp.where(sub == 0, prev, cur)
    for k in range(2, count):
        prev, cur = cur, 2.0 * y * cur - prev
        out = jnp.where(sub == k, cur, out)
    return out


def coord(b_pos, ccd, rows_local, ccd_devs):
    base = (ccd * rows_local).astype(F32)
    return (2.0 * (base + b_pos) + float(TAPS)) / float(rows_local * ccd_devs) - 1.0


def project_kernel(
    srow_hbm, raw_hbm, res_hbm, w_hbm, pid_hbm, live_hbm, const_hbm,
    pay_ref, srow_ref, raw_ref, res_ref, w_ref, pid_ref, live_ref, const_ref,
    hi_sc, lo_sc, code_sc, hot_sc, member_sc, acc_sc, sems,
):
    vis, rows, pix = raw_ref.shape
    owners, slots = srow_ref.shape
    blocks = owners * P_DEV // 128
    group = owners // blocks
    small = (
        (srow_hbm, srow_ref), (w_hbm, w_ref), (pid_hbm, pid_ref), (live_hbm, live_ref),
        (const_hbm, const_ref), (res_hbm, res_ref),
    )
    copies = [pltpu.make_async_copy(a, b, sems.at[n]) for n, (a, b) in enumerate(small)]
    raw_copies = [
        pltpu.make_async_copy(raw_hbm.at[v], raw_ref.at[v], sems.at[len(small) + v])
        for v in range(vis)
    ]
    for copy in copies + raw_copies:
        copy.start()
    for copy in copies:
        copy.wait()
    wide = 256
    span = wide - TAPS + 1
    srow = srow_ref[...].astype(F32)
    high = jnp.floor((srow + 0.5) * (1.0 / span))
    hi_sc[...] = high
    lo_sc[...] = srow - span * high
    place = P_DEV * (iota((owners, slots), 0) % group) + pid_ref[...]
    code_sc[...] = jnp.where(live_ref[...] > 0, place, -1).astype(F32)
    c_parts = jnp.concatenate(split(const_ref[CXT], 2), axis=0)
    kernels = []
    for v in range(vis):
        both = dot_t(c_parts, res_ref[v])
        kernels.append(jnp.concatenate(split(both[:ORDER] + both[ORDER:], 2), axis=0))
    rid = iota((wide, slots), 0).astype(F32).astype(BF16)
    ids = rid[:128]
    unit = jnp.ones((128, slots), BF16)
    def operands(j):
        low = lo_sc[pl.ds(j, 1), :]
        one = jnp.zeros((wide, slots), BF16)
        for t in range(TAPS):
            hit = rid == (low + float(t)).astype(BF16)
            one = jnp.where(hit, w_ref[t, pl.ds(j, 1), :].astype(BF16), one)
        code = code_sc[pl.ds(j, 1), :].astype(BF16)
        return one, jnp.where(ids == code, unit, jnp.zeros_like(unit))

    def build(j, carry):
        hot_sc[j], member_sc[j] = operands(j)
        return carry

    early = blocks // 4
    lax.fori_loop(0, early * group, build, 0, unroll=UNROLL_W)
    for copy in raw_copies:
        copy.wait()
    pieces = []
    for v in range(vis):
        both = dot_t(kernels[v], raw_ref[v])
        pieces.append(both[:ORDER] + both[ORDER:])
    table = jnp.concatenate(pieces, axis=1)
    tiles = vis * rows // 128
    lane = iota((ORDER, 128), 1)

    def window(start):
        first, shift = start // 128, start % 128
        a, b = (
            table[:, 128 * t : 128 * (t + 1)]
            for t in (min(first, tiles - 1), min(first + 1, tiles - 1))
        )
        if not shift:
            return a
        a, b = pltpu.roll(a, 128 - shift, 1), pltpu.roll(b, 128 - shift, 1)
        return jnp.where(lane < 128 - shift, a, b)

    windows = []
    for k in range(-(-(vis * rows - TAPS + 1) // span)):
        parts = [window(span * k + c) for c in range(0, wide, 128)]
        windows.append(jnp.concatenate(parts, axis=1))
    if len(windows) % 2:
        windows.append(jnp.zeros((ORDER, wide), F32))
    left = jnp.concatenate(windows, axis=0).astype(BF16)
    ones = jnp.ones((ORDER, slots), BF16)

    def pair_sums(m, made):
        both = [2 * m, 2 * m + 1]
        pairs = [(hot_sc[j], member_sc[j]) if made else operands(j) for j in both]
        vals = dot(left, jnp.concatenate([p[0] for p in pairs], axis=1))
        left_sums = []
        for h, j in enumerate(both):
            high = jnp.broadcast_to(hi_sc[pl.ds(j, 1), :], (ORDER, slots))
            got = jnp.zeros((ORDER, slots), F32)
            for k in range(len(windows)):
                part = vals[ORDER * k : ORDER * (k + 1), slots * h : slots * (h + 1)]
                got = jnp.where(high == float(k), part, got)
            left_sums.append(jnp.concatenate(split(got, 2) + [ones, ones], axis=0))
        members = jnp.concatenate([p[1] for p in pairs], axis=1)
        return dot_t(jnp.concatenate(left_sums, axis=1), members)

    def body(made, q, carry):
        pairs = group // 2
        total = pair_sums(q * pairs, made)
        for m in range(1, pairs):
            total = total + pair_sums(q * pairs + m, made)
        acc_sc[q] = total
        return carry

    lax.fori_loop(0, early, functools.partial(body, True), 0, unroll=True)
    lax.fori_loop(early, blocks, functools.partial(body, False), 0, unroll=True)
    sub = iota((8, 128), 0)
    tail = jnp.zeros((8, 128), F32)
    rows_out = []
    for q in range(blocks):
        rows_out.append(acc_sc[q, 0:ORDER] + acc_sc[q, ORDER : 2 * ORDER])
        tail = jnp.where(sub == q, acc_sc[q, 2 * ORDER : 3 * ORDER], tail)
    block = jnp.concatenate(rows_out + [tail], axis=0).astype(BF16)
    for i in range(owners):
        pay_ref[i] = block


def gather_kernel(
    ccd_devs, rows_smem, raw_ref, res_ref, srow_ref, w_ref, pid_ref, live_ref, const_ref,
    t_ref, qb_ref, sy_ref, mw_ref, mtw_ref,
    res_sc, row_sc, code_sc, wi_sc, q_sc, m_sc,
):
    vis, rows, pix = raw_ref.shape
    owners, slots = srow_ref.shape
    wide = slots * TAPS
    n = vis * ORDER
    ccd = lax.axis_index("ccd")
    off = iota((slots, wide), 1) - TAPS * iota((slots, wide), 0)
    rep = jnp.where((off >= 0) & (off < TAPS), 1.0, 0.0).astype(BF16)
    srow = srow_ref[...]
    code = pid_ref[...] + P_DEV * (1 - live_ref[...])
    high, low = srow >> 8, srow & 255
    whole = jnp.concatenate([high, low, code], axis=0).astype(F32).astype(BF16)
    whole = dot(whole, rep)
    row_sc[...] = 256.0 * whole[:owners] + whole[owners : 2 * owners]
    code_sc[...] = whole[2 * owners :]
    wi = None
    for t in range(TAPS):
        pick = jnp.where(off == t, 1.0, 0.0).astype(BF16)
        part = dot(w_ref[t].astype(BF16), pick)
        wi = part if wi is None else wi + part
    wi_sc[...] = wi
    q_sc[...] = jnp.zeros_like(q_sc)
    m_sc[...] = jnp.zeros_like(m_sc)
    half = iota((8, pix), 0) < TAPS
    kid = iota((P_DEV, wide), 0).astype(F32)
    kid_s = iota((P_DEV, slots), 0)
    zero = jnp.zeros((pix, pix), BF16)
    for v in range(0, vis, 2):
        pair = jnp.concatenate([raw_ref[v], raw_ref[v + 1]], axis=1)
        diag = jnp.concatenate(
            [
                jnp.concatenate([res_ref[v], zero], axis=1),
                jnp.concatenate([zero, res_ref[v + 1]], axis=1),
            ],
            axis=0,
        )
        both = dot(pair, diag)
        res_sc[pl.ds(8 + v * rows, rows), :] = both[:, :pix]
        res_sc[pl.ds(8 + (v + 1) * rows, rows), :] = both[:, pix:]

    def design(j):
        srow = srow_ref[pl.ds(j, 1), :]
        live = live_ref[pl.ds(j, 1), :]
        pid = pid_ref[pl.ds(j, 1), :]
        visit = srow // rows
        y = coord((srow - visit * rows).astype(F32), ccd, rows, ccd_devs)
        ty = cheb_rows(jnp.broadcast_to(y, (ORDER, slots)), ORDER)
        member = jnp.where((pid == kid_s) & (live > 0), 1.0, 0.0).astype(BF16)
        vt = jnp.concatenate(
            [jnp.where((visit == v) & (live > 0), ty, 0.0) for v in range(vis)], axis=0
        )
        parts = jnp.concatenate([p.astype(F32) for p in split(ty, 3)] + [jnp.zeros_like(ty)], axis=0)
        left = jnp.concatenate([member, parts.astype(BF16)], axis=0)
        both = None
        for piece in split(vt, 3):
            part = dot_t(left, piece)
            both = part if both is None else both + part
        m_sc[pl.ds(pl.multiple_of(j * P_DEV, P_DEV), P_DEV), 0:n] = both[:P_DEV]
        return both[P_DEV:]

    def body(j, acc):
        start = pl.multiple_of(j * slots, slots)
        row_at = [
            rows_smem.at[pl.ds(i, (owners - 1) * slots + 1)][start] for i in range(slots)
        ]
        pieces = []
        for g in range(slots // 4):
            pair = []
            for h in range(2):
                s = 4 * g + 2 * h
                first = res_sc[pl.ds(row_at[s] + 8, 8), :]
                second = res_sc[pl.ds(row_at[s + 1] + 4, 8), :]
                pair.append(jnp.where(half, first, second))
            pieces.append(jnp.concatenate(pair, axis=0).astype(BF16))
        taps = jnp.concatenate(pieces, axis=0)
        row = row_sc[pl.ds(j, 1), :]
        cod = code_sc[pl.ds(j, 1), :]
        wgt = wi_sc[pl.ds(j, 1), :]
        visit = jnp.floor(row * (1.0 / rows))
        y = coord(row - visit * rows, ccd, rows, ccd_devs)
        ty = cheb_rows(jnp.broadcast_to(y, (ORDER, wide)), ORDER)
        ty = ty * jnp.where(cod < float(P_DEV), wgt, 0.0)
        lhs = [jnp.where(cod == kid, wgt, 0.0)]
        for v in range(vis):
            lhs.append(jnp.where(visit == float(v), ty, 0.0))
        lhs = jnp.concatenate(lhs, axis=0).astype(BF16)
        sums = dot(lhs, taps)
        t_ref[pl.ds(pl.multiple_of(j * P_DEV, P_DEV), P_DEV), :] = sums[:P_DEV]
        q_sc[...] += sums[P_DEV:]
        return acc + design(j)

    sy = lax.fori_loop(0, owners, body, jnp.zeros((4 * ORDER, n), F32), unroll=UNROLL)
    sy = sy[:ORDER] + sy[ORDER : 2 * ORDER] + sy[2 * ORDER : 3 * ORDER]
    sy_ref[...] = widen(sy)
    m_hi, m_lo = split(m_sc[...], 2)
    mtw_ref[...] = jnp.concatenate(split(m_sc[...].T[:n], 2), axis=0)
    m_hi, m_lo = m_hi.astype(F32), m_lo.astype(F32)
    wide_m = m_hi + pltpu.roll(m_hi, n, 1) + pltpu.roll(m_lo, 2 * n, 1)
    mw_ref[...] = wide_m.astype(BF16)
    full = dot_t(q_sc[...], tile_rows(const_ref[CXT], vis), HI)
    qb_ref[...] = widen(blocks_of(full, vis))


def tile_rows(x, times):
    return jnp.concatenate([x] * times, axis=0)


def blocks_of(full, vis):
    lane = iota((ORDER, full.shape[1]), 1) // ORDER
    out = jnp.zeros((ORDER, full.shape[1]), F32)
    for v in range(vis):
        out = out + jnp.where(lane == v, full[v * ORDER : (v + 1) * ORDER], 0.0)
    return out


def widen(x):
    return jnp.concatenate([x, jnp.zeros((x.shape[0], 128 - x.shape[1]), F32)], axis=1)


def pack(x):
    turned = [x] + [pltpu.roll(x, 32 * g, 1) for g in range(1, 4)]
    out = []
    for r in range(ORDER // 4):
        row = turned[0][4 * r : 4 * r + 1]
        for g in range(1, 4):
            row = row + turned[g][4 * r + g : 4 * r + g + 1]
        out.append(row)
    return out


def unpack(x):
    out = []
    for row in x:
        row = jnp.broadcast_to(row, (ORDER, 128))
        out.append(row[0:1])
        for g in range(1, 4):
            out.append(pltpu.roll(row, 128 - 32 * g, 1)[0:1])
    return out


def stack(rows):
    sub = iota((8, 128), 0)
    out = jnp.broadcast_to(rows[0], (8, 128))
    for i in range(1, len(rows)):
        out = jnp.where(sub == i, rows[i], out)
    return out


def moments_block(mtw_ref, back, q):
    n = mtw_ref.shape[0] // 2
    vis = n // ORDER
    b_hi, b_lo = split(back, 2)
    b_hi, b_lo = (tile_rows(x.astype(F32), vis).astype(BF16) for x in (b_hi, b_lo))
    full = dot_t(mtw_ref[...], b_hi)
    full = full[:n] + full[n:] + dot_t(mtw_ref[0:n], b_lo)
    return q - widen(blocks_of(full, vis))


def senders_sum(ref, lo, hi):
    total = ref[0, lo:hi].astype(F32)
    for i in range(1, ref.shape[0]):
        total = total + ref[i, lo:hi].astype(F32)
    return total


def first_kernel(arr_ref, mtw_ref, qb_ref, sy_ref, b_ref, den_ref, pay_ref):
    blocks = b_ref.shape[1] // 128
    total = senders_sum(arr_ref, 0, arr_ref.shape[1])
    back, dens = [], []
    for q in range(blocks):
        den = total[ORDER * blocks + q : ORDER * blocks + q + 1] + 1.0
        dens.append(jnp.broadcast_to(den, (ORDER, 128)))
        back.append(total[ORDER * q : ORDER * (q + 1)] / dens[-1])
    back = jnp.concatenate(back, axis=1)
    den_ref[...] = jnp.concatenate(dens, axis=1)
    b_ref[...] = back
    mom = moments_block(mtw_ref, back, qb_ref[...])
    block = stack(pack(mom) + pack(sy_ref[...]))[: pay_ref.shape[1]]
    for i in range(pay_ref.shape[0]):
        pay_ref[i] = block


def systems(sy, lam, vis):
    sub = iota((ORDER, 128), 0)
    base = iota((ORDER, 128), 1) // ORDER * ORDER
    return [
        jnp.take_along_axis(sy, base + b, axis=1, mode="promise_in_bounds") * lam
        + jnp.where(sub == b, RIDGE, 0.0)
        for b in range(ORDER)
    ]


def eliminate(mat, rhs):
    mat, rhs = list(mat), list(rhs)
    for p in range(ORDER):
        inv = 1.0 / mat[p][p : p + 1]
        mat[p] = mat[p] * inv
        rhs[p] = rhs[p] * inv
        for b in range(ORDER):
            if b != p:
                factor = mat[b][p : p + 1]
                mat[b] = mat[b] - factor * mat[p]
                rhs[b] = rhs[b] - factor * rhs[p]
    return rhs


def solve(mom, sy, lam, vis):
    out = stack(eliminate(systems(sy, lam, vis), mom))
    return jnp.where(iota((ORDER, 128), 1) < vis * ORDER, out, 0.0)


def block_diag(z, vis):
    n = vis * ORDER
    keep = iota((n, 128), 0) // ORDER == iota((n, 128), 1) // ORDER
    return jnp.where(keep, tile_rows(z, vis), 0.0)


def model_kernel(arr_ref, const_ref, mtw_ref, mw_ref, t_ref, sy_ref, pay_ref):
    vis = mtw_ref.shape[0] // (2 * ORDER)
    n = vis * ORDER
    total = arr_ref[0]
    for i in range(1, arr_ref.shape[0]):
        total = total + arr_ref[i]
    rows = ORDER // 4
    sy = stack(unpack([total[i : i + 1] for i in range(rows, 2 * rows)]))
    sy_ref[...] = sy
    mom = unpack([total[i : i + 1] for i in range(rows)])
    z = solve(mom, sy, const_ref[LAM_LANE], vis)
    square = block_diag(z, vis)
    diag = square.T[:n]
    weights = diag[:ORDER]
    for v in range(1, vis):
        weights = weights + diag[v * ORDER : (v + 1) * ORDER]
    w_hi, w_lo = split(weights, 2)
    model = (
        dot(w_hi, mtw_ref[0:n]) + dot(w_lo, mtw_ref[0:n]) + dot(w_hi, mtw_ref[n : 2 * n])
    )
    z_hi, z_lo = split(square, 2)
    c_hi, c_lo = split(tile_rows(const_ref[CXT], 128 // ORDER), 2)
    surface = dot(jnp.concatenate([z_hi, z_lo], axis=0), c_hi)
    surface = surface[:n] + surface[n:] + dot(z_hi, c_lo)
    s_hi, s_lo = split(surface, 2)
    surface = jnp.concatenate([s_hi, s_lo, s_hi, jnp.zeros((128 - 3 * n, 128), BF16)], axis=0)
    corrected = t_ref[...] - dot(mw_ref[...], surface)
    blocks = model.shape[1] // 128
    block = jnp.concatenate(
        [model[:, 128 * q : 128 * (q + 1)] for q in range(blocks)], axis=0
    ).astype(BF16)
    rows = ORDER * blocks
    for i in range(pay_ref.shape[0]):
        pay_ref[i, 0:rows] = block
        pay_ref[i, rows : rows + P_DEV] = corrected[P_DEV * i : P_DEV * (i + 1)].astype(BF16)


def second_kernel(arr_ref, b_ref, den_ref, mtw_ref, qb_ref, const_ref, pay_ref, lam_ref):
    blocks = b_ref.shape[1] // 128
    total = senders_sum(arr_ref, 0, ORDER * blocks)
    model = jnp.concatenate(
        [total[ORDER * q : ORDER * (q + 1)] for q in range(blocks)], axis=1
    )
    lam = const_ref[LAM_SUB][:, 0:1]
    mom = moments_block(mtw_ref, b_ref[...] - lam * model / den_ref[...], qb_ref[...])
    lam_ref[...] = const_ref[LAM_LANE]
    block = stack(pack(mom))[: pay_ref.shape[1]]
    for i in range(pay_ref.shape[0]):
        pay_ref[i] = block


def final_kernel(
    arr_ref, sums_ref, den_ref, sy_ref, const_ref, lam_ref, out_ref, back_ref
):
    vis = out_ref.shape[0]
    n = vis * ORDER
    total = arr_ref[0]
    for i in range(1, arr_ref.shape[0]):
        total = total + arr_ref[i]
    mom = unpack([total[i : i + 1] for i in range(ORDER // 4)])
    z = solve(mom, sy_ref[...], lam_ref[...], vis)
    flat = tile_rows(z, ORDER).T[:n] * tile_rows(const_ref[ROT][:, : ORDER * ORDER], vis)
    for v in range(vis):
        out_ref[v : v + 1] = jnp.sum(flat[v * ORDER : (v + 1) * ORDER], axis=0, keepdims=True)
    rows = sums_ref.shape[1] - P_DEV
    sums = senders_sum(sums_ref, rows, rows + P_DEV)
    own = lax.axis_index("visit") * P_DEV
    width = den_ref.shape[1]
    pick = iota((P_DEV, width), 1) == iota((P_DEV, width), 0) + own
    d_hi, d_lo = split(den_ref[...], 2)
    pick = jnp.where(pick, 1.0, 0.0).astype(BF16)
    den = dot_t(pick, d_hi) + dot_t(pick, d_lo)
    back_ref[...] = sums / den[:, 0:1]


def call(kernel, out_shape, scratch=(), n_in=1, hbm=(), smem=()):
    spec = {i: HBM for i in hbm} | {i: SMEM for i in smem}
    fn = pl.pallas_call(
        kernel,
        out_shape=out_shape,
        in_specs=[spec.get(i, VMEM) for i in range(n_in)],
        out_specs=jax.tree.map(lambda _: VMEM, out_shape),
        scratch_shapes=list(scratch),
    )

    def run(*args):
        return fn(
            *(
                x if i in spec else pltpu.with_memory_space_constraint(x, pltpu.VMEM)
                for i, x in enumerate(args)
            )
        )

    return run


def shape(dims, dtype=F32):
    return pltpu.VMEM(dims, dtype)


def result(dims, dtype=F32):
    return jax.ShapeDtypeStruct(dims, dtype)


def exchange(x, axis):
    return lax.all_to_all(x, axis, split_axis=0, concat_axis=0, tiled=True)


def per_device(raw_rows, resample, slot_row, tap_weight, patch_id, live_mask):
    owners = lax.axis_size("visit")
    ccd_devs = lax.axis_size("ccd")
    vis, rows, pix = raw_rows.shape
    slots = slot_row.shape[3]
    patches = owners * P_DEV
    blocks = patches // 128
    nvb = vis * ORDER
    lam, rot, cxt = constants(pix)
    const = np.zeros((32, 128))
    const[CXT] = cxt
    const[LAM_LANE, :nvb] = np.tile(lam, vis)
    const[LAM_SUB] = lam[:, None]
    const[ROT, : ORDER * ORDER] = np.repeat(rot.T, ORDER, axis=1)
    const = jnp.asarray(const, F32)
    srow, pid, live = slot_row[0, 0], patch_id[0, 0], live_mask[0, 0]
    weights = tap_weight[:, 0, 0]
    pay_rows = ORDER * blocks + P_DEV

    ints = shape((owners, slots), jnp.int32)
    pay1, srow_v, raw_v, res_v, w_v, pid_v, live_v, const = call(
        project_kernel,
        (
            shape((owners, ORDER * blocks + 8, 128), BF16),
            ints,
            shape(raw_rows.shape, BF16),
            shape(resample.shape, BF16),
            shape((TAPS, owners, slots)),
            ints,
            ints,
            shape(const.shape),
        ),
        scratch=(
            pltpu.VMEM((owners, slots), F32),
            pltpu.VMEM((owners, slots), F32),
            pltpu.VMEM((owners, slots), F32),
            pltpu.VMEM((owners // 4, 256, slots), BF16),
            pltpu.VMEM((owners // 4, 128, slots), BF16),
            pltpu.VMEM((blocks, 4 * ORDER, 128), F32),
            pltpu.SemaphoreType.DMA((6 + vis,)),
        ),
        n_in=7,
        hbm=range(7),
    )(srow, raw_rows, resample, weights, pid, live, const)
    arr1 = exchange(pay1, "visit")
    tsum, qb, sy, mw, mtw = call(
        functools.partial(gather_kernel, ccd_devs),
        (
            shape((patches, pix)),
            shape((ORDER, 128)),
            shape((ORDER, 128)),
            shape((patches, 128), BF16),
            shape((2 * nvb, patches), BF16),
        ),
        scratch=(
            pltpu.VMEM((vis * rows + 16, pix), F32),
            pltpu.VMEM((owners, slots * TAPS), F32),
            pltpu.VMEM((owners, slots * TAPS), F32),
            pltpu.VMEM((owners, slots * TAPS), F32),
            pltpu.VMEM((nvb, pix), F32),
            pltpu.VMEM((patches, 128), F32),
        ),
        n_in=8,
        smem=(0,),
    )(srow.reshape(-1), raw_v, res_v, srow_v, w_v, pid_v, live_v, const)
    back, den, pay2 = call(
        first_kernel,
        (
            shape((ORDER, patches)),
            shape((ORDER, patches)),
            shape((ccd_devs, ORDER // 2, 128)),
        ),
        n_in=4,
    )(arr1, mtw, qb, sy)
    arr2 = exchange(pay2, "ccd")
    sy_all, pay3 = call(
        model_kernel,
        (shape((ORDER, 128)), shape((owners, pay_rows, 128), BF16)),
        n_in=5,
    )(arr2, const, mtw, mw, tsum)
    arr3 = exchange(pay3, "visit")
    pay4, lam = call(
        second_kernel, (shape((ccd_devs, ORDER // 4, 128)), shape((ORDER, 128))), n_in=6
    )(
        arr3, back, den, mtw, qb, const
    )
    arr4 = exchange(pay4, "ccd")
    offsets, background = call(
        final_kernel, (result((vis, ORDER * ORDER)), result((P_DEV, pix))), n_in=6
    )(arr4, arr3, den, sy_all, const, lam)
    return offsets, background


def solution(mesh):
    in_specs = (
        P("visit", "ccd", None),
        P("visit", None, None),
        P("visit", "ccd", None, None),
        P(None, "visit", "ccd", None, None),
        P("visit", "ccd", None, None),
        P("visit", "ccd", None, None),
    )
    out_specs = (P("visit", None), P(("visit", "ccd"), None))
    return jax.shard_map(
        per_device, mesh=mesh, in_specs=in_specs, out_specs=out_specs, check_vma=False
    )
```
